512 devices in a mesh: seq: 64 (over z, x, core), tp: 8 (over y).
Axes of the slice: x: 4, y: 8, z: 8, core: 2. Of those that a mesh axis runs over, the one named last changes fastest.
Arguments:
- x_in: bfloat16 [32768, 8192], P('seq', 'tp'), may hold values from -120 to 120
- z_in: bfloat16 [32768, 8192], P('seq', 'tp'), may hold values from -6 to 6
- b_in: bfloat16 [32768, 1024], P('seq', 'tp'), may hold values from -0.5 to 0.5
- c_in: bfloat16 [32768, 1024], P('seq', 'tp'), may hold values from -6 to 6
- decays: float32 [64, 32768], P('tp', 'seq'), may hold values from 0.4 to 1
- d_skip: float32 [64], P('tp'), may hold values from 0.5 to 2
- norm_weight: bfloat16 [8192], P('tp'), may hold values from 0.25 to 1.75
Outputs:
- ssd_output: bfloat16 [32768, 8192], P('seq', 'tp')
The draws below stay inside these ranges and needn't reach their ends.
All inputs are finite; a program needn't handle non-finite values.
Results may differ from the reference program's by a relative error of at most 0.0051.
Values sent between devices are 32-bit elements; how exact they have to be, the bound alone decides.
No kernel may reach another device: no remote copies, remote signals or barrier semaphores. Data moves between devices by JAX's collectives and lax.ppermute only.
A program may use at most 128 MiB of HBM per device.

```python
import math
import jax
import jax.numpy as jnp
from jax import lax

HEAD_TOTAL = 64
HEAD_DIM = 128
STATE = 128
GROUPS = 8
BLOCK = 256
TOKEN_TOTAL = 32768


def draw_x_in(key, part):
    key_rows = jax.random.split(key, 2)
    columns = HEAD_TOTAL * HEAD_DIM
    head_index = (jnp.arange(columns) // HEAD_DIM).astype(jnp.float32)
    rising = 0.3 * jnp.exp(jnp.log(10.0) * head_index / max(HEAD_TOTAL - 1, 1))
    rough = jnp.exp(jax.random.uniform(key_rows[1], (columns,), jnp.float32, jnp.log(0.5), jnp.log(2.0)))
    column_scale = rising * rough
    base = jnp.clip(jax.random.normal(key_rows[0], (TOKEN_TOTAL, columns), jnp.float32), -4.0, 4.0)
    values = base * column_scale[None, :]
    return values.astype(jnp.bfloat16)


def draw_decays(key, part):
    key_rows = jax.random.split(key, 6)
    slow_share = 0.5
    slow = jax.random.uniform(key_rows[0], (HEAD_TOTAL, 1), jnp.float32) < slow_share
    slow_rate = jnp.exp(jax.random.uniform(key_rows[1], (HEAD_TOTAL, 1), jnp.float32, jnp.log(0.02 / TOKEN_TOTAL), jnp.log(0.5 / TOKEN_TOTAL)))
    fast_rate = jnp.exp(jax.random.uniform(key_rows[2], (HEAD_TOTAL, 1), jnp.float32, jnp.log(1.0 / 50.0), jnp.log(1.0 / 20.0)))
    rate = jnp.where(slow, slow_rate, fast_rate)
    rough = jnp.exp(jax.random.uniform(key_rows[3], (HEAD_TOTAL, TOKEN_TOTAL), jnp.float32, jnp.log(0.5), jnp.log(2.0)))
    decay_factor = jnp.exp(-rate * rough)
    slab_output = jax.random.uniform(key_rows[4], (HEAD_TOTAL, TOKEN_TOTAL), jnp.float32) < 3.0 / TOKEN_TOTAL
    retained_state = jax.random.uniform(key_rows[5], (HEAD_TOTAL, TOKEN_TOTAL), jnp.float32, 0.5, 0.8)
    decay_factor = jnp.where(slab_output, decay_factor * retained_state, decay_factor)
    return decay_factor.astype(jnp.float32)


def levels(own_key, shape, cuts, low, top_value):
    gain = 1.0
    for position, blocks in cuts:
        heights = jax.random.uniform(jax.random.fold_in(jax.random.fold_in(own_key, 6), position), (blocks,), jnp.float32, low / len(cuts), top_value / len(cuts))
        gain = gain * jnp.repeat(jnp.exp(heights), shape[position] // blocks).reshape((-1,) + (1,) * (len(shape) - 1 - position))
    return gain


def scatter_about(own_key, extent, spread, limit, shards=(), held_as=jnp.bfloat16):
    drawn = jax.random.normal(own_key, extent, jnp.float32) * spread
    if len(shards) > 0:
        drawn = levels(own_key, extent, shards, -0.22, 0.18) * drawn
    return jnp.clip(drawn, min=-limit, max=limit).astype(held_as)


def setup_inputs(seed: int = 0) -> dict:
    keys = jax.random.split(jax.random.key(seed), 8)
    x_in = draw_x_in(jax.random.fold_in(keys[7], 71), 0)
    z_in = scatter_about(keys[1], (TOKEN_TOTAL, HEAD_TOTAL * HEAD_DIM), 1.0, 6.0, ((0, 64), (1, 8)))
    b_in = scatter_about(keys[2], (TOKEN_TOTAL, GROUPS * STATE), STATE ** -0.5, 0.5, ((0, 64), (1, 8)))
    c_in = scatter_about(keys[3], (TOKEN_TOTAL, GROUPS * STATE), 1.0, 6.0, ((0, 64), (1, 8)))
    decays = draw_decays(jax.random.fold_in(keys[7], 71), 0)
    d_skip = jnp.clip(jnp.exp(math.log(2.0) - 1.3862944 * jax.random.uniform(keys[5], (HEAD_TOTAL,), jnp.float32) ** levels(keys[5], (HEAD_TOTAL,), ((0, 8),), -0.2, 0.2)), 0.5, 2.0)
    norm_weight = jnp.clip(1.0 + 0.15 * jax.random.normal(keys[6], (HEAD_TOTAL * HEAD_DIM,), jnp.float32), 0.25, 1.75).astype(jnp.bfloat16)
    return dict(x_in=x_in, z_in=z_in, b_in=b_in, c_in=c_in, decays=decays, d_skip=d_skip, norm_weight=norm_weight)


epsilon = 1e-05

def to_bf16_once(value):
    return lax.optimization_barrier(value.astype(jnp.bfloat16)).astype(jnp.float32)

def reference(x_in, z_in, b_in, c_in, decays, d_skip, norm_weight):
    block_count = TOKEN_TOTAL // BLOCK
    per_group = HEAD_TOTAL // GROUPS
    x_blocks = x_in.reshape(block_count, BLOCK, GROUPS, per_group, HEAD_DIM)
    z_blocks = z_in.reshape(block_count, BLOCK, HEAD_TOTAL * HEAD_DIM)
    b_blocks = b_in.reshape(block_count, BLOCK, GROUPS, STATE)
    c_blocks = c_in.reshape(block_count, BLOCK, GROUPS, STATE)
    log_blocks = jnp.log(decays).reshape(GROUPS, per_group, block_count, BLOCK).transpose(2, 0, 1, 3)
    skip_gain = d_skip.reshape(GROUPS, per_group)
    gain_full = norm_weight.astype(jnp.float32)
    causal = jnp.arange(BLOCK)[:, None] >= jnp.arange(BLOCK)[None, :]
    highest = lax.Precision.HIGHEST

    def advance(carried, inputs):
        x_block, z_block, b_block, c_block, log_block = inputs
        cumulative = jnp.cumsum(log_block, axis=-1)
        block_log = cumulative[..., -1]
        x_float = x_block.astype(jnp.float32)
        b_float = b_block.astype(jnp.float32)
        c_float = c_block.astype(jnp.float32)
        scores = jnp.einsum('qgn,sgn->gqs', c_float, b_float, precision=highest)
        exponent = jnp.where(causal, cumulative[..., :, None] - cumulative[..., None, :], -jnp.inf)
        weights = to_bf16_once(scores[:, None] * jnp.exp(exponent))
        y_diag = jnp.einsum('gkqs,sgkp->qgkp', weights, x_float, precision=highest)
        entry_state = to_bf16_once(carried)
        y_off = jnp.einsum('qgn,pgkn->qgkp', c_float, entry_state, precision=highest)
        y_off = y_off * jnp.exp(cumulative).transpose(2, 0, 1)[..., None]
        y_full = y_diag + y_off + skip_gain[None, :, :, None] * x_float
        to_end = jnp.exp(block_log[..., None] - cumulative)
        weighted = to_bf16_once(x_float * to_end.transpose(2, 0, 1)[..., None])
        block_state = jnp.einsum('sgkp,sgn->pgkn', weighted, b_float, precision=highest)
        new_state = jnp.exp(block_log)[None, :, :, None] * carried + block_state
        gated = y_full.reshape(BLOCK, HEAD_TOTAL * HEAD_DIM) * jax.nn.silu(z_block.astype(jnp.float32))
        mean_square = lax.optimization_barrier(jnp.sum(gated * gated, axis=1, keepdims=True)) / (HEAD_TOTAL * HEAD_DIM)
        normed = (gated * lax.rsqrt(mean_square + epsilon) * gain_full).astype(jnp.bfloat16)
        return (new_state, normed)
    start_state = jnp.zeros((HEAD_DIM, GROUPS, per_group, STATE), jnp.float32)
    final_state, outputs = lax.scan(advance, start_state, (x_blocks, z_blocks, b_blocks, c_blocks, log_blocks))
    return outputs.reshape(TOKEN_TOTAL, HEAD_TOTAL * HEAD_DIM)
```

```python
import functools

import jax
import jax.numpy as jnp
from jax import lax
from jax.experimental import pallas as pl
from jax.experimental.pallas import tpu as pltpu
from jax.sharding import PartitionSpec as P

HEAD_TOTAL = 64
HEAD_DIM = 128
STATE = 128
BLOCK = 256
CHIPS = 32

epsilon = 1e-05

HEADS = 8
TOK = 512
WIDTH = HEADS * HEAD_DIM
HALF = WIDTH // 2
ROWS = STATE // CHIPS

VMEM_BYTES = 48 << 20
f32 = jnp.float32
bf16 = jnp.bfloat16


def params(grid_rank=0):
    kwargs = {"vmem_limit_bytes": VMEM_BYTES}
    if grid_rank:
        kwargs["dimension_semantics"] = ("arbitrary",) * grid_rank
    return pltpu.CompilerParams(**kwargs)


def smem_spec():
    return pl.BlockSpec(memory_space=pltpu.SMEM)


def vmem_spec():
    return pl.BlockSpec(memory_space=pltpu.VMEM)


def split3(value):
    high = value.astype(bf16)
    rest = value - high.astype(f32)
    middle = rest.astype(bf16)
    low = (rest - middle.astype(f32)).astype(bf16)
    return high, middle, low


def state_kernel(core_ref, x_ref, b_ref, decay_ref, first_ref, send_ref, keep_ref, cum_ref, b_t, to_end):
    step = pl.program_id(0)

    @pl.when(step == 0)
    def _():
        logs = jnp.log2(decay_ref[...])
        row = lax.broadcasted_iota(jnp.int32, (BLOCK, BLOCK), 0)
        col = lax.broadcasted_iota(jnp.int32, (BLOCK, BLOCK), 1)
        upper = jnp.where(row <= col, 1.0, 0.0).astype(bf16)
        for block in range(2):
            span = slice(block * BLOCK, (block + 1) * BLOCK)
            total = jnp.zeros((HEADS, BLOCK), f32)
            for part in reversed(split3(logs[:, span])):
                total = total + jnp.dot(part, upper, preferred_element_type=f32)
            cum_ref[:, span] = total
            to_end[:, span] = jnp.exp2(total[:, BLOCK - 1 :] - total)
        b_t[...] = b_ref[...].astype(f32).T

    half = step // 2
    for pair in range(2):
        head = step * 2 + pair
        columns = slice(pair * HEAD_DIM, (pair + 1) * HEAD_DIM)
        weight = to_end[pl.ds(head, 1), :]
        cum = cum_ref[pl.ds(head, 1), :]
        last0 = cum[:, BLOCK - 1 : BLOCK]
        last1 = cum[:, 2 * BLOCK - 1 :]
        b_weighted = (b_t[...] * weight).astype(bf16)
        state0 = jnp.dot(b_weighted[:, :BLOCK], x_ref[:BLOCK, columns], preferred_element_type=f32)
        state1 = jnp.dot(b_weighted[:, BLOCK:], x_ref[BLOCK:, columns], preferred_element_type=f32)
        first_ref[:, columns] = state0
        slab = jnp.exp2(last1) * state0 + state1
        slab_log = jnp.broadcast_to(last0 + last1, (8, HEAD_DIM))
        target = pl.ds(pl.multiple_of((step % 2) * 256 + pair * HEAD_DIM, HEAD_DIM), HEAD_DIM)

        @pl.when(half == core_ref[0])
        def _():
            keep_ref[:STATE, target] = slab
            keep_ref[STATE:, target] = slab_log

        @pl.when(half != core_ref[0])
        def _():
            send_ref[:STATE, target] = slab
            send_ref[STATE:, target] = slab_log


def state_call(core, x_in, b_in, decays):
    half_shape = jax.ShapeDtypeStruct((STATE + 8, HALF), f32)
    return pl.pallas_call(
        state_kernel,
        grid=(4,),
        in_specs=[
            smem_spec(),
            pl.BlockSpec((TOK, 256), lambda i: (0, i)),
            pl.BlockSpec((TOK, STATE), lambda i: (0, 0)),
            pl.BlockSpec((HEADS, TOK), lambda i: (0, 0)),
        ],
        out_specs=[
            pl.BlockSpec((STATE, 256), lambda i: (0, i)),
            pl.BlockSpec((STATE + 8, HALF), lambda i: (0, 0)),
            pl.BlockSpec((STATE + 8, HALF), lambda i: (0, 0)),
            pl.BlockSpec((HEADS, TOK), lambda i: (0, 0)),
        ],
        out_shape=[
            jax.ShapeDtypeStruct((STATE, WIDTH), f32),
            half_shape,
            half_shape,
            jax.ShapeDtypeStruct((HEADS, TOK), f32),
        ],
        scratch_shapes=[pltpu.VMEM((STATE, TOK), f32), pltpu.VMEM((HEADS, TOK), f32)],
        compiler_params=params(1),
        name="slab_state",
    )(core, x_in, b_in, decays)


def chip_kernel(core_ref, keep_ref, recv_ref, pay_ref, base_ref):
    def write(early_ref, late_ref):
        base_ref[...] = early_ref[...]
        for head in range(4):
            columns = slice(head * HEAD_DIM, (head + 1) * HEAD_DIM)
            late_log = late_ref[STATE : STATE + 1, columns]
            chip_log = early_ref[STATE : STATE + 1, columns] + late_log
            state = jnp.exp2(late_log) * early_ref[:STATE, columns] + late_ref[:STATE, columns]
            for chip in range(CHIPS):
                pay_ref[chip, :, columns] = state[chip * ROWS : (chip + 1) * ROWS, :]
                pay_ref[chip, head : head + 1, HALF:] = chip_log

    @pl.when(core_ref[0] == 0)
    def _():
        write(keep_ref, recv_ref)

    @pl.when(core_ref[0] != 0)
    def _():
        write(recv_ref, keep_ref)


def chip_call(core, keep, recv):
    return pl.pallas_call(
        chip_kernel,
        in_specs=[smem_spec(), vmem_spec(), vmem_spec()],
        out_specs=[vmem_spec(), vmem_spec()],
        out_shape=[
            jax.ShapeDtypeStruct((CHIPS, ROWS, HALF + HEAD_DIM), f32),
            jax.ShapeDtypeStruct((STATE + 8, HALF), f32),
        ],
        compiler_params=params(),
        name="chip_state",
    )(core, keep, recv)


def scan_kernel(pay_ref, out_ref):
    for head in range(4):
        columns = slice(head * HEAD_DIM, (head + 1) * HEAD_DIM)
        carry = jnp.zeros((ROWS, HEAD_DIM), f32)
        for chip in range(CHIPS):
            out_ref[chip, :, columns] = carry
            if chip < CHIPS - 1:
                factor = jnp.exp2(pay_ref[chip, head : head + 1, HALF:])
                carry = factor * carry + pay_ref[chip, :, columns]


def scan_call(pay):
    return pl.pallas_call(
        scan_kernel,
        in_specs=[vmem_spec()],
        out_specs=vmem_spec(),
        out_shape=jax.ShapeDtypeStruct((CHIPS, ROWS, HALF), f32),
        compiler_params=params(),
        name="chip_scan",
    )(pay)


def entry_kernel(core_ref, pre_ref, base_ref, send_ref, own_ref):
    def write(plain_ref, moved_ref):
        for head in range(4):
            columns = slice(head * HEAD_DIM, (head + 1) * HEAD_DIM)
            factor = jnp.exp2(base_ref[STATE : STATE + 1, columns])
            entry = jnp.concatenate([pre_ref[chip, :, columns] for chip in range(CHIPS)], axis=0)
            plain_ref[:, columns] = entry
            moved_ref[:, columns] = factor * entry + base_ref[:STATE, columns]

    @pl.when(core_ref[0] == 0)
    def _():
        write(own_ref, send_ref)

    @pl.when(core_ref[0] != 0)
    def _():
        write(send_ref, own_ref)


def entry_call(core, pre, base):
    half_shape = jax.ShapeDtypeStruct((STATE, HALF), f32)
    return pl.pallas_call(
        entry_kernel,
        in_specs=[smem_spec(), vmem_spec(), vmem_spec()],
        out_specs=[vmem_spec(), vmem_spec()],
        out_shape=[half_shape, half_shape],
        compiler_params=params(),
        name="slab_entry",
    )(core, pre, base)


def diagonal_kernel(skip_ref, x_ref, z_ref, b_ref, c_ref, cum_ref, plain_ref, gain_ref):
    scores = lax.dot_general(
        c_ref[...], b_ref[...], (((1,), (1,)), ((), ())), preferred_element_type=f32
    )
    row = lax.broadcasted_iota(jnp.int32, (BLOCK, BLOCK), 0)
    col = lax.broadcasted_iota(jnp.int32, (BLOCK, BLOCK), 1)
    causal = row >= col
    cum = cum_ref[...]
    cum_t = cum.T
    for head in range(HEADS):
        columns = slice(head * HEAD_DIM, (head + 1) * HEAD_DIM)
        cum_col = cum_t[:, head : head + 1]
        exponent = jnp.where(causal, cum_col - cum[head : head + 1, :], -jnp.inf)
        weights = (scores * jnp.exp2(exponent)).astype(bf16)
        x_head = x_ref[:, columns]
        y = jnp.dot(weights, x_head, preferred_element_type=f32)
        y = y + skip_ref[head] * x_head.astype(f32)
        z = z_ref[:, columns].astype(f32)
        gate = z / (1.0 + jnp.exp(-z))
        plain_ref[:, columns] = y * gate
        gain_ref[:, columns] = jnp.exp2(cum_col) * gate


def diagonal_call(d_skip, x_in, z_in, b_in, c_in, cum):
    wide = pl.BlockSpec((BLOCK, WIDTH), lambda i: (i, 0))
    thin = pl.BlockSpec((BLOCK, STATE), lambda i: (i, 0))
    shape = jax.ShapeDtypeStruct((TOK, WIDTH), f32)
    return pl.pallas_call(
        diagonal_kernel,
        grid=(2,),
        in_specs=[
            smem_spec(),
            wide,
            wide,
            thin,
            thin,
            pl.BlockSpec((HEADS, BLOCK), lambda i: (0, i)),
        ],
        out_specs=[wide, wide],
        out_shape=[shape, shape],
        compiler_params=params(1),
        cost_estimate=pl.CostEstimate(
            flops=600_000_000, bytes_accessed=7_000_000, transcendentals=2_000_000
        ),
        name="diagonal",
    )(d_skip, x_in, z_in, b_in, c_in, cum)


def column_to_row(column):
    row = lax.broadcasted_iota(jnp.int32, (128, 128), 0)
    col = lax.broadcasted_iota(jnp.int32, (128, 128), 1)
    spread = jnp.where(row == col, jnp.broadcast_to(column, (128, 128)), 0.0)
    return jnp.sum(spread, axis=0, keepdims=True)


def gated_kernel(core_ref, own_ref, recv_ref, first_ref, cum_ref, c_ref, plain_ref, gain_ref, gated_ref, sum_ref, entry):
    block = pl.program_id(0)

    @pl.when(block == 0)
    def _():
        core = core_ref[0]
        entry[:, pl.ds(pl.multiple_of(core * HALF, HALF), HALF)] = own_ref[...]
        entry[:, pl.ds(pl.multiple_of((1 - core) * HALF, HALF), HALF)] = recv_ref[...]

    @pl.when(block == 1)
    def _():
        for head in range(HEADS):
            columns = slice(head * HEAD_DIM, (head + 1) * HEAD_DIM)
            factor = jnp.exp2(cum_ref[head : head + 1, BLOCK - 1 : BLOCK])
            entry[:, columns] = factor * entry[:, columns] + first_ref[:, columns]

    squares = jnp.zeros((BLOCK, HEAD_DIM), f32)
    for part in range(4):
        columns = slice(part * 256, (part + 1) * 256)
        off = jnp.dot(c_ref[...], entry[:, columns].astype(bf16), preferred_element_type=f32)
        gated = plain_ref[:, columns] + gain_ref[:, columns] * off
        gated_ref[:, columns] = gated
        square = gated * gated
        squares = squares + square[:, :128] + square[:, 128:]
    column = jnp.sum(squares, axis=1, keepdims=True)
    rows = jnp.concatenate([column_to_row(column[:128]), column_to_row(column[128:])], axis=0)
    for peer in range(8):
        sum_ref[peer, pl.ds(block * 2, 2), :] = rows


def gated_call(core, own, recv, first, cum, c_in, plain, gain):
    wide = pl.BlockSpec((BLOCK, WIDTH), lambda i: (i, 0))
    whole = lambda *shape: pl.BlockSpec(shape, lambda i: (0,) * len(shape))
    return pl.pallas_call(
        gated_kernel,
        grid=(2,),
        in_specs=[
            smem_spec(),
            whole(STATE, HALF),
            whole(STATE, HALF),
            whole(STATE, WIDTH),
            whole(HEADS, TOK),
            pl.BlockSpec((BLOCK, STATE), lambda i: (i, 0)),
            wide,
            wide,
        ],
        out_specs=[wide, whole(8, 4, 128)],
        out_shape=[
            jax.ShapeDtypeStruct((TOK, WIDTH), f32),
            jax.ShapeDtypeStruct((8, 4, 128), f32),
        ],
        scratch_shapes=[pltpu.VMEM((STATE, WIDTH), f32)],
        compiler_params=params(1),
        name="gated",
    )(core, own, recv, first, cum, c_in, plain, gain)


def scale_kernel(sums_ref, weight_ref, gated_ref, out_ref):
    step = pl.program_id(0)
    total = jnp.sum(sums_ref[:, pl.ds(step, 1), :], axis=0)
    inverse = lax.rsqrt(total / (HEAD_TOTAL * HEAD_DIM) + epsilon)
    column = jnp.broadcast_to(inverse, (128, 128)).T
    for head in range(HEADS):
        columns = slice(head * HEAD_DIM, (head + 1) * HEAD_DIM)
        weight = weight_ref[:, columns].astype(f32)
        out_ref[:, columns] = (gated_ref[:, columns] * column * weight).astype(bf16)


def scale_call(sums, norm_weight, gated):
    return pl.pallas_call(
        scale_kernel,
        grid=(4,),
        in_specs=[
            pl.BlockSpec((8, 4, 128), lambda i: (0, 0, 0)),
            pl.BlockSpec((1, WIDTH), lambda i: (0, 0)),
            pl.BlockSpec((128, WIDTH), lambda i: (i, 0)),
        ],
        out_specs=pl.BlockSpec((128, WIDTH), lambda i: (i, 0)),
        out_shape=jax.ShapeDtypeStruct((TOK, WIDTH), bf16),
        compiler_params=params(1),
        name="scale",
    )(sums, norm_weight.reshape(1, WIDTH), gated)


def shards(x_in, z_in, b_in, c_in, decays, d_skip, norm_weight):
    core = (lax.axis_index("seq") % 2).astype(jnp.int32).reshape(1)
    swap = [(i, i ^ 1) for i in range(2 * CHIPS)]
    groups = [[2 * chip + c for chip in range(CHIPS)] for c in range(2)]
    first, send, keep, cum = state_call(core, x_in, b_in, decays)
    recv = lax.ppermute(send, "seq", swap)
    pay, base = chip_call(core, keep, recv)
    pay = lax.all_to_all(pay, "seq", 0, 0, axis_index_groups=groups, tiled=True)
    plain, gain = diagonal_call(d_skip, x_in, z_in, b_in, c_in, cum)
    pre = scan_call(pay)
    pre = lax.all_to_all(pre, "seq", 0, 0, axis_index_groups=groups, tiled=True)
    send, own = entry_call(core, pre, base)
    recv = lax.ppermute(send, "seq", swap)
    gated, sums = gated_call(core, own, recv, first, cum, c_in, plain, gain)
    sums = lax.all_to_all(sums, "tp", 0, 0, tiled=True)
    return scale_call(sums, norm_weight, gated)


def solution(mesh):
    return jax.shard_map(
        shards,
        mesh=mesh,
        in_specs=(
            P("seq", "tp"),
            P("seq", "tp"),
            P("seq", "tp"),
            P("seq", "tp"),
            P("tp", "seq"),
            P("tp"),
            P("tp"),
        ),
        out_specs=P("seq", "tp"),
        check_vma=False,
    )
```

```python
import functools

import jax
import jax.numpy as jnp
from jax import lax
from jax.experimental import pallas as pl
from jax.experimental.pallas import tpu as pltpu
from jax.sharding import PartitionSpec as P

HEAD_TOTAL = 64
HEAD_DIM = 128
STATE = 128
BLOCK = 256
CHIPS = 32

epsilon = 1e-05

HEADS = 8
TOK = 512
WIDTH = HEADS * HEAD_DIM
HALF = WIDTH // 2
ROWS = STATE // CHIPS

VMEM_BYTES = 16 << 20
f32 = jnp.float32
bf16 = jnp.bfloat16


def params():
    return pltpu.CompilerParams(vmem_limit_bytes=VMEM_BYTES)


def smem_spec():
    return pl.BlockSpec(memory_space=pltpu.SMEM)


def vmem_spec():
    return pl.BlockSpec(memory_space=pltpu.VMEM)


def hbm_spec():
    return pl.BlockSpec(memory_space=pltpu.HBM)


def head_columns(head):
    return slice(head * HEAD_DIM, (head + 1) * HEAD_DIM)


def split3(value):
    high = value.astype(bf16)
    rest = value - high.astype(f32)
    middle = rest.astype(bf16)
    low = (rest - middle.astype(f32)).astype(bf16)
    return high, middle, low


def state_kernel(
    core_ref, x_hbm, z_hbm, b_hbm, c_hbm, decay_hbm, skip_hbm,
    first_ref, send_ref, keep_ref, cum_ref, skip_ref, x_ref, z_ref, b_ref, c_ref,
    decay_ref, skip_smem, sems,
):
    decay_copy = pltpu.make_async_copy(decay_hbm, decay_ref, sems.at[0])
    decay_copy.start()
    b_copy = pltpu.make_async_copy(b_hbm, b_ref, sems.at[1])
    b_copy.start()
    x_copies = []
    for part in range(4):
        columns = slice(part * 256, (part + 1) * 256)
        copy = pltpu.make_async_copy(x_hbm.at[:, columns], x_ref.at[:, columns], sems.at[2 + part])
        copy.start()
        x_copies.append(copy)
    later_copies = [
        pltpu.make_async_copy(skip_hbm, skip_smem, sems.at[6]),
        pltpu.make_async_copy(c_hbm, c_ref, sems.at[7]),
        pltpu.make_async_copy(z_hbm, z_ref, sems.at[8]),
    ]
    for copy in later_copies:
        copy.start()

    row = lax.broadcasted_iota(jnp.int32, (BLOCK, BLOCK), 0)
    col = lax.broadcasted_iota(jnp.int32, (BLOCK, BLOCK), 1)
    upper = jnp.where(row <= col, 1.0, 0.0).astype(bf16)
    decay_copy.wait()
    logs = jnp.log2(decay_ref[...])
    totals = []
    weights = []
    for block in range(2):
        span = slice(block * BLOCK, (block + 1) * BLOCK)
        total = jnp.zeros((HEADS, BLOCK), f32)
        for part in reversed(split3(logs[:, span])):
            total = total + jnp.dot(part, upper, preferred_element_type=f32)
        cum_ref[:, span] = total
        last = total[:, BLOCK - 1 :]
        totals.append(last)
        weights.append(jnp.exp2(last - total))
    second = jnp.exp2(totals[1])
    slab_logs = jnp.broadcast_to(totals[0] + totals[1], (HEADS, HEAD_DIM))
    b_copy.wait()
    b_t = b_ref[...].astype(f32).T
    for head in range(HEADS):
        columns = head_columns(head)
        if head % 2 == 0:
            x_copies[head // 2].wait()
        states = []
        for block in range(2):
            span = slice(block * BLOCK, (block + 1) * BLOCK)
            b_weighted = (b_t[:, span] * weights[block][head : head + 1, :]).astype(bf16)
            states.append(jnp.dot(b_weighted, x_ref[span, columns], preferred_element_type=f32))
        first_ref[:, columns] = states[0]
        slab = second[head : head + 1, :] * states[0] + states[1]
        slab_log = jnp.broadcast_to(slab_logs[head : head + 1, :], (8, HEAD_DIM))
        target = head_columns(head % 4)

        @pl.when(core_ref[0] == head // 4)
        def _():
            keep_ref[:STATE, target] = slab
            keep_ref[STATE:, target] = slab_log

        @pl.when(core_ref[0] != head // 4)
        def _():
            send_ref[:STATE, target] = slab
            send_ref[STATE:, target] = slab_log

    for copy in later_copies:
        copy.wait()
    for head in range(HEADS):
        skip_ref[head : head + 1, :] = jnp.full((1, HEAD_DIM), skip_smem[head], f32)


def state_call(core, x_in, z_in, b_in, c_in, decays, d_skip):
    half_shape = jax.ShapeDtypeStruct((STATE + 8, HALF), f32)
    arrays = [
        pltpu.with_memory_space_constraint(array, pltpu.HBM)
        for array in (x_in, z_in, b_in, c_in, decays, d_skip)
    ]
    return pl.pallas_call(
        state_kernel,
        in_specs=[smem_spec()] + [hbm_spec()] * 6,
        out_specs=[vmem_spec()] * 9,
        out_shape=[
            jax.ShapeDtypeStruct((STATE, WIDTH), f32),
            half_shape,
            half_shape,
            jax.ShapeDtypeStruct((HEADS, TOK), f32),
            jax.ShapeDtypeStruct((HEADS, HEAD_DIM), f32),
            jax.ShapeDtypeStruct((TOK, WIDTH), bf16),
            jax.ShapeDtypeStruct((TOK, WIDTH), bf16),
            jax.ShapeDtypeStruct((TOK, STATE), bf16),
            jax.ShapeDtypeStruct((TOK, STATE), bf16),
        ],
        scratch_shapes=[
            pltpu.VMEM((HEADS, TOK), f32),
            pltpu.SMEM((HEADS,), f32),
            pltpu.SemaphoreType.DMA((9,)),
        ],
        compiler_params=params(),
        name="slab_state",
    )(core, *arrays)


def chip_kernel(core_ref, keep_ref, recv_ref, pay_ref, base_ref):
    def write(early_ref, late_ref):
        base_ref[...] = early_ref[...]
        for head in range(4):
            columns = head_columns(head)
            late_log = late_ref[STATE : STATE + 1, columns]
            chip_log = early_ref[STATE : STATE + 1, columns] + late_log
            state = jnp.exp2(late_log) * early_ref[:STATE, columns] + late_ref[:STATE, columns]
            for chip in range(CHIPS):
                pay_ref[chip, :, columns] = state[chip * ROWS : (chip + 1) * ROWS, :]
                pay_ref[chip, head : head + 1, HALF:] = chip_log

    @pl.when(core_ref[0] == 0)
    def _():
        write(keep_ref, recv_ref)

    @pl.when(core_ref[0] != 0)
    def _():
        write(recv_ref, keep_ref)


def chip_call(core, keep, recv):
    return pl.pallas_call(
        chip_kernel,
        in_specs=[smem_spec(), vmem_spec(), vmem_spec()],
        out_specs=[vmem_spec(), vmem_spec()],
        out_shape=[
            jax.ShapeDtypeStruct((CHIPS, ROWS, HALF + HEAD_DIM), f32),
            jax.ShapeDtypeStruct((STATE + 8, HALF), f32),
        ],
        compiler_params=params(),
        name="chip_state",
    )(core, keep, recv)


def scan_kernel(pay_ref, out_ref):
    for head in range(4):
        columns = head_columns(head)
        carry = jnp.zeros((ROWS, HEAD_DIM), f32)
        for chip in range(CHIPS):
            out_ref[chip, :, columns] = carry
            if chip < CHIPS - 1:
                factor = jnp.exp2(pay_ref[chip, head : head + 1, HALF:])
                carry = factor * carry + pay_ref[chip, :, columns]


def scan_call(pay):
    return pl.pallas_call(
        scan_kernel,
        in_specs=[vmem_spec()],
        out_specs=vmem_spec(),
        out_shape=jax.ShapeDtypeStruct((CHIPS, ROWS, HALF), f32),
        compiler_params=params(),
        name="chip_scan",
    )(pay)


def entry_kernel(core_ref, pre_ref, base_ref, send_ref, own_ref):
    def write(plain_ref, moved_ref):
        for head in range(4):
            columns = head_columns(head)
            factor = jnp.exp2(base_ref[STATE : STATE + 1, columns])
            entry = jnp.concatenate([pre_ref[chip, :, columns] for chip in range(CHIPS)], axis=0)
            plain_ref[:, columns] = entry
            moved_ref[:, columns] = factor * entry + base_ref[:STATE, columns]

    @pl.when(core_ref[0] == 0)
    def _():
        write(own_ref, send_ref)

    @pl.when(core_ref[0] != 0)
    def _():
        write(send_ref, own_ref)


def entry_call(core, pre, base):
    half_shape = jax.ShapeDtypeStruct((STATE, HALF), f32)
    return pl.pallas_call(
        entry_kernel,
        in_specs=[smem_spec(), vmem_spec(), vmem_spec()],
        out_specs=[vmem_spec(), vmem_spec()],
        out_shape=[half_shape, half_shape],
        compiler_params=params(),
        name="slab_entry",
    )(core, pre, base)


def diagonal_kernel(block, skip_ref, x_ref, z_ref, b_ref, c_ref, cum_ref, plain_ref, gain_ref):
    tokens = slice(block * BLOCK, (block + 1) * BLOCK)
    start = block * BLOCK
    cum = cum_ref[:, tokens]
    cum_t = cum.T
    row = lax.broadcasted_iota(jnp.int32, (128, 128), 0)
    col = lax.broadcasted_iota(jnp.int32, (128, 128), 1)
    causal = row >= col
    c_block = c_ref[tokens, :]
    b_block = b_ref[tokens, :]
    scores = []
    for tile in range(2):
        rows = slice(tile * 128, (tile + 1) * 128)
        for other in range(tile + 1):
            across = slice(other * 128, (other + 1) * 128)
            scores.append(
                lax.dot_general(
                    c_block[rows], b_block[across], (((1,), (1,)), ((), ())), preferred_element_type=f32
                )
            )
    for head in range(HEADS):
        columns = head_columns(head)
        cum_row = cum[head : head + 1, :]
        for tile in range(2):
            rows = slice(tile * 128, (tile + 1) * 128)
            here = slice(start + tile * 128, start + (tile + 1) * 128)
            cum_col = jnp.broadcast_to(cum_t[rows, head : head + 1], (128, HEAD_DIM))
            exponent = jnp.where(causal, cum_col - cum_row[:, rows], -jnp.inf)
            weights = (scores[0 if tile == 0 else 2] * jnp.exp2(exponent)).astype(bf16)
            if tile == 1:
                before = (scores[1] * jnp.exp2(cum_col - cum_row[:, :128])).astype(bf16)
                weights = jnp.concatenate([before, weights], axis=1)
            x_head = x_ref[slice(start, start + (tile + 1) * 128), columns]
            y = jnp.dot(weights, x_head, preferred_element_type=f32)
            y = y + skip_ref[head : head + 1, :] * x_ref[here, columns].astype(f32)
            half_z = 0.5 * z_ref[here, columns].astype(f32)
            gate = half_z + half_z * jnp.tanh(half_z)
            plain_ref[rows, columns] = y * gate
            gain_ref[rows, columns] = jnp.exp2(cum_col) * gate


def diagonal_call(block, skip, x_in, z_in, b_in, c_in, cum):
    shape = jax.ShapeDtypeStruct((BLOCK, WIDTH), f32)
    return pl.pallas_call(
        functools.partial(diagonal_kernel, block),
        in_specs=[vmem_spec()] * 6,
        out_specs=[vmem_spec(), vmem_spec()],
        out_shape=[shape, shape],
        compiler_params=params(),
        cost_estimate=pl.CostEstimate(
            flops=300_000_000, bytes_accessed=3_500_000, transcendentals=1_000_000
        ),
        name="diagonal",
    )(skip, x_in, z_in, b_in, c_in, cum)


def column_to_row(column):
    row = lax.broadcasted_iota(jnp.int32, (128, 128), 0)
    col = lax.broadcasted_iota(jnp.int32, (128, 128), 1)
    spread = jnp.where(row == col, jnp.broadcast_to(column, (128, 128)), 0.0)
    return jnp.sum(spread, axis=0, keepdims=True)


def gated_kernel(
    core_ref, own_ref, recv_ref, first_ref, cum_ref, c_ref, weight_ref,
    plain0_ref, gain0_ref, plain1_ref, gain1_ref, gated_ref, sum_ref, entry,
):
    core = core_ref[0]
    entry[:, pl.ds(pl.multiple_of(core * HALF, HALF), HALF)] = own_ref[...]
    entry[:, pl.ds(pl.multiple_of((1 - core) * HALF, HALF), HALF)] = recv_ref[...]
    weight = weight_ref[...].astype(f32)
    factors = jnp.exp2(cum_ref[:, BLOCK - 1 : BLOCK])
    for block in range(2):
        plain_ref, gain_ref = ((plain0_ref, gain0_ref), (plain1_ref, gain1_ref))[block]
        tokens = slice(block * BLOCK, (block + 1) * BLOCK)
        squares = jnp.zeros((BLOCK, HEAD_DIM), f32)
        for pair in range(4):
            states = []
            for head in (2 * pair, 2 * pair + 1):
                columns = head_columns(head)
                state = entry[:, columns]
                if block == 1:
                    state = factors[head : head + 1, :] * state + first_ref[:, columns]
                states.append(state.astype(bf16))
            columns = slice(pair * 256, (pair + 1) * 256)
            off = jnp.dot(
                c_ref[tokens, :], jnp.concatenate(states, axis=1), preferred_element_type=f32
            )
            gated = plain_ref[:, columns] + gain_ref[:, columns] * off
            gated_ref[tokens, columns] = gated * weight[:, columns]
            square = gated * gated
            squares = squares + square[:, :128] + square[:, 128:]
        column = jnp.sum(squares, axis=1, keepdims=True)
        rows = jnp.concatenate([column_to_row(column[:128]), column_to_row(column[128:])], axis=0)
        for peer in range(8):
            sum_ref[peer, 2 * block : 2 * block + 2, :] = rows


def gated_call(core, own, recv, first, cum, c_in, norm_weight, parts):
    return pl.pallas_call(
        gated_kernel,
        in_specs=[smem_spec()] + [vmem_spec()] * 10,
        out_specs=[vmem_spec(), vmem_spec()],
        out_shape=[
            jax.ShapeDtypeStruct((TOK, WIDTH), f32),
            jax.ShapeDtypeStruct((8, 4, 128), f32),
        ],
        scratch_shapes=[pltpu.VMEM((STATE, WIDTH), f32)],
        compiler_params=params(),
        name="gated",
    )(core, own, recv, first, cum, c_in, norm_weight.reshape(1, WIDTH), *parts)


def scale_kernel(sums_ref, gated_ref, out_hbm, buffer, sems):
    total = jnp.sum(sums_ref[...], axis=0)
    inverse = lax.rsqrt(total / (HEAD_TOTAL * HEAD_DIM) + epsilon)
    copies = []
    for part in range(4):
        tokens = slice(part * 128, (part + 1) * 128)
        column = jnp.broadcast_to(inverse[part : part + 1, :], (128, 128)).T
        for head in range(HEADS):
            columns = head_columns(head)
            buffer[tokens, columns] = (gated_ref[tokens, columns] * column).astype(bf16)
        copy = pltpu.make_async_copy(buffer.at[tokens, :], out_hbm.at[tokens, :], sems.at[part])
        copy.start()
        copies.append(copy)
    for copy in copies:
        copy.wait()


def scale_call(sums, gated):
    return pl.pallas_call(
        scale_kernel,
        in_specs=[vmem_spec(), vmem_spec()],
        out_specs=hbm_spec(),
        out_shape=jax.ShapeDtypeStruct((TOK, WIDTH), bf16),
        scratch_shapes=[pltpu.VMEM((TOK, WIDTH), bf16), pltpu.SemaphoreType.DMA((4,))],
        compiler_params=params(),
        name="scale",
    )(sums, gated)


def shards(x_in, z_in, b_in, c_in, decays, d_skip, norm_weight):
    core = (lax.axis_index("seq") % 2).astype(jnp.int32).reshape(1)
    swap = [(i, i ^ 1) for i in range(2 * CHIPS)]
    groups = [[2 * chip + c for chip in range(CHIPS)] for c in range(2)]
    first, send, keep, cum, *inputs = state_call(core, x_in, z_in, b_in, c_in, decays, d_skip)
    c_in = inputs[-1]
    recv = lax.ppermute(send, "seq", swap)
    part0 = diagonal_call(0, *inputs, cum)
    recv, *part0 = lax.optimization_barrier((recv, *part0))
    pay, base = chip_call(core, keep, recv)
    pay = lax.all_to_all(pay, "seq", 0, 0, axis_index_groups=groups, tiled=True)
    pre = scan_call(pay)
    pre = lax.all_to_all(pre, "seq", 0, 0, axis_index_groups=groups, tiled=True)
    send, own = entry_call(core, pre, base)
    recv = lax.ppermute(send, "seq", swap)
    part1 = diagonal_call(1, *inputs, cum)
    gated, sums = gated_call(core, own, recv, first, cum, c_in, norm_weight, (*part0, *part1))
    sums = lax.all_to_all(sums, "tp", 0, 0, tiled=True)
    return scale_call(sums, gated)


def solution(mesh):
    return jax.shard_map(
        shards,
        mesh=mesh,
        in_specs=(
            P("seq", "tp"),
            P("seq", "tp"),
            P("seq", "tp"),
            P("seq", "tp"),
            P("tp", "seq"),
            P("tp"),
            P("tp"),
        ),
        out_specs=P("seq", "tp"),
        check_vma=False,
    )
```

```python
import functools

import jax
import jax.numpy as jnp
from jax import lax
from jax.experimental import pallas as pl
from jax.experimental.pallas import tpu as pltpu
from jax.sharding import PartitionSpec as P

HEAD_TOTAL = 64
HEAD_DIM = 128
STATE = 128
BLOCK = 256
CHIPS = 32

epsilon = 1e-05

HEADS = 8
TOK = 512
WIDTH = HEADS * HEAD_DIM
HALF = WIDTH // 2
ROWS = STATE // CHIPS

VMEM_BYTES = 16 << 20
f32 = jnp.float32
bf16 = jnp.bfloat16


def params():
    return pltpu.CompilerParams(vmem_limit_bytes=VMEM_BYTES)


def smem_spec():
    return pl.BlockSpec(memory_space=pltpu.SMEM)


def vmem_spec():
    return pl.BlockSpec(memory_space=pltpu.VMEM)


def hbm_spec():
    return pl.BlockSpec(memory_space=pltpu.HBM)


def head_columns(head):
    return slice(head * HEAD_DIM, (head + 1) * HEAD_DIM)


def split3(value):
    high = value.astype(bf16)
    rest = value - high.astype(f32)
    middle = rest.astype(bf16)
    low = (rest - middle.astype(f32)).astype(bf16)
    return high, middle, low


def state_kernel(
    core_ref, x_hbm, z_hbm, b_hbm, c_hbm, decay_hbm, skip_hbm,
    first_ref, send_ref, keep_ref, cum_ref, skip_ref, x_ref, z_ref, b_ref, c_ref,
    decay_ref, skip_smem, sems,
):
    copies = [
        pltpu.make_async_copy(source, target, sems.at[index])
        for index, (source, target) in enumerate(
            (
                (decay_hbm, decay_ref),
                (b_hbm, b_ref),
                (x_hbm, x_ref),
                (skip_hbm, skip_smem),
                (c_hbm, c_ref),
                (z_hbm, z_ref),
            )
        )
    ]
    for copy in copies:
        copy.start()
    row = lax.broadcasted_iota(jnp.int32, (BLOCK, BLOCK), 0)
    col = lax.broadcasted_iota(jnp.int32, (BLOCK, BLOCK), 1)
    upper = jnp.where(row <= col, 1.0, 0.0).astype(bf16)
    copies[0].wait()
    copies[1].wait()
    b_t = b_ref[...].astype(f32).T
    logs = jnp.log2(decay_ref[...])
    totals = []
    weights = []
    for block in range(2):
        span = slice(block * BLOCK, (block + 1) * BLOCK)
        total = jnp.zeros((HEADS, BLOCK), f32)
        for part in reversed(split3(logs[:, span])):
            total = total + jnp.dot(part, upper, preferred_element_type=f32)
        cum_ref[:, span] = total
        last = total[:, BLOCK - 1 :]
        totals.append(last)
        weights.append(jnp.exp2(last - total))
    second = jnp.exp2(totals[1])
    slab_logs = jnp.broadcast_to(totals[0] + totals[1], (HEADS, HEAD_DIM))
    copies[2].wait()
    low_core = core_ref[0] == 0
    for pair in range(4):
        slabs = []
        slab_rows = []
        for head in (pair, pair + 4):
            columns = head_columns(head)
            states = []
            for block in range(2):
                span = slice(block * BLOCK, (block + 1) * BLOCK)
                b_weighted = (b_t[:, span] * weights[block][head : head + 1, :]).astype(bf16)
                states.append(jnp.dot(b_weighted, x_ref[span, columns], preferred_element_type=f32))
            first_ref[:, columns] = states[0]
            slabs.append(second[head : head + 1, :] * states[0] + states[1])
            slab_rows.append(jnp.broadcast_to(slab_logs[head : head + 1, :], (8, HEAD_DIM)))
        target = head_columns(pair)
        keep_ref[:STATE, target] = jnp.where(low_core, slabs[0], slabs[1])
        send_ref[:STATE, target] = jnp.where(low_core, slabs[1], slabs[0])
        keep_ref[STATE:, target] = jnp.where(low_core, slab_rows[0], slab_rows[1])
        send_ref[STATE:, target] = jnp.where(low_core, slab_rows[1], slab_rows[0])

    for copy in copies[3:]:
        copy.wait()
    for head in range(HEADS):
        skip_ref[head : head + 1, :] = jnp.full((1, HEAD_DIM), skip_smem[head], f32)


def state_call(core, x_in, z_in, b_in, c_in, decays, d_skip):
    half_shape = jax.ShapeDtypeStruct((STATE + 8, HALF), f32)
    arrays = [
        pltpu.with_memory_space_constraint(array, pltpu.HBM)
        for array in (x_in, z_in, b_in, c_in, decays, d_skip)
    ]
    return pl.pallas_call(
        state_kernel,
        in_specs=[smem_spec()] + [hbm_spec()] * 6,
        out_specs=[vmem_spec()] * 9,
        out_shape=[
            jax.ShapeDtypeStruct((STATE, WIDTH), f32),
            half_shape,
            half_shape,
            jax.ShapeDtypeStruct((HEADS, TOK), f32),
            jax.ShapeDtypeStruct((HEADS, HEAD_DIM), f32),
            jax.ShapeDtypeStruct((TOK, WIDTH), bf16),
            jax.ShapeDtypeStruct((TOK, WIDTH), bf16),
            jax.ShapeDtypeStruct((TOK, STATE), bf16),
            jax.ShapeDtypeStruct((TOK, STATE), bf16),
        ],
        scratch_shapes=[
            pltpu.VMEM((HEADS, TOK), f32),
            pltpu.SMEM((HEADS,), f32),
            pltpu.SemaphoreType.DMA((6,)),
        ],
        compiler_params=params(),
        name="slab_state",
    )(core, *arrays)


def chip_kernel(core_ref, keep_ref, recv_ref, pay_ref, base_ref):
    def write(early_ref, late_ref):
        base_ref[...] = early_ref[...]
        chip_logs = []
        for head in range(4):
            columns = head_columns(head)
            late_log = late_ref[STATE : STATE + 1, columns]
            chip_logs.append(early_ref[STATE : STATE + 1, columns] + late_log)
            state = jnp.exp2(late_log) * early_ref[:STATE, columns] + late_ref[:STATE, columns]
            for chip in range(CHIPS):
                for part in range(2):
                    first_row = chip * ROWS + 2 * part
                    pay_ref[chip, :, head_columns(4 * part + head)] = state[first_row : first_row + 2, :]
        left = lax.broadcasted_iota(jnp.int32, (1, HEAD_DIM), 1) < HEAD_DIM // 2
        for part in range(2):
            row = jnp.where(left, chip_logs[2 * part], chip_logs[2 * part + 1])
            for chip in range(CHIPS):
                pay_ref[chip, part : part + 1, WIDTH:] = row

    @pl.when(core_ref[0] == 0)
    def _():
        write(keep_ref, recv_ref)

    @pl.when(core_ref[0] != 0)
    def _():
        write(recv_ref, keep_ref)


def chip_call(core, keep, recv):
    return pl.pallas_call(
        chip_kernel,
        in_specs=[smem_spec(), vmem_spec(), vmem_spec()],
        out_specs=[vmem_spec(), vmem_spec()],
        out_shape=[
            jax.ShapeDtypeStruct((CHIPS, 2, WIDTH + HEAD_DIM), f32),
            jax.ShapeDtypeStruct((STATE + 8, HALF), f32),
        ],
        compiler_params=params(),
        name="chip_state",
    )(core, keep, recv)


def scan_kernel(pay_ref, out_ref):
    carries = [[jnp.zeros((2, HEAD_DIM), f32) for _ in range(2)] for _ in range(4)]
    for chip in range(CHIPS):
        factors = jnp.exp2(pay_ref[chip, :, WIDTH:])
        for head in range(4):
            lane = (head % 2) * (HEAD_DIM // 2)
            factor = factors[head // 2 : head // 2 + 1, lane : lane + 1]
            for part in range(2):
                row = 4 * head + 2 * part
                carry = carries[head][part]
                out_ref[chip, row : row + 2, :] = carry
                state = pay_ref[chip, :, head_columns(4 * part + head)]
                carries[head][part] = factor * carry + state


def scan_call(pay):
    return pl.pallas_call(
        scan_kernel,
        in_specs=[vmem_spec()],
        out_specs=vmem_spec(),
        out_shape=jax.ShapeDtypeStruct((CHIPS, 4 * ROWS, HEAD_DIM), f32),
        compiler_params=params(),
        name="chip_scan",
    )(pay)


def entry_kernel(core_ref, pre_ref, base_ref, send_ref, own_ref):
    def write(plain_ref, moved_ref):
        for head in range(4):
            columns = head_columns(head)
            factor = jnp.exp2(base_ref[STATE : STATE + 1, columns])
            rows = slice(head * ROWS, (head + 1) * ROWS)
            entry = jnp.concatenate([pre_ref[chip, rows, :] for chip in range(CHIPS)], axis=0)
            plain_ref[:, columns] = entry
            moved_ref[:, columns] = factor * entry + base_ref[:STATE, columns]

    @pl.when(core_ref[0] == 0)
    def _():
        write(own_ref, send_ref)

    @pl.when(core_ref[0] != 0)
    def _():
        write(send_ref, own_ref)


def entry_call(core, pre, base):
    half_shape = jax.ShapeDtypeStruct((STATE, HALF), f32)
    return pl.pallas_call(
        entry_kernel,
        in_specs=[smem_spec(), vmem_spec(), vmem_spec()],
        out_specs=[vmem_spec(), vmem_spec()],
        out_shape=[half_shape, half_shape],
        compiler_params=params(),
        name="slab_entry",
    )(core, pre, base)


def diagonal_kernel(block, skip_ref, x_ref, z_ref, b_ref, c_ref, cum_ref, plain_ref, gain_ref):
    tokens = slice(block * BLOCK, (block + 1) * BLOCK)
    start = block * BLOCK
    cum = cum_ref[:, tokens]
    cum_t = cum.T
    row = lax.broadcasted_iota(jnp.int32, (128, 128), 0)
    col = lax.broadcasted_iota(jnp.int32, (128, 128), 1)
    causal = row >= col
    c_block = c_ref[tokens, :]
    b_block = b_ref[tokens, :]
    scores = []
    for tile in range(2):
        rows = slice(tile * 128, (tile + 1) * 128)
        for other in range(tile + 1):
            across = slice(other * 128, (other + 1) * 128)
            scores.append(
                lax.dot_general(
                    c_block[rows], b_block[across], (((1,), (1,)), ((), ())), preferred_element_type=f32
                )
            )
    for head in range(HEADS):
        columns = head_columns(head)
        cum_row = cum[head : head + 1, :]
        for tile in range(2):
            rows = slice(tile * 128, (tile + 1) * 128)
            here = slice(start + tile * 128, start + (tile + 1) * 128)
            cum_col = jnp.broadcast_to(cum_t[rows, head : head + 1], (128, HEAD_DIM))
            exponent = jnp.where(causal, cum_col - cum_row[:, rows], -jnp.inf)
            weights = (scores[0 if tile == 0 else 2] * jnp.exp2(exponent)).astype(bf16)
            if tile == 1:
                before = (scores[1] * jnp.exp2(cum_col - cum_row[:, :128])).astype(bf16)
                weights = jnp.concatenate([before, weights], axis=1)
            x_head = x_ref[slice(start, start + (tile + 1) * 128), columns]
            y = jnp.dot(weights, x_head, preferred_element_type=f32)
            y = y + skip_ref[head : head + 1, :] * x_ref[here, columns].astype(f32)
            half_z = 0.5 * z_ref[here, columns].astype(f32)
            gate = half_z + half_z * jnp.tanh(half_z)
            plain_ref[rows, columns] = y * gate
            gain_ref[rows, columns] = jnp.exp2(cum_col) * gate


def diagonal_call(block, skip, x_in, z_in, b_in, c_in, cum):
    shape = jax.ShapeDtypeStruct((BLOCK, WIDTH), f32)
    return pl.pallas_call(
        functools.partial(diagonal_kernel, block),
        in_specs=[vmem_spec()] * 6,
        out_specs=[vmem_spec(), vmem_spec()],
        out_shape=[shape, shape],
        compiler_params=params(),
        cost_estimate=pl.CostEstimate(
            flops=300_000_000, bytes_accessed=3_500_000, transcendentals=1_000_000
        ),
        name="diagonal",
    )(skip, x_in, z_in, b_in, c_in, cum)


def column_to_row(column):
    row = lax.broadcasted_iota(jnp.int32, (128, 128), 0)
    col = lax.broadcasted_iota(jnp.int32, (128, 128), 1)
    spread = jnp.where(row == col, jnp.broadcast_to(column, (128, 128)), 0.0)
    return jnp.sum(spread, axis=0, keepdims=True)


def gated_kernel(
    core_ref, own_ref, recv_ref, first_ref, cum_ref, c_ref, weight_ref,
    plain0_ref, gain0_ref, plain1_ref, gain1_ref, gated_ref, sum_ref, entry,
):
    core = core_ref[0]
    entry[:, pl.ds(pl.multiple_of(core * HALF, HALF), HALF)] = own_ref[...]
    entry[:, pl.ds(pl.multiple_of((1 - core) * HALF, HALF), HALF)] = recv_ref[...]
    weight = weight_ref[...].astype(f32)
    factors = jnp.exp2(cum_ref[:, BLOCK - 1 : BLOCK])
    for block in range(2):
        plain_ref, gain_ref = ((plain0_ref, gain0_ref), (plain1_ref, gain1_ref))[block]
        tokens = slice(block * BLOCK, (block + 1) * BLOCK)
        squares = jnp.zeros((BLOCK, HEAD_DIM), f32)
        for pair in range(4):
            states = []
            for head in (2 * pair, 2 * pair + 1):
                columns = head_columns(head)
                state = entry[:, columns]
                if block == 1:
                    state = factors[head : head + 1, :] * state + first_ref[:, columns]
                states.append(state.astype(bf16))
            columns = slice(pair * 256, (pair + 1) * 256)
            off = jnp.dot(
                c_ref[tokens, :], jnp.concatenate(states, axis=1), preferred_element_type=f32
            )
            gated = plain_ref[:, columns] + gain_ref[:, columns] * off
            gated_ref[tokens, columns] = gated * weight[:, columns]
            square = gated * gated
            squares = squares + square[:, :128] + square[:, 128:]
        column = jnp.sum(squares, axis=1, keepdims=True)
        rows = jnp.concatenate([column_to_row(column[:128]), column_to_row(column[128:])], axis=0)
        for peer in range(8):
            sum_ref[peer, 2 * block : 2 * block + 2, :] = rows


def gated_call(core, own, recv, first, cum, c_in, norm_weight, parts):
    return pl.pallas_call(
        gated_kernel,
        in_specs=[smem_spec()] + [vmem_spec()] * 10,
        out_specs=[vmem_spec(), vmem_spec()],
        out_shape=[
            jax.ShapeDtypeStruct((TOK, WIDTH), f32),
            jax.ShapeDtypeStruct((8, 4, 128), f32),
        ],
        scratch_shapes=[pltpu.VMEM((STATE, WIDTH), f32)],
        compiler_params=params(),
        name="gated",
    )(core, own, recv, first, cum, c_in, norm_weight.reshape(1, WIDTH), *parts)


def scale_kernel(sums_ref, gated_ref, out_hbm, buffer, sems):
    total = jnp.sum(sums_ref[...], axis=0)
    inverse = lax.rsqrt(total / (HEAD_TOTAL * HEAD_DIM) + epsilon)
    copies = []
    for part in range(4):
        tokens = slice(part * 128, (part + 1) * 128)
        column = jnp.broadcast_to(inverse[part : part + 1, :], (128, 128)).T
        for head in range(HEADS):
            columns = head_columns(head)
            buffer[tokens, columns] = (gated_ref[tokens, columns] * column).astype(bf16)
        copy = pltpu.make_async_copy(buffer.at[tokens, :], out_hbm.at[tokens, :], sems.at[part])
        copy.start()
        copies.append(copy)
    for copy in copies:
        copy.wait()


def scale_call(sums, gated):
    return pl.pallas_call(
        scale_kernel,
        in_specs=[vmem_spec(), vmem_spec()],
        out_specs=hbm_spec(),
        out_shape=jax.ShapeDtypeStruct((TOK, WIDTH), bf16),
        scratch_shapes=[pltpu.VMEM((TOK, WIDTH), bf16), pltpu.SemaphoreType.DMA((4,))],
        compiler_params=params(),
        name="scale",
    )(sums, gated)


def shards(x_in, z_in, b_in, c_in, decays, d_skip, norm_weight):
    core = (lax.axis_index("seq") % 2).astype(jnp.int32).reshape(1)
    swap = [(i, i ^ 1) for i in range(2 * CHIPS)]
    groups = [[2 * chip + c for chip in range(CHIPS)] for c in range(2)]
    first, send, keep, cum, *inputs = state_call(core, x_in, z_in, b_in, c_in, decays, d_skip)
    c_in = inputs[-1]
    recv = lax.ppermute(send, "seq", swap)
    part0 = diagonal_call(0, *inputs, cum)
    recv, *part0 = lax.optimization_barrier((recv, *part0))
    pay, base = chip_call(core, keep, recv)
    pay = lax.all_to_all(pay, "seq", 0, 0, axis_index_groups=groups, tiled=True)
    pre = scan_call(pay)
    pre = lax.all_to_all(pre, "seq", 0, 0, axis_index_groups=groups, tiled=True)
    send, own = entry_call(core, pre, base)
    recv = lax.ppermute(send, "seq", swap)
    part1 = diagonal_call(1, *inputs, cum)
    gated, sums = gated_call(core, own, recv, first, cum, c_in, norm_weight, (*part0, *part1))
    sums = lax.all_to_all(sums, "tp", 0, 0, tiled=True)
    return scale_call(sums, gated)


def solution(mesh):
    return jax.shard_map(
        shards,
        mesh=mesh,
        in_specs=(
            P("seq", "tp"),
            P("seq", "tp"),
            P("seq", "tp"),
            P("seq", "tp"),
            P("tp", "seq"),
            P("tp"),
            P("tp"),
        ),
        out_specs=P("seq", "tp"),
        check_vma=False,
    )
```

```python
import functools

import jax
import jax.numpy as jnp
from jax import lax
from jax.experimental import pallas as pl
from jax.experimental.pallas import tpu as pltpu
from jax.sharding import PartitionSpec as P

HEAD_TOTAL = 64
HEAD_DIM = 128
STATE = 128
BLOCK = 256
CHIPS = 32

epsilon = 1e-05

HEADS = 8
TOK = 512
WIDTH = HEADS * HEAD_DIM
HALF = WIDTH // 2
ROWS = STATE // CHIPS

VMEM_BYTES = 16 << 20
f32 = jnp.float32
bf16 = jnp.bfloat16


def params():
    return pltpu.CompilerParams(vmem_limit_bytes=VMEM_BYTES)


def smem_spec():
    return pl.BlockSpec(memory_space=pltpu.SMEM)


def vmem_spec():
    return pl.BlockSpec(memory_space=pltpu.VMEM)


def hbm_spec():
    return pl.BlockSpec(memory_space=pltpu.HBM)


def head_columns(head):
    return slice(head * HEAD_DIM, (head + 1) * HEAD_DIM)


def split3(value):
    high = value.astype(bf16)
    rest = value - high.astype(f32)
    middle = rest.astype(bf16)
    low = (rest - middle.astype(f32)).astype(bf16)
    return high, middle, low


def state_kernel(
    core_ref, x_hbm, z_hbm, b_hbm, c_hbm, decay_hbm, skip_hbm,
    first_ref, send_ref, keep_ref, cum_ref, skip_ref, x_ref, z_ref, b_ref, c_ref,
    decay_ref, skip_smem, sems,
):
    copies = [
        pltpu.make_async_copy(source, target, sems.at[index])
        for index, (source, target) in enumerate(
            (
                (decay_hbm, decay_ref),
                (b_hbm, b_ref),
                (x_hbm, x_ref),
                (skip_hbm, skip_smem),
                (c_hbm, c_ref),
                (z_hbm, z_ref),
            )
        )
    ]
    for copy in copies:
        copy.start()
    row = lax.broadcasted_iota(jnp.int32, (BLOCK, BLOCK), 0)
    col = lax.broadcasted_iota(jnp.int32, (BLOCK, BLOCK), 1)
    upper = jnp.where(row <= col, 1.0, 0.0).astype(bf16)
    copies[0].wait()
    copies[1].wait()
    b_t = b_ref[...].astype(f32).T
    logs = jnp.log2(decay_ref[...])
    totals = []
    weights = []
    for block in range(2):
        span = slice(block * BLOCK, (block + 1) * BLOCK)
        total = jnp.zeros((HEADS, BLOCK), f32)
        for part in reversed(split3(logs[:, span])):
            total = total + jnp.dot(part, upper, preferred_element_type=f32)
        cum_ref[:, span] = total
        last = total[:, BLOCK - 1 :]
        totals.append(last)
        weights.append(jnp.exp2(last - total))
    second = jnp.exp2(totals[1])
    slab_logs = jnp.broadcast_to(totals[0] + totals[1], (HEADS, HEAD_DIM))
    copies[2].wait()
    low_core = core_ref[0] == 0
    for pair in range(4):
        slabs = []
        slab_rows = []
        for head in (pair, pair + 4):
            columns = head_columns(head)
            states = []
            for block in range(2):
                span = slice(block * BLOCK, (block + 1) * BLOCK)
                b_weighted = (b_t[:, span] * weights[block][head : head + 1, :]).astype(bf16)
                states.append(jnp.dot(b_weighted, x_ref[span, columns], preferred_element_type=f32))
            first_ref[:, columns] = states[0]
            slabs.append(second[head : head + 1, :] * states[0] + states[1])
            slab_rows.append(jnp.broadcast_to(slab_logs[head : head + 1, :], (8, HEAD_DIM)))
        target = head_columns(pair)
        keep_ref[:STATE, target] = jnp.where(low_core, slabs[0], slabs[1])
        send_ref[:STATE, target] = jnp.where(low_core, slabs[1], slabs[0])
        keep_ref[STATE:, target] = jnp.where(low_core, slab_rows[0], slab_rows[1])
        send_ref[STATE:, target] = jnp.where(low_core, slab_rows[1], slab_rows[0])

    for copy in copies[3:]:
        copy.wait()
    for head in range(HEADS):
        skip_ref[head : head + 1, :] = jnp.full((1, HEAD_DIM), skip_smem[head], f32)


def state_call(core, x_in, z_in, b_in, c_in, decays, d_skip):
    half_shape = jax.ShapeDtypeStruct((STATE + 8, HALF), f32)
    arrays = [
        pltpu.with_memory_space_constraint(array, pltpu.HBM)
        for array in (x_in, z_in, b_in, c_in, decays, d_skip)
    ]
    return pl.pallas_call(
        state_kernel,
        in_specs=[smem_spec()] + [hbm_spec()] * 6,
        out_specs=[vmem_spec()] * 9,
        out_shape=[
            jax.ShapeDtypeStruct((STATE, WIDTH), f32),
            half_shape,
            half_shape,
            jax.ShapeDtypeStruct((HEADS, TOK), f32),
            jax.ShapeDtypeStruct((HEADS, HEAD_DIM), f32),
            jax.ShapeDtypeStruct((TOK, WIDTH), bf16),
            jax.ShapeDtypeStruct((TOK, WIDTH), bf16),
            jax.ShapeDtypeStruct((TOK, STATE), bf16),
            jax.ShapeDtypeStruct((TOK, STATE), bf16),
        ],
        scratch_shapes=[
            pltpu.VMEM((HEADS, TOK), f32),
            pltpu.SMEM((HEADS,), f32),
            pltpu.SemaphoreType.DMA((6,)),
        ],
        compiler_params=params(),
        name="slab_state",
    )(core, *arrays)


def chip_kernel(core_ref, keep_ref, recv_ref, pay_ref, base_ref):
    def write(early_ref, late_ref):
        base_ref[...] = early_ref[...]
        chip_logs = []
        for head in range(4):
            columns = head_columns(head)
            late_log = late_ref[STATE : STATE + 1, columns]
            chip_logs.append(early_ref[STATE : STATE + 1, columns] + late_log)
            state = jnp.exp2(late_log) * early_ref[:STATE, columns] + late_ref[:STATE, columns]
            for chip in range(CHIPS):
                for part in range(2):
                    first_row = chip * ROWS + 2 * part
                    pay_ref[chip, :, head_columns(4 * part + head)] = state[first_row : first_row + 2, :]
        left = lax.broadcasted_iota(jnp.int32, (1, HEAD_DIM), 1) < HEAD_DIM // 2
        for part in range(2):
            row = jnp.where(left, chip_logs[2 * part], chip_logs[2 * part + 1])
            for chip in range(CHIPS):
                pay_ref[chip, part : part + 1, WIDTH:] = row

    @pl.when(core_ref[0] == 0)
    def _():
        write(keep_ref, recv_ref)

    @pl.when(core_ref[0] != 0)
    def _():
        write(recv_ref, keep_ref)


def chip_call(core, keep, recv):
    return pl.pallas_call(
        chip_kernel,
        in_specs=[smem_spec(), vmem_spec(), vmem_spec()],
        out_specs=[vmem_spec(), vmem_spec()],
        out_shape=[
            jax.ShapeDtypeStruct((CHIPS, 2, WIDTH + HEAD_DIM), f32),
            jax.ShapeDtypeStruct((STATE + 8, HALF), f32),
        ],
        compiler_params=params(),
        name="chip_state",
    )(core, keep, recv)


def scan_kernel(pay_ref, out_ref):
    carries = [[jnp.zeros((2, HEAD_DIM), f32) for _ in range(2)] for _ in range(4)]
    for chip in range(CHIPS):
        factors = jnp.exp2(pay_ref[chip, :, WIDTH:])
        for head in range(4):
            lane = (head % 2) * (HEAD_DIM // 2)
            factor = factors[head // 2 : head // 2 + 1, lane : lane + 1]
            for part in range(2):
                row = 4 * head + 2 * part
                carry = carries[head][part]
                out_ref[chip, row : row + 2, :] = carry
                state = pay_ref[chip, :, head_columns(4 * part + head)]
                carries[head][part] = factor * carry + state


def scan_call(pay):
    return pl.pallas_call(
        scan_kernel,
        in_specs=[vmem_spec()],
        out_specs=vmem_spec(),
        out_shape=jax.ShapeDtypeStruct((CHIPS, 4 * ROWS, HEAD_DIM), f32),
        compiler_params=params(),
        name="chip_scan",
    )(pay)


def entry_kernel(core_ref, pre_ref, base_ref, send_ref, own_ref):
    def write(plain_ref, moved_ref):
        for head in range(4):
            columns = head_columns(head)
            factor = jnp.exp2(base_ref[STATE : STATE + 1, columns])
            rows = slice(head * ROWS, (head + 1) * ROWS)
            entry = jnp.concatenate([pre_ref[chip, rows, :] for chip in range(CHIPS)], axis=0)
            plain_ref[:, columns] = entry
            moved_ref[:, columns] = factor * entry + base_ref[:STATE, columns]

    @pl.when(core_ref[0] == 0)
    def _():
        write(own_ref, send_ref)

    @pl.when(core_ref[0] != 0)
    def _():
        write(send_ref, own_ref)


def entry_call(core, pre, base):
    half_shape = jax.ShapeDtypeStruct((STATE, HALF), f32)
    return pl.pallas_call(
        entry_kernel,
        in_specs=[smem_spec(), vmem_spec(), vmem_spec()],
        out_specs=[vmem_spec(), vmem_spec()],
        out_shape=[half_shape, half_shape],
        compiler_params=params(),
        name="slab_entry",
    )(core, pre, base)


def diagonal_kernel(block, only, core_ref, skip_ref, x_ref, z_ref, b_ref, c_ref, cum_ref, *refs):
    if only is None:
        diagonal_body(block, skip_ref, x_ref, z_ref, b_ref, c_ref, cum_ref, *refs[-2:])
    else:

        @pl.when(core_ref[0] == only)
        def _():
            diagonal_body(block, skip_ref, x_ref, z_ref, b_ref, c_ref, cum_ref, *refs[-2:])


def diagonal_body(block, skip_ref, x_ref, z_ref, b_ref, c_ref, cum_ref, plain_ref, gain_ref):
    tokens = slice(block * BLOCK, (block + 1) * BLOCK)
    start = block * BLOCK
    cum = cum_ref[:, tokens]
    cum_t = cum.T
    row = lax.broadcasted_iota(jnp.int32, (128, 128), 0)
    col = lax.broadcasted_iota(jnp.int32, (128, 128), 1)
    causal = row >= col
    c_block = c_ref[tokens, :]
    b_block = b_ref[tokens, :]
    scores = []
    for tile in range(2):
        rows = slice(tile * 128, (tile + 1) * 128)
        for other in range(tile + 1):
            across = slice(other * 128, (other + 1) * 128)
            scores.append(
                lax.dot_general(
                    c_block[rows], b_block[across], (((1,), (1,)), ((), ())), preferred_element_type=f32
                )
            )
    for head in range(HEADS):
        columns = head_columns(head)
        cum_row = cum[head : head + 1, :]
        for tile in range(2):
            rows = slice(tile * 128, (tile + 1) * 128)
            here = slice(start + tile * 128, start + (tile + 1) * 128)
            cum_col = jnp.broadcast_to(cum_t[rows, head : head + 1], (128, HEAD_DIM))
            exponent = jnp.where(causal, cum_col - cum_row[:, rows], -jnp.inf)
            weights = (scores[0 if tile == 0 else 2] * jnp.exp2(exponent)).astype(bf16)
            if tile == 1:
                before = (scores[1] * jnp.exp2(cum_col - cum_row[:, :128])).astype(bf16)
                weights = jnp.concatenate([before, weights], axis=1)
            x_head = x_ref[slice(start, start + (tile + 1) * 128), columns]
            y = jnp.dot(weights, x_head, preferred_element_type=f32)
            y = y + skip_ref[head : head + 1, :] * x_ref[here, columns].astype(f32)
            half_z = 0.5 * z_ref[here, columns].astype(f32)
            gate = half_z + half_z * jnp.tanh(half_z)
            plain_ref[rows, columns] = y * gate
            gain_ref[rows, columns] = jnp.exp2(cum_col) * gate


def diagonal_call(block, core, inputs, cum, only=None, previous=()):
    shape = jax.ShapeDtypeStruct((BLOCK, WIDTH), f32)
    return pl.pallas_call(
        functools.partial(diagonal_kernel, block, only),
        in_specs=[smem_spec()] + [vmem_spec()] * (6 + len(previous)),
        out_specs=[vmem_spec(), vmem_spec()],
        out_shape=[shape, shape],
        input_output_aliases={7 + index: index for index in range(len(previous))},
        compiler_params=params(),
        cost_estimate=pl.CostEstimate(
            flops=300_000_000, bytes_accessed=3_500_000, transcendentals=1_000_000
        ),
        name="diagonal",
    )(core, *inputs, cum, *previous)


def column_to_row(column):
    row = lax.broadcasted_iota(jnp.int32, (128, 128), 0)
    col = lax.broadcasted_iota(jnp.int32, (128, 128), 1)
    spread = jnp.where(row == col, jnp.broadcast_to(column, (128, 128)), 0.0)
    return jnp.sum(spread, axis=0, keepdims=True)


def gated_kernel(
    core_ref, own_ref, recv_ref, first_ref, cum_ref, c_ref, weight_ref,
    plain0_ref, gain0_ref, plain1_ref, gain1_ref, gated_ref, sum_ref, entry,
):
    core = core_ref[0]
    entry[:, pl.ds(pl.multiple_of(core * HALF, HALF), HALF)] = own_ref[...]
    entry[:, pl.ds(pl.multiple_of((1 - core) * HALF, HALF), HALF)] = recv_ref[...]
    weight = weight_ref[...].astype(f32)
    factors = jnp.exp2(cum_ref[:, BLOCK - 1 : BLOCK])
    for block in range(2):
        plain_ref, gain_ref = ((plain0_ref, gain0_ref), (plain1_ref, gain1_ref))[block]
        tokens = slice(block * BLOCK, (block + 1) * BLOCK)
        squares = jnp.zeros((BLOCK, HEAD_DIM), f32)
        for pair in range(4):
            states = []
            for head in (2 * pair, 2 * pair + 1):
                columns = head_columns(head)
                state = entry[:, columns]
                if block == 1:
                    state = factors[head : head + 1, :] * state + first_ref[:, columns]
                states.append(state.astype(bf16))
            columns = slice(pair * 256, (pair + 1) * 256)
            off = jnp.dot(
                c_ref[tokens, :], jnp.concatenate(states, axis=1), preferred_element_type=f32
            )
            gated = plain_ref[:, columns] + gain_ref[:, columns] * off
            gated_ref[tokens, columns] = gated * weight[:, columns]
            square = gated * gated
            squares = squares + square[:, :128] + square[:, 128:]
        column = jnp.sum(squares, axis=1, keepdims=True)
        rows = jnp.concatenate([column_to_row(column[:128]), column_to_row(column[128:])], axis=0)
        for peer in range(8):
            sum_ref[peer, 2 * block : 2 * block + 2, :] = rows


def gated_call(core, own, recv, first, cum, c_in, norm_weight, parts):
    return pl.pallas_call(
        gated_kernel,
        in_specs=[smem_spec()] + [vmem_spec()] * 10,
        out_specs=[vmem_spec(), vmem_spec()],
        out_shape=[
            jax.ShapeDtypeStruct((TOK, WIDTH), f32),
            jax.ShapeDtypeStruct((8, 4, 128), f32),
        ],
        scratch_shapes=[pltpu.VMEM((STATE, WIDTH), f32)],
        compiler_params=params(),
        name="gated",
    )(core, own, recv, first, cum, c_in, norm_weight.reshape(1, WIDTH), *parts)


def scale_kernel(sums_ref, gated_ref, out_hbm, buffer, sems):
    total = jnp.sum(sums_ref[...], axis=0)
    inverse = lax.rsqrt(total / (HEAD_TOTAL * HEAD_DIM) + epsilon)
    copies = []
    for part in range(4):
        tokens = slice(part * 128, (part + 1) * 128)
        column = jnp.broadcast_to(inverse[part : part + 1, :], (128, 128)).T
        for head in range(HEADS):
            columns = head_columns(head)
            buffer[tokens, columns] = (gated_ref[tokens, columns] * column).astype(bf16)
        copy = pltpu.make_async_copy(buffer.at[tokens, :], out_hbm.at[tokens, :], sems.at[part])
        copy.start()
        copies.append(copy)
    for copy in copies:
        copy.wait()


def scale_call(sums, gated):
    return pl.pallas_call(
        scale_kernel,
        in_specs=[vmem_spec(), vmem_spec()],
        out_specs=hbm_spec(),
        out_shape=jax.ShapeDtypeStruct((TOK, WIDTH), bf16),
        scratch_shapes=[pltpu.VMEM((TOK, WIDTH), bf16), pltpu.SemaphoreType.DMA((4,))],
        compiler_params=params(),
        name="scale",
    )(sums, gated)


def shards(x_in, z_in, b_in, c_in, decays, d_skip, norm_weight):
    core = (lax.axis_index("seq") % 2).astype(jnp.int32).reshape(1)
    swap = [(i, i ^ 1) for i in range(2 * CHIPS)]
    groups = [[2 * chip + c for chip in range(CHIPS)] for c in range(2)]
    first, send, keep, cum, *inputs = state_call(core, x_in, z_in, b_in, c_in, decays, d_skip)
    c_in = inputs[-1]
    recv = lax.ppermute(send, "seq", swap)
    part0 = diagonal_call(0, core, inputs, cum)
    recv, *part0 = lax.optimization_barrier((recv, *part0))
    pay, base = chip_call(core, keep, recv)
    part1 = diagonal_call(1, core, inputs, cum, only=1)
    pay, *part1 = lax.optimization_barrier((pay, *part1))
    pay = lax.all_to_all(pay, "seq", 0, 0, axis_index_groups=groups, tiled=True)
    pre = scan_call(pay)
    pre = lax.all_to_all(pre, "seq", 0, 0, axis_index_groups=groups, tiled=True)
    send, own = entry_call(core, pre, base)
    send, *part1 = lax.optimization_barrier((send, *part1))
    recv = lax.ppermute(send, "seq", swap)
    part1 = diagonal_call(1, core, inputs, cum, only=0, previous=part1)
    gated, sums = gated_call(core, own, recv, first, cum, c_in, norm_weight, (*part0, *part1))
    sums = lax.all_to_all(sums, "tp", 0, 0, tiled=True)
    return scale_call(sums, gated)


def solution(mesh):
    return jax.shard_map(
        shards,
        mesh=mesh,
        in_specs=(
            P("seq", "tp"),
            P("seq", "tp"),
            P("seq", "tp"),
            P("seq", "tp"),
            P("tp", "seq"),
            P("tp"),
            P("tp"),
        ),
        out_specs=P("seq", "tp"),
        check_vma=False,
    )
```

```python
import functools

import jax
import jax.numpy as jnp
from jax import lax
from jax.experimental import pallas as pl
from jax.experimental.pallas import tpu as pltpu
from jax.sharding import PartitionSpec as P

HEAD_TOTAL = 64
HEAD_DIM = 128
STATE = 128
BLOCK = 256
CHIPS = 32

epsilon = 1e-05

HEADS = 8
TOK = 512
WIDTH = HEADS * HEAD_DIM
HALF = WIDTH // 2
ROWS = STATE // CHIPS

VMEM_BYTES = 16 << 20
f32 = jnp.float32
bf16 = jnp.bfloat16


def params():
    return pltpu.CompilerParams(vmem_limit_bytes=VMEM_BYTES)


def smem_spec():
    return pl.BlockSpec(memory_space=pltpu.SMEM)


def vmem_spec():
    return pl.BlockSpec(memory_space=pltpu.VMEM)


def hbm_spec():
    return pl.BlockSpec(memory_space=pltpu.HBM)


def head_columns(head):
    return slice(head * HEAD_DIM, (head + 1) * HEAD_DIM)


def split3(value):
    high = value.astype(bf16)
    rest = value - high.astype(f32)
    middle = rest.astype(bf16)
    low = (rest - middle.astype(f32)).astype(bf16)
    return high, middle, low


def half_states(base, b_t, to_end, cum_ref, x_ref, first_ref, slab_ref):
    for index in range(4):
        head = base + index
        source = pl.ds(pl.multiple_of(head * HEAD_DIM, HEAD_DIM), HEAD_DIM)
        target = head_columns(index)
        weight = to_end[pl.ds(head, 1), :]
        cum = cum_ref[pl.ds(head, 1), :]
        last0 = cum[:, BLOCK - 1 : BLOCK]
        last1 = cum[:, 2 * BLOCK - 1 :]
        states = []
        for block in range(2):
            span = slice(block * BLOCK, (block + 1) * BLOCK)
            b_weighted = (b_t[:, span] * weight[:, span]).astype(bf16)
            states.append(jnp.dot(b_weighted, x_ref[span, source], preferred_element_type=f32))
        first_ref[:, target] = states[0]
        slab_ref[:STATE, target] = jnp.exp2(last1) * states[0] + states[1]
        slab_ref[STATE:, target] = jnp.broadcast_to(last0 + last1, (8, HEAD_DIM))


def send_state_kernel(
    core_ref, x_hbm, z_hbm, b_hbm, c_hbm, decay_hbm, skip_hbm,
    send_ref, first_ref, cum_ref, to_end_ref, b_t_ref, skip_ref, x_ref, z_ref, b_ref, c_ref,
    decay_ref, skip_smem, sems,
):
    copies = [
        pltpu.make_async_copy(source, target, sems.at[index])
        for index, (source, target) in enumerate(
            (
                (decay_hbm, decay_ref),
                (b_hbm, b_ref),
                (x_hbm, x_ref),
                (skip_hbm, skip_smem),
                (c_hbm, c_ref),
                (z_hbm, z_ref),
            )
        )
    ]
    for copy in copies:
        copy.start()
    row = lax.broadcasted_iota(jnp.int32, (BLOCK, BLOCK), 0)
    col = lax.broadcasted_iota(jnp.int32, (BLOCK, BLOCK), 1)
    upper = jnp.where(row <= col, 1.0, 0.0).astype(bf16)
    copies[0].wait()
    copies[1].wait()
    b_t = b_ref[...].astype(f32).T
    b_t_ref[...] = b_t
    logs = jnp.log2(decay_ref[...])
    for block in range(2):
        span = slice(block * BLOCK, (block + 1) * BLOCK)
        total = jnp.zeros((HEADS, BLOCK), f32)
        for part in reversed(split3(logs[:, span])):
            total = total + jnp.dot(part, upper, preferred_element_type=f32)
        cum_ref[:, span] = total
        to_end_ref[:, span] = jnp.exp2(total[:, BLOCK - 1 :] - total)
    copies[2].wait()
    half_states(4 * (1 - core_ref[0]), b_t, to_end_ref, cum_ref, x_ref, first_ref, send_ref)
    for copy in copies[3:]:
        copy.wait()
    for head in range(HEADS):
        skip_ref[head : head + 1, :] = jnp.full((1, HEAD_DIM), skip_smem[head], f32)


def send_state_call(core, x_in, z_in, b_in, c_in, decays, d_skip):
    arrays = [
        pltpu.with_memory_space_constraint(array, pltpu.HBM)
        for array in (x_in, z_in, b_in, c_in, decays, d_skip)
    ]
    return pl.pallas_call(
        send_state_kernel,
        in_specs=[smem_spec()] + [hbm_spec()] * 6,
        out_specs=[vmem_spec()] * 10,
        out_shape=[
            jax.ShapeDtypeStruct((STATE + 8, HALF), f32),
            jax.ShapeDtypeStruct((STATE, HALF), f32),
            jax.ShapeDtypeStruct((HEADS, TOK), f32),
            jax.ShapeDtypeStruct((HEADS, TOK), f32),
            jax.ShapeDtypeStruct((STATE, TOK), f32),
            jax.ShapeDtypeStruct((HEADS, HEAD_DIM), f32),
            jax.ShapeDtypeStruct((TOK, WIDTH), bf16),
            jax.ShapeDtypeStruct((TOK, WIDTH), bf16),
            jax.ShapeDtypeStruct((TOK, STATE), bf16),
            jax.ShapeDtypeStruct((TOK, STATE), bf16),
        ],
        scratch_shapes=[
            pltpu.VMEM((HEADS, TOK), f32),
            pltpu.SMEM((HEADS,), f32),
            pltpu.SemaphoreType.DMA((6,)),
        ],
        compiler_params=params(),
        name="send_state",
    )(core, *arrays)


def keep_state_kernel(core_ref, b_t_ref, to_end_ref, cum_ref, x_ref, keep_ref, first_ref):
    half_states(4 * core_ref[0], b_t_ref[...], to_end_ref, cum_ref, x_ref, first_ref, keep_ref)


def keep_state_call(core, b_t, to_end, cum, x_in):
    return pl.pallas_call(
        keep_state_kernel,
        in_specs=[smem_spec()] + [vmem_spec()] * 4,
        out_specs=[vmem_spec()] * 2,
        out_shape=[
            jax.ShapeDtypeStruct((STATE + 8, HALF), f32),
            jax.ShapeDtypeStruct((STATE, HALF), f32),
        ],
        compiler_params=params(),
        cost_estimate=pl.CostEstimate(
            flops=70_000_000, bytes_accessed=1_500_000, transcendentals=1_000
        ),
        name="keep_state",
    )(core, b_t, to_end, cum, x_in)


def chip_kernel(core_ref, keep_ref, recv_ref, pay_ref, base_ref):
    def write(early_ref, late_ref):
        base_ref[...] = early_ref[...]
        chip_logs = []
        for head in range(4):
            columns = head_columns(head)
            late_log = late_ref[STATE : STATE + 1, columns]
            chip_logs.append(early_ref[STATE : STATE + 1, columns] + late_log)
            state = jnp.exp2(late_log) * early_ref[:STATE, columns] + late_ref[:STATE, columns]
            for chip in range(CHIPS):
                for part in range(2):
                    first_row = chip * ROWS + 2 * part
                    pay_ref[chip, :, head_columns(4 * part + head)] = state[first_row : first_row + 2, :]
        left = lax.broadcasted_iota(jnp.int32, (1, HEAD_DIM), 1) < HEAD_DIM // 2
        for part in range(2):
            row = jnp.where(left, chip_logs[2 * part], chip_logs[2 * part + 1])
            for chip in range(CHIPS):
                pay_ref[chip, part : part + 1, WIDTH:] = row

    @pl.when(core_ref[0] == 0)
    def _():
        write(keep_ref, recv_ref)

    @pl.when(core_ref[0] != 0)
    def _():
        write(recv_ref, keep_ref)


def chip_call(core, keep, recv):
    return pl.pallas_call(
        chip_kernel,
        in_specs=[smem_spec(), vmem_spec(), vmem_spec()],
        out_specs=[vmem_spec(), vmem_spec()],
        out_shape=[
            jax.ShapeDtypeStruct((CHIPS, 2, WIDTH + HEAD_DIM), f32),
            jax.ShapeDtypeStruct((STATE + 8, HALF), f32),
        ],
        compiler_params=params(),
        name="chip_state",
    )(core, keep, recv)


def scan_kernel(pay_ref, out_ref):
    carries = [[jnp.zeros((2, HEAD_DIM), f32) for _ in range(2)] for _ in range(4)]
    for chip in range(CHIPS):
        factors = jnp.exp2(pay_ref[chip, :, WIDTH:])
        for head in range(4):
            lane = (head % 2) * (HEAD_DIM // 2)
            factor = factors[head // 2 : head // 2 + 1, lane : lane + 1]
            for part in range(2):
                row = 4 * head + 2 * part
                carry = carries[head][part]
                out_ref[chip, row : row + 2, :] = carry
                state = pay_ref[chip, :, head_columns(4 * part + head)]
                carries[head][part] = factor * carry + state


def scan_call(pay):
    return pl.pallas_call(
        scan_kernel,
        in_specs=[vmem_spec()],
        out_specs=vmem_spec(),
        out_shape=jax.ShapeDtypeStruct((CHIPS, 4 * ROWS, HEAD_DIM), f32),
        compiler_params=params(),
        name="chip_scan",
    )(pay)


def entry_kernel(core_ref, pre_ref, base_ref, send_ref, own_ref):
    def write(plain_ref, moved_ref):
        for head in range(4):
            columns = head_columns(head)
            factor = jnp.exp2(base_ref[STATE : STATE + 1, columns])
            rows = slice(head * ROWS, (head + 1) * ROWS)
            entry = jnp.concatenate([pre_ref[chip, rows, :] for chip in range(CHIPS)], axis=0)
            plain_ref[:, columns] = entry
            moved_ref[:, columns] = factor * entry + base_ref[:STATE, columns]

    @pl.when(core_ref[0] == 0)
    def _():
        write(own_ref, send_ref)

    @pl.when(core_ref[0] != 0)
    def _():
        write(send_ref, own_ref)


def entry_call(core, pre, base):
    half_shape = jax.ShapeDtypeStruct((STATE, HALF), f32)
    return pl.pallas_call(
        entry_kernel,
        in_specs=[smem_spec(), vmem_spec(), vmem_spec()],
        out_specs=[vmem_spec(), vmem_spec()],
        out_shape=[half_shape, half_shape],
        compiler_params=params(),
        name="slab_entry",
    )(core, pre, base)


def diagonal_kernel(block, skip_ref, x_ref, z_ref, b_ref, c_ref, cum_ref, plain_ref, gain_ref):
    tokens = slice(block * BLOCK, (block + 1) * BLOCK)
    start = block * BLOCK
    cum = cum_ref[:, tokens]
    cum_t = cum.T
    row = lax.broadcasted_iota(jnp.int32, (128, 128), 0)
    col = lax.broadcasted_iota(jnp.int32, (128, 128), 1)
    causal = row >= col
    c_block = c_ref[tokens, :]
    b_block = b_ref[tokens, :]
    scores = []
    for tile in range(2):
        rows = slice(tile * 128, (tile + 1) * 128)
        for other in range(tile + 1):
            across = slice(other * 128, (other + 1) * 128)
            scores.append(
                lax.dot_general(
                    c_block[rows], b_block[across], (((1,), (1,)), ((), ())), preferred_element_type=f32
                )
            )
    for head in range(HEADS):
        columns = head_columns(head)
        cum_row = cum[head : head + 1, :]
        for tile in range(2):
            rows = slice(tile * 128, (tile + 1) * 128)
            here = slice(start + tile * 128, start + (tile + 1) * 128)
            cum_col = jnp.broadcast_to(cum_t[rows, head : head + 1], (128, HEAD_DIM))
            exponent = jnp.where(causal, cum_col - cum_row[:, rows], -jnp.inf)
            weights = (scores[0 if tile == 0 else 2] * jnp.exp2(exponent)).astype(bf16)
            if tile == 1:
                before = (scores[1] * jnp.exp2(cum_col - cum_row[:, :128])).astype(bf16)
                weights = jnp.concatenate([before, weights], axis=1)
            x_head = x_ref[slice(start, start + (tile + 1) * 128), columns]
            y = jnp.dot(weights, x_head, preferred_element_type=f32)
            y = y + skip_ref[head : head + 1, :] * x_ref[here, columns].astype(f32)
            half_z = 0.5 * z_ref[here, columns].astype(f32)
            gate = half_z + half_z * jnp.tanh(half_z)
            plain_ref[rows, columns] = y * gate
            gain_ref[rows, columns] = jnp.exp2(cum_col) * gate


def diagonal_call(block, skip, x_in, z_in, b_in, c_in, cum):
    shape = jax.ShapeDtypeStruct((BLOCK, WIDTH), f32)
    return pl.pallas_call(
        functools.partial(diagonal_kernel, block),
        in_specs=[vmem_spec()] * 6,
        out_specs=[vmem_spec(), vmem_spec()],
        out_shape=[shape, shape],
        compiler_params=params(),
        cost_estimate=pl.CostEstimate(
            flops=300_000_000, bytes_accessed=3_500_000, transcendentals=1_000_000
        ),
        name="diagonal",
    )(skip, x_in, z_in, b_in, c_in, cum)


def column_to_row(column):
    row = lax.broadcasted_iota(jnp.int32, (128, 128), 0)
    col = lax.broadcasted_iota(jnp.int32, (128, 128), 1)
    spread = jnp.where(row == col, jnp.broadcast_to(column, (128, 128)), 0.0)
    return jnp.sum(spread, axis=0, keepdims=True)


def gated_half(
    base, entry_ref, first_ref, cum_ref, c_ref, weight_ref, parts, gated_ref, block
):
    plain_ref, gain_ref = parts[2 * block : 2 * block + 2]
    tokens = slice(block * BLOCK, (block + 1) * BLOCK)
    squares = None
    for pair in range(2):
        states = []
        for index in (2 * pair, 2 * pair + 1):
            columns = head_columns(index)
            state = entry_ref[:, columns]
            if block == 1:
                last = cum_ref[pl.ds(base + index, 1), :BLOCK][:, BLOCK - 1 :]
                state = jnp.exp2(last) * state + first_ref[:, columns]
            states.append(state.astype(bf16))
        off = jnp.dot(
            c_ref[tokens, :], jnp.concatenate(states, axis=1), preferred_element_type=f32
        )
        for index in (2 * pair, 2 * pair + 1):
            source = pl.ds(pl.multiple_of((base + index) * HEAD_DIM, HEAD_DIM), HEAD_DIM)
            part = off[:, head_columns(index - 2 * pair)]
            gated = plain_ref[:, source] + gain_ref[:, source] * part
            gated_ref[tokens, head_columns(index)] = gated * weight_ref[:, source]
            square = gated * gated
            squares = square if squares is None else squares + square
    return squares


def own_gated_kernel(
    core_ref, entry_ref, first_ref, cum_ref, c_ref, weight_ref,
    plain0_ref, gain0_ref, plain1_ref, gain1_ref, gated_ref, squares_ref,
):
    parts = (plain0_ref, gain0_ref, plain1_ref, gain1_ref)
    for block in range(2):
        tokens = slice(block * BLOCK, (block + 1) * BLOCK)
        squares_ref[tokens, :] = gated_half(
            4 * core_ref[0], entry_ref, first_ref, cum_ref, c_ref, weight_ref, parts, gated_ref, block
        )


def other_gated_kernel(
    core_ref, entry_ref, first_ref, cum_ref, c_ref, weight_ref,
    plain0_ref, gain0_ref, plain1_ref, gain1_ref, squares_ref, gated_ref, sum_ref,
):
    parts = (plain0_ref, gain0_ref, plain1_ref, gain1_ref)
    for block in range(2):
        tokens = slice(block * BLOCK, (block + 1) * BLOCK)
        squares = squares_ref[tokens, :] + gated_half(
            4 * (1 - core_ref[0]), entry_ref, first_ref, cum_ref, c_ref, weight_ref, parts, gated_ref, block
        )
        column = jnp.sum(squares, axis=1, keepdims=True)
        rows = jnp.concatenate([column_to_row(column[:128]), column_to_row(column[128:])], axis=0)
        for peer in range(8):
            sum_ref[peer, 2 * block : 2 * block + 2, :] = rows


def gated_call(core, entry, first, cum, c_in, weight, parts, squares=None):
    last = squares is not None
    extra = (squares,) if last else ()
    shape = jax.ShapeDtypeStruct((8, 4, 128) if last else (TOK, HEAD_DIM), f32)
    return pl.pallas_call(
        other_gated_kernel if last else own_gated_kernel,
        in_specs=[smem_spec()] + [vmem_spec()] * (9 + len(extra)),
        out_specs=[vmem_spec(), vmem_spec()],
        out_shape=[jax.ShapeDtypeStruct((TOK, HALF), f32), shape],
        compiler_params=params(),
        cost_estimate=pl.CostEstimate(
            flops=70_000_000, bytes_accessed=3_000_000, transcendentals=1_000
        ),
        name="other_gated" if last else "own_gated",
    )(core, entry, first, cum, c_in, weight, *parts, *extra)


def scale_kernel(core_ref, sums_ref, own_ref, other_ref, out_hbm, buffer, sems):
    total = jnp.sum(sums_ref[...], axis=0)
    inverse = lax.rsqrt(total / (HEAD_TOTAL * HEAD_DIM) + epsilon)
    core = core_ref[0]
    copies = []
    for part in range(4):
        tokens = slice(part * 128, (part + 1) * 128)
        column = jnp.broadcast_to(inverse[part : part + 1, :], (128, 128)).T
        for base, gated_ref in ((core * HALF, own_ref), ((1 - core) * HALF, other_ref)):
            for head in range(4):
                columns = pl.ds(pl.multiple_of(base + head * HEAD_DIM, HEAD_DIM), HEAD_DIM)
                scaled = gated_ref[tokens, head_columns(head)] * column
                buffer[tokens, columns] = scaled.astype(bf16)
        copy = pltpu.make_async_copy(buffer.at[tokens, :], out_hbm.at[tokens, :], sems.at[part])
        copy.start()
        copies.append(copy)
    for copy in copies:
        copy.wait()


def scale_call(core, sums, own, other):
    return pl.pallas_call(
        scale_kernel,
        in_specs=[smem_spec()] + [vmem_spec()] * 3,
        out_specs=hbm_spec(),
        out_shape=jax.ShapeDtypeStruct((TOK, WIDTH), bf16),
        scratch_shapes=[pltpu.VMEM((TOK, WIDTH), bf16), pltpu.SemaphoreType.DMA((4,))],
        compiler_params=params(),
        name="scale",
    )(core, sums, own, other)


def shards(x_in, z_in, b_in, c_in, decays, d_skip, norm_weight):
    core = (lax.axis_index("seq") % 2).astype(jnp.int32).reshape(1)
    swap = [(i, i ^ 1) for i in range(2 * CHIPS)]
    groups = [[2 * chip + c for chip in range(CHIPS)] for c in range(2)]
    send, first_send, cum, to_end, b_t, *inputs = send_state_call(
        core, x_in, z_in, b_in, c_in, decays, d_skip
    )
    skip, x_in, z_in, b_in, c_in = inputs
    recv = lax.ppermute(send, "seq", swap)
    keep, first_keep = keep_state_call(core, b_t, to_end, cum, x_in)
    part0 = diagonal_call(0, *inputs, cum)
    recv, *part0 = lax.optimization_barrier((recv, *part0))
    pay, base = chip_call(core, keep, recv)
    pay = lax.all_to_all(pay, "seq", 0, 0, axis_index_groups=groups, tiled=True)
    pre = scan_call(pay)
    pre = lax.all_to_all(pre, "seq", 0, 0, axis_index_groups=groups, tiled=True)
    send, own = entry_call(core, pre, base)
    recv = lax.ppermute(send, "seq", swap)
    parts = (*part0, *diagonal_call(1, *inputs, cum))
    weight = norm_weight.astype(f32).reshape(1, WIDTH)
    own_gated, squares = gated_call(core, own, first_keep, cum, c_in, weight, parts)
    other_gated, sums = gated_call(core, recv, first_send, cum, c_in, weight, parts, squares)
    sums = lax.all_to_all(sums, "tp", 0, 0, tiled=True)
    return scale_call(core, sums, own_gated, other_gated)


def solution(mesh):
    return jax.shard_map(
        shards,
        mesh=mesh,
        in_specs=(
            P("seq", "tp"),
            P("seq", "tp"),
            P("seq", "tp"),
            P("seq", "tp"),
            P("tp", "seq"),
            P("tp"),
            P("tp"),
        ),
        out_specs=P("seq", "tp"),
        check_vma=False,
    )
```

```python
import functools

import jax
import jax.numpy as jnp
from jax import lax
from jax.experimental import pallas as pl
from jax.experimental.pallas import tpu as pltpu
from jax.sharding import PartitionSpec as P

HEAD_TOTAL = 64
HEAD_DIM = 128
STATE = 128
BLOCK = 256
CHIPS = 32

epsilon = 1e-05

HEADS = 8
TOK = 512
WIDTH = HEADS * HEAD_DIM
HALF = WIDTH // 2
ROWS = STATE // CHIPS
PIECE = 4 * ROWS + 1

VMEM_BYTES = 16 << 20
f32 = jnp.float32
bf16 = jnp.bfloat16


def params():
    return pltpu.CompilerParams(vmem_limit_bytes=VMEM_BYTES)


def smem_spec():
    return pl.BlockSpec(memory_space=pltpu.SMEM)


def vmem_spec():
    return pl.BlockSpec(memory_space=pltpu.VMEM)


def hbm_spec():
    return pl.BlockSpec(memory_space=pltpu.HBM)


def head_columns(head):
    return slice(head * HEAD_DIM, (head + 1) * HEAD_DIM)


def split3(value):
    high = value.astype(bf16)
    rest = value - high.astype(f32)
    middle = rest.astype(bf16)
    low = (rest - middle.astype(f32)).astype(bf16)
    return high, middle, low


def state_kernel(
    core_ref, x_hbm, z_hbm, b_hbm, c_hbm, decay_hbm, skip_hbm,
    first_ref, send_ref, keep_ref, cum_ref, skip_ref, x_ref, z_ref, b_ref, c_ref,
    decay_ref, skip_smem, sems,
):
    copies = [
        pltpu.make_async_copy(source, target, sems.at[index])
        for index, (source, target) in enumerate(
            (
                (decay_hbm, decay_ref),
                (b_hbm, b_ref),
                (x_hbm, x_ref),
                (skip_hbm, skip_smem),
                (c_hbm, c_ref),
                (z_hbm, z_ref),
            )
        )
    ]
    for copy in copies:
        copy.start()
    row = lax.broadcasted_iota(jnp.int32, (BLOCK, BLOCK), 0)
    col = lax.broadcasted_iota(jnp.int32, (BLOCK, BLOCK), 1)
    upper = jnp.where(row <= col, 1.0, 0.0).astype(bf16)
    copies[0].wait()
    copies[1].wait()
    b_t = b_ref[...].astype(f32).T
    logs = jnp.log2(decay_ref[...])
    totals = []
    weights = []
    for block in range(2):
        span = slice(block * BLOCK, (block + 1) * BLOCK)
        total = jnp.zeros((HEADS, BLOCK), f32)
        for part in reversed(split3(logs[:, span])):
            total = total + jnp.dot(part, upper, preferred_element_type=f32)
        cum_ref[:, span] = total
        last = total[:, BLOCK - 1 :]
        totals.append(last)
        weights.append(jnp.exp2(last - total))
    second = jnp.exp2(totals[1])
    slab_logs = jnp.broadcast_to(totals[0] + totals[1], (HEADS, HEAD_DIM))
    copies[2].wait()
    low_core = core_ref[0] == 0
    for pair in range(4):
        slabs = []
        slab_rows = []
        for head in (pair, pair + 4):
            columns = head_columns(head)
            states = []
            for block in range(2):
                span = slice(block * BLOCK, (block + 1) * BLOCK)
                b_weighted = (b_t[:, span] * weights[block][head : head + 1, :]).astype(bf16)
                states.append(jnp.dot(b_weighted, x_ref[span, columns], preferred_element_type=f32))
            first_ref[:, columns] = states[0]
            slabs.append(second[head : head + 1, :] * states[0] + states[1])
            slab_rows.append(jnp.broadcast_to(slab_logs[head : head + 1, :], (8, HEAD_DIM)))
        target = head_columns(pair)
        keep_ref[:STATE, target] = jnp.where(low_core, slabs[0], slabs[1])
        send_ref[:STATE, target] = jnp.where(low_core, slabs[1], slabs[0])
        keep_ref[STATE:, target] = jnp.where(low_core, slab_rows[0], slab_rows[1])
        send_ref[STATE:, target] = jnp.where(low_core, slab_rows[1], slab_rows[0])

    for copy in copies[3:]:
        copy.wait()
    for head in range(HEADS):
        skip_ref[head : head + 1, :] = jnp.full((1, HEAD_DIM), skip_smem[head], f32)


def state_call(core, x_in, z_in, b_in, c_in, decays, d_skip):
    half_shape = jax.ShapeDtypeStruct((STATE + 8, HALF), f32)
    arrays = [
        pltpu.with_memory_space_constraint(array, pltpu.HBM)
        for array in (x_in, z_in, b_in, c_in, decays, d_skip)
    ]
    return pl.pallas_call(
        state_kernel,
        in_specs=[smem_spec()] + [hbm_spec()] * 6,
        out_specs=[vmem_spec()] * 9,
        out_shape=[
            jax.ShapeDtypeStruct((STATE, WIDTH), f32),
            half_shape,
            half_shape,
            jax.ShapeDtypeStruct((HEADS, TOK), f32),
            jax.ShapeDtypeStruct((HEADS, HEAD_DIM), f32),
            jax.ShapeDtypeStruct((TOK, WIDTH), bf16),
            jax.ShapeDtypeStruct((TOK, WIDTH), bf16),
            jax.ShapeDtypeStruct((TOK, STATE), bf16),
            jax.ShapeDtypeStruct((TOK, STATE), bf16),
        ],
        scratch_shapes=[
            pltpu.VMEM((HEADS, TOK), f32),
            pltpu.SMEM((HEADS,), f32),
            pltpu.SemaphoreType.DMA((6,)),
        ],
        compiler_params=params(),
        name="slab_state",
    )(core, *arrays)


def chip_kernel(core_ref, keep_ref, recv_ref, pay_ref, base_ref):
    def write(early_ref, late_ref):
        base_ref[...] = early_ref[...]
        chip_logs = []
        for head in range(4):
            columns = head_columns(head)
            late_log = late_ref[STATE : STATE + 1, columns]
            chip_logs.append(early_ref[STATE : STATE + 1, columns] + late_log)
            state = jnp.exp2(late_log) * early_ref[:STATE, columns] + late_ref[:STATE, columns]
            for chip in range(CHIPS):
                row = chip * PIECE + head * ROWS
                pay_ref[row : row + ROWS, :] = state[chip * ROWS : (chip + 1) * ROWS, :]
        lane = lax.broadcasted_iota(jnp.int32, (1, HEAD_DIM), 1)
        logs = chip_logs[3]
        for head in range(3):
            quarter = (head + 1) * (HEAD_DIM // 4)
            inside = (lane >= quarter - HEAD_DIM // 4) & (lane < quarter)
            logs = jnp.where(inside, chip_logs[head], logs)
        for chip in range(CHIPS):
            row = (chip + 1) * PIECE - 1
            pay_ref[row : row + 1, :] = logs

    @pl.when(core_ref[0] == 0)
    def _():
        write(keep_ref, recv_ref)

    @pl.when(core_ref[0] != 0)
    def _():
        write(recv_ref, keep_ref)


def chip_call(core, keep, recv):
    return pl.pallas_call(
        chip_kernel,
        in_specs=[smem_spec(), vmem_spec(), vmem_spec()],
        out_specs=[vmem_spec(), vmem_spec()],
        out_shape=[
            jax.ShapeDtypeStruct((CHIPS * PIECE, HEAD_DIM), f32),
            jax.ShapeDtypeStruct((STATE + 8, HALF), f32),
        ],
        compiler_params=params(),
        name="chip_state",
    )(core, keep, recv)


def scan_kernel(pay_ref, out_ref):
    carries = [jnp.zeros((ROWS, HEAD_DIM), f32) for _ in range(4)]
    for chip in range(CHIPS):
        first_row = chip * PIECE
        factors = jnp.exp2(pay_ref[first_row + PIECE - 1 : first_row + PIECE, :])
        for head in range(4):
            lane = head * (HEAD_DIM // 4)
            out_ref[chip, head * ROWS : (head + 1) * ROWS, :] = carries[head]
            row = first_row + head * ROWS
            carries[head] = factors[:, lane : lane + 1] * carries[head] + pay_ref[row : row + ROWS, :]


def scan_call(pay):
    return pl.pallas_call(
        scan_kernel,
        in_specs=[vmem_spec()],
        out_specs=vmem_spec(),
        out_shape=jax.ShapeDtypeStruct((CHIPS, 4 * ROWS, HEAD_DIM), f32),
        compiler_params=params(),
        name="chip_scan",
    )(pay)


def entry_kernel(core_ref, pre_ref, base_ref, send_ref, own_ref):
    def write(plain_ref, moved_ref):
        for head in range(4):
            columns = head_columns(head)
            factor = jnp.exp2(base_ref[STATE : STATE + 1, columns])
            rows = slice(head * ROWS, (head + 1) * ROWS)
            entry = jnp.concatenate([pre_ref[chip, rows, :] for chip in range(CHIPS)], axis=0)
            plain_ref[:, columns] = entry
            moved_ref[:, columns] = factor * entry + base_ref[:STATE, columns]

    @pl.when(core_ref[0] == 0)
    def _():
        write(own_ref, send_ref)

    @pl.when(core_ref[0] != 0)
    def _():
        write(send_ref, own_ref)


def entry_call(core, pre, base):
    half_shape = jax.ShapeDtypeStruct((STATE, HALF), f32)
    return pl.pallas_call(
        entry_kernel,
        in_specs=[smem_spec(), vmem_spec(), vmem_spec()],
        out_specs=[vmem_spec(), vmem_spec()],
        out_shape=[half_shape, half_shape],
        compiler_params=params(),
        name="slab_entry",
    )(core, pre, base)


def diagonal_kernel(block, skip_ref, x_ref, z_ref, b_ref, c_ref, cum_ref, plain_ref, gain_ref):
    tokens = slice(block * BLOCK, (block + 1) * BLOCK)
    start = block * BLOCK
    cum = cum_ref[:, tokens]
    cum_t = cum.T
    row = lax.broadcasted_iota(jnp.int32, (128, 128), 0)
    col = lax.broadcasted_iota(jnp.int32, (128, 128), 1)
    causal = row >= col
    c_block = c_ref[tokens, :]
    b_block = b_ref[tokens, :]
    scores = []
    for tile in range(2):
        rows = slice(tile * 128, (tile + 1) * 128)
        for other in range(tile + 1):
            across = slice(other * 128, (other + 1) * 128)
            scores.append(
                lax.dot_general(
                    c_block[rows], b_block[across], (((1,), (1,)), ((), ())), preferred_element_type=f32
                )
            )
    for head in range(HEADS):
        columns = head_columns(head)
        cum_row = cum[head : head + 1, :]
        for tile in range(2):
            rows = slice(tile * 128, (tile + 1) * 128)
            here = slice(start + tile * 128, start + (tile + 1) * 128)
            cum_col = jnp.broadcast_to(cum_t[rows, head : head + 1], (128, HEAD_DIM))
            exponent = jnp.where(causal, cum_col - cum_row[:, rows], -jnp.inf)
            weights = (scores[0 if tile == 0 else 2] * jnp.exp2(exponent)).astype(bf16)
            if tile == 1:
                before = (scores[1] * jnp.exp2(cum_col - cum_row[:, :128])).astype(bf16)
                weights = jnp.concatenate([before, weights], axis=1)
            x_head = x_ref[slice(start, start + (tile + 1) * 128), columns]
            y = jnp.dot(weights, x_head, preferred_element_type=f32)
            y = y + skip_ref[head : head + 1, :] * x_ref[here, columns].astype(f32)
            half_z = 0.5 * z_ref[here, columns].astype(f32)
            gate = half_z + half_z * jnp.tanh(half_z)
            plain_ref[rows, columns] = y * gate
            gain_ref[rows, columns] = jnp.exp2(cum_col) * gate


def diagonal_call(block, skip, x_in, z_in, b_in, c_in, cum):
    shape = jax.ShapeDtypeStruct((BLOCK, WIDTH), f32)
    return pl.pallas_call(
        functools.partial(diagonal_kernel, block),
        in_specs=[vmem_spec()] * 6,
        out_specs=[vmem_spec(), vmem_spec()],
        out_shape=[shape, shape],
        compiler_params=params(),
        cost_estimate=pl.CostEstimate(
            flops=300_000_000, bytes_accessed=3_500_000, transcendentals=1_000_000
        ),
        name="diagonal",
    )(skip, x_in, z_in, b_in, c_in, cum)


def column_to_row(column):
    row = lax.broadcasted_iota(jnp.int32, (128, 128), 0)
    col = lax.broadcasted_iota(jnp.int32, (128, 128), 1)
    spread = jnp.where(row == col, jnp.broadcast_to(column, (128, 128)), 0.0)
    return jnp.sum(spread, axis=0, keepdims=True)


def gated_kernel(
    core_ref, own_ref, recv_ref, first_ref, cum_ref, c_ref, weight_ref,
    plain0_ref, gain0_ref, plain1_ref, gain1_ref, gated_ref, sum_ref, entry,
):
    core = core_ref[0]
    entry[:, pl.ds(pl.multiple_of(core * HALF, HALF), HALF)] = own_ref[...]
    entry[:, pl.ds(pl.multiple_of((1 - core) * HALF, HALF), HALF)] = recv_ref[...]
    weight = weight_ref[...].astype(f32)
    factors = jnp.exp2(cum_ref[:, BLOCK - 1 : BLOCK])
    for block in range(2):
        plain_ref, gain_ref = ((plain0_ref, gain0_ref), (plain1_ref, gain1_ref))[block]
        tokens = slice(block * BLOCK, (block + 1) * BLOCK)
        squares = jnp.zeros((BLOCK, HEAD_DIM), f32)
        for pair in range(4):
            states = []
            for head in (2 * pair, 2 * pair + 1):
                columns = head_columns(head)
                state = entry[:, columns]
                if block == 1:
                    state = factors[head : head + 1, :] * state + first_ref[:, columns]
                states.append(state.astype(bf16))
            columns = slice(pair * 256, (pair + 1) * 256)
            off = jnp.dot(
                c_ref[tokens, :], jnp.concatenate(states, axis=1), preferred_element_type=f32
            )
            gated = plain_ref[:, columns] + gain_ref[:, columns] * off
            gated_ref[tokens, columns] = gated * weight[:, columns]
            square = gated * gated
            squares = squares + square[:, :128] + square[:, 128:]
        column = jnp.sum(squares, axis=1, keepdims=True)
        rows = jnp.concatenate([column_to_row(column[:128]), column_to_row(column[128:])], axis=0)
        for peer in range(8):
            sum_ref[peer, 2 * block : 2 * block + 2, :] = rows


def gated_call(core, own, recv, first, cum, c_in, norm_weight, parts):
    return pl.pallas_call(
        gated_kernel,
        in_specs=[smem_spec()] + [vmem_spec()] * 10,
        out_specs=[vmem_spec(), vmem_spec()],
        out_shape=[
            jax.ShapeDtypeStruct((TOK, WIDTH), f32),
            jax.ShapeDtypeStruct((8, 4, 128), f32),
        ],
        scratch_shapes=[pltpu.VMEM((STATE, WIDTH), f32)],
        compiler_params=params(),
        name="gated",
    )(core, own, recv, first, cum, c_in, norm_weight.reshape(1, WIDTH), *parts)


def scale_kernel(sums_ref, gated_ref, out_hbm, buffer, sems):
    total = jnp.sum(sums_ref[...], axis=0)
    inverse = lax.rsqrt(total / (HEAD_TOTAL * HEAD_DIM) + epsilon)
    copies = []
    for part in range(4):
        tokens = slice(part * 128, (part + 1) * 128)
        column = jnp.broadcast_to(inverse[part : part + 1, :], (128, 128)).T
        for head in range(HEADS):
            columns = head_columns(head)
            buffer[tokens, columns] = (gated_ref[tokens, columns] * column).astype(bf16)
        copy = pltpu.make_async_copy(buffer.at[tokens, :], out_hbm.at[tokens, :], sems.at[part])
        copy.start()
        copies.append(copy)
    for copy in copies:
        copy.wait()


def scale_call(sums, gated):
    return pl.pallas_call(
        scale_kernel,
        in_specs=[vmem_spec(), vmem_spec()],
        out_specs=hbm_spec(),
        out_shape=jax.ShapeDtypeStruct((TOK, WIDTH), bf16),
        scratch_shapes=[pltpu.VMEM((TOK, WIDTH), bf16), pltpu.SemaphoreType.DMA((4,))],
        compiler_params=params(),
        name="scale",
    )(sums, gated)


def shards(x_in, z_in, b_in, c_in, decays, d_skip, norm_weight):
    core = (lax.axis_index("seq") % 2).astype(jnp.int32).reshape(1)
    swap = [(i, i ^ 1) for i in range(2 * CHIPS)]
    groups = [[2 * chip + c for chip in range(CHIPS)] for c in range(2)]
    first, send, keep, cum, *inputs = state_call(core, x_in, z_in, b_in, c_in, decays, d_skip)
    c_in = inputs[-1]
    recv = lax.ppermute(send, "seq", swap)
    part0 = diagonal_call(0, *inputs, cum)
    recv, *part0 = lax.optimization_barrier((recv, *part0))
    pay, base = chip_call(core, keep, recv)
    pay = pay.reshape(CHIPS, 1, PIECE * HEAD_DIM)
    pay = lax.all_to_all(pay, "seq", 0, 0, axis_index_groups=groups, tiled=True)
    pay = pay.reshape(CHIPS * PIECE, HEAD_DIM)
    pre = scan_call(pay)
    pre = lax.all_to_all(pre, "seq", 0, 0, axis_index_groups=groups, tiled=True)
    send, own = entry_call(core, pre, base)
    recv = lax.ppermute(send, "seq", swap)
    part1 = diagonal_call(1, *inputs, cum)
    gated, sums = gated_call(core, own, recv, first, cum, c_in, norm_weight, (*part0, *part1))
    sums = lax.all_to_all(sums, "tp", 0, 0, tiled=True)
    return scale_call(sums, gated)


def solution(mesh):
    return jax.shard_map(
        shards,
        mesh=mesh,
        in_specs=(
            P("seq", "tp"),
            P("seq", "tp"),
            P("seq", "tp"),
            P("seq", "tp"),
            P("tp", "seq"),
            P("tp"),
            P("tp"),
        ),
        out_specs=P("seq", "tp"),
        check_vma=False,
    )
```

```python
import functools

import jax
import jax.numpy as jnp
from jax import lax
from jax.experimental import pallas as pl
from jax.experimental.pallas import tpu as pltpu
from jax.sharding import PartitionSpec as P

HEAD_TOTAL = 64
HEAD_DIM = 128
STATE = 128
BLOCK = 256
CHIPS = 32

epsilon = 1e-05

HEADS = 8
TOK = 512
WIDTH = HEADS * HEAD_DIM
HALF = WIDTH // 2
ROWS = STATE // CHIPS
PIECE = 4 * ROWS + 1

VMEM_BYTES = 16 << 20
f32 = jnp.float32
bf16 = jnp.bfloat16


def params():
    return pltpu.CompilerParams(vmem_limit_bytes=VMEM_BYTES)


def smem_spec():
    return pl.BlockSpec(memory_space=pltpu.SMEM)


def vmem_spec():
    return pl.BlockSpec(memory_space=pltpu.VMEM)


def hbm_spec():
    return pl.BlockSpec(memory_space=pltpu.HBM)


def head_columns(head):
    return slice(head * HEAD_DIM, (head + 1) * HEAD_DIM)


def split3(value):
    high = value.astype(bf16)
    rest = value - high.astype(f32)
    middle = rest.astype(bf16)
    low = (rest - middle.astype(f32)).astype(bf16)
    return high, middle, low


def state_kernel(
    core_ref, x_hbm, z_hbm, b_hbm, c_hbm, decay_hbm, skip_hbm,
    first_ref, send_ref, keep_ref, cum_ref, skip_ref, x_ref, z_ref, b_ref, c_ref,
    decay_ref, skip_smem, sems,
):
    copies = [
        pltpu.make_async_copy(source, target, sems.at[index])
        for index, (source, target) in enumerate(
            (
                (decay_hbm, decay_ref),
                (b_hbm, b_ref),
                (x_hbm, x_ref),
                (skip_hbm, skip_smem),
                (c_hbm, c_ref),
                (z_hbm, z_ref),
            )
        )
    ]
    for copy in copies:
        copy.start()
    row = lax.broadcasted_iota(jnp.int32, (BLOCK, BLOCK), 0)
    col = lax.broadcasted_iota(jnp.int32, (BLOCK, BLOCK), 1)
    upper = jnp.where(row <= col, 1.0, 0.0).astype(bf16)
    copies[0].wait()
    copies[1].wait()
    b_t = b_ref[...].astype(f32).T
    logs = jnp.log2(decay_ref[...])
    totals = []
    weights = []
    for block in range(2):
        span = slice(block * BLOCK, (block + 1) * BLOCK)
        total = jnp.zeros((HEADS, BLOCK), f32)
        for part in reversed(split3(logs[:, span])):
            total = total + jnp.dot(part, upper, preferred_element_type=f32)
        cum_ref[:, span] = total
        last = total[:, BLOCK - 1 :]
        totals.append(last)
        weights.append(jnp.exp2(last - total))
    second = jnp.exp2(totals[1])
    slab_logs = jnp.broadcast_to(totals[0] + totals[1], (HEADS, HEAD_DIM))
    copies[2].wait()
    low_core = core_ref[0] == 0
    for pair in range(4):
        slabs = []
        slab_rows = []
        for head in (pair, pair + 4):
            columns = head_columns(head)
            states = []
            for block in range(2):
                span = slice(block * BLOCK, (block + 1) * BLOCK)
                b_weighted = (b_t[:, span] * weights[block][head : head + 1, :]).astype(bf16)
                states.append(jnp.dot(b_weighted, x_ref[span, columns], preferred_element_type=f32))
            first_ref[:, columns] = states[0]
            slabs.append(second[head : head + 1, :] * states[0] + states[1])
            slab_rows.append(jnp.broadcast_to(slab_logs[head : head + 1, :], (8, HEAD_DIM)))
        target = head_columns(pair)
        keep_ref[:STATE, target] = jnp.where(low_core, slabs[0], slabs[1])
        send_ref[:STATE, target] = jnp.where(low_core, slabs[1], slabs[0])
        keep_ref[STATE:, target] = jnp.where(low_core, slab_rows[0], slab_rows[1])
        send_ref[STATE:, target] = jnp.where(low_core, slab_rows[1], slab_rows[0])

    for copy in copies[3:]:
        copy.wait()
    for head in range(HEADS):
        skip_ref[head : head + 1, :] = jnp.full((1, HEAD_DIM), skip_smem[head], f32)


def state_call(core, x_in, z_in, b_in, c_in, decays, d_skip):
    half_shape = jax.ShapeDtypeStruct((STATE + 8, HALF), f32)
    arrays = [
        pltpu.with_memory_space_constraint(array, pltpu.HBM)
        for array in (x_in, z_in, b_in, c_in, decays, d_skip)
    ]
    return pl.pallas_call(
        state_kernel,
        in_specs=[smem_spec()] + [hbm_spec()] * 6,
        out_specs=[vmem_spec()] * 9,
        out_shape=[
            jax.ShapeDtypeStruct((STATE, WIDTH), f32),
            half_shape,
            half_shape,
            jax.ShapeDtypeStruct((HEADS, TOK), f32),
            jax.ShapeDtypeStruct((HEADS, HEAD_DIM), f32),
            jax.ShapeDtypeStruct((TOK, WIDTH), bf16),
            jax.ShapeDtypeStruct((TOK, WIDTH), bf16),
            jax.ShapeDtypeStruct((TOK, STATE), bf16),
            jax.ShapeDtypeStruct((TOK, STATE), bf16),
        ],
        scratch_shapes=[
            pltpu.VMEM((HEADS, TOK), f32),
            pltpu.SMEM((HEADS,), f32),
            pltpu.SemaphoreType.DMA((6,)),
        ],
        compiler_params=params(),
        name="slab_state",
    )(core, *arrays)


def chip_kernel(core_ref, keep_ref, recv_ref, pay_ref, base_ref):
    def write(early_ref, late_ref):
        base_ref[...] = early_ref[...]
        chip_logs = []
        for head in range(4):
            columns = head_columns(head)
            late_log = late_ref[STATE : STATE + 1, columns]
            chip_logs.append(early_ref[STATE : STATE + 1, columns] + late_log)
            state = jnp.exp2(late_log) * early_ref[:STATE, columns] + late_ref[:STATE, columns]
            for chip in range(CHIPS):
                row = chip * PIECE + head * ROWS
                pay_ref[row : row + ROWS, :] = state[chip * ROWS : (chip + 1) * ROWS, :]
        lane = lax.broadcasted_iota(jnp.int32, (1, HEAD_DIM), 1)
        logs = chip_logs[3]
        for head in range(3):
            quarter = (head + 1) * (HEAD_DIM // 4)
            inside = (lane >= quarter - HEAD_DIM // 4) & (lane < quarter)
            logs = jnp.where(inside, chip_logs[head], logs)
        for chip in range(CHIPS):
            row = (chip + 1) * PIECE - 1
            pay_ref[row : row + 1, :] = logs

    @pl.when(core_ref[0] == 0)
    def _():
        write(keep_ref, recv_ref)

    @pl.when(core_ref[0] != 0)
    def _():
        write(recv_ref, keep_ref)


def chip_call(core, keep, recv):
    return pl.pallas_call(
        chip_kernel,
        in_specs=[smem_spec(), vmem_spec(), vmem_spec()],
        out_specs=[vmem_spec(), vmem_spec()],
        out_shape=[
            jax.ShapeDtypeStruct((CHIPS * PIECE, HEAD_DIM), f32),
            jax.ShapeDtypeStruct((STATE + 8, HALF), f32),
        ],
        compiler_params=params(),
        name="chip_state",
    )(core, keep, recv)


def scan_kernel(pay_ref, out_ref):
    carries = [jnp.zeros((ROWS, HEAD_DIM), f32) for _ in range(4)]
    for chip in range(CHIPS):
        first_row = chip * PIECE
        factors = jnp.exp2(pay_ref[first_row + PIECE - 1 : first_row + PIECE, :])
        for head in range(4):
            lane = head * (HEAD_DIM // 4)
            out_ref[chip, head * ROWS : (head + 1) * ROWS, :] = carries[head]
            row = first_row + head * ROWS
            carries[head] = factors[:, lane : lane + 1] * carries[head] + pay_ref[row : row + ROWS, :]


def scan_call(pay):
    return pl.pallas_call(
        scan_kernel,
        in_specs=[vmem_spec()],
        out_specs=vmem_spec(),
        out_shape=jax.ShapeDtypeStruct((CHIPS, 4 * ROWS, HEAD_DIM), f32),
        compiler_params=params(),
        name="chip_scan",
    )(pay)


def entry_kernel(core_ref, pre_ref, base_ref, send_ref, own_ref):
    def write(plain_ref, moved_ref):
        for head in range(4):
            columns = head_columns(head)
            factor = jnp.exp2(base_ref[STATE : STATE + 1, columns])
            rows = slice(head * ROWS, (head + 1) * ROWS)
            entry = jnp.concatenate([pre_ref[chip, rows, :] for chip in range(CHIPS)], axis=0)
            plain_ref[:, columns] = entry
            moved_ref[:, columns] = factor * entry + base_ref[:STATE, columns]

    @pl.when(core_ref[0] == 0)
    def _():
        write(own_ref, send_ref)

    @pl.when(core_ref[0] != 0)
    def _():
        write(send_ref, own_ref)


def entry_call(core, pre, base):
    half_shape = jax.ShapeDtypeStruct((STATE, HALF), f32)
    return pl.pallas_call(
        entry_kernel,
        in_specs=[smem_spec(), vmem_spec(), vmem_spec()],
        out_specs=[vmem_spec(), vmem_spec()],
        out_shape=[half_shape, half_shape],
        compiler_params=params(),
        name="slab_entry",
    )(core, pre, base)


def diagonal_kernel(block, only, core_ref, skip_ref, x_ref, z_ref, b_ref, c_ref, cum_ref, *refs):
    if only is None:
        diagonal_body(block, skip_ref, x_ref, z_ref, b_ref, c_ref, cum_ref, *refs[-2:])
    else:

        @pl.when(core_ref[0] == only)
        def _():
            diagonal_body(block, skip_ref, x_ref, z_ref, b_ref, c_ref, cum_ref, *refs[-2:])


def diagonal_body(block, skip_ref, x_ref, z_ref, b_ref, c_ref, cum_ref, plain_ref, gain_ref):
    tokens = slice(block * BLOCK, (block + 1) * BLOCK)
    start = block * BLOCK
    cum = cum_ref[:, tokens]
    cum_t = cum.T
    row = lax.broadcasted_iota(jnp.int32, (128, 128), 0)
    col = lax.broadcasted_iota(jnp.int32, (128, 128), 1)
    causal = row >= col
    c_block = c_ref[tokens, :]
    b_block = b_ref[tokens, :]
    scores = []
    for tile in range(2):
        rows = slice(tile * 128, (tile + 1) * 128)
        for other in range(tile + 1):
            across = slice(other * 128, (other + 1) * 128)
            scores.append(
                lax.dot_general(
                    c_block[rows], b_block[across], (((1,), (1,)), ((), ())), preferred_element_type=f32
                )
            )
    for head in range(HEADS):
        columns = head_columns(head)
        cum_row = cum[head : head + 1, :]
        for tile in range(2):
            rows = slice(tile * 128, (tile + 1) * 128)
            here = slice(start + tile * 128, start + (tile + 1) * 128)
            cum_col = jnp.broadcast_to(cum_t[rows, head : head + 1], (128, HEAD_DIM))
            exponent = jnp.where(causal, cum_col - cum_row[:, rows], -jnp.inf)
            weights = (scores[0 if tile == 0 else 2] * jnp.exp2(exponent)).astype(bf16)
            if tile == 1:
                before = (scores[1] * jnp.exp2(cum_col - cum_row[:, :128])).astype(bf16)
                weights = jnp.concatenate([before, weights], axis=1)
            x_head = x_ref[slice(start, start + (tile + 1) * 128), columns]
            y = jnp.dot(weights, x_head, preferred_element_type=f32)
            y = y + skip_ref[head : head + 1, :] * x_ref[here, columns].astype(f32)
            half_z = 0.5 * z_ref[here, columns].astype(f32)
            gate = half_z + half_z * jnp.tanh(half_z)
            plain_ref[rows, columns] = y * gate
            gain_ref[rows, columns] = jnp.exp2(cum_col) * gate


def diagonal_call(block, core, inputs, cum, only=None, previous=()):
    shape = jax.ShapeDtypeStruct((BLOCK, WIDTH), f32)
    return pl.pallas_call(
        functools.partial(diagonal_kernel, block, only),
        in_specs=[smem_spec()] + [vmem_spec()] * (6 + len(previous)),
        out_specs=[vmem_spec(), vmem_spec()],
        out_shape=[shape, shape],
        input_output_aliases={7 + index: index for index in range(len(previous))},
        compiler_params=params(),
        cost_estimate=pl.CostEstimate(
            flops=300_000_000, bytes_accessed=3_500_000, transcendentals=1_000_000
        ),
        name="diagonal",
    )(core, *inputs, cum, *previous)


def column_to_row(column):
    row = lax.broadcasted_iota(jnp.int32, (128, 128), 0)
    col = lax.broadcasted_iota(jnp.int32, (128, 128), 1)
    spread = jnp.where(row == col, jnp.broadcast_to(column, (128, 128)), 0.0)
    return jnp.sum(spread, axis=0, keepdims=True)


def head_span(head):
    return pl.ds(pl.multiple_of(head * HEAD_DIM, HEAD_DIM), HEAD_DIM)


def gated_half(
    base, entry_ref, first_ref, cum_ref, c_ref, weight_ref, parts, gated_ref, block
):
    plain_ref, gain_ref = parts[2 * block : 2 * block + 2]
    tokens = slice(block * BLOCK, (block + 1) * BLOCK)
    squares = None
    for pair in range(2):
        states = []
        for index in (2 * pair, 2 * pair + 1):
            columns = head_columns(index)
            state = entry_ref[:, columns]
            if block == 1:
                last = cum_ref[pl.ds(base + index, 1), :BLOCK][:, BLOCK - 1 :]
                state = jnp.exp2(last) * state + first_ref[:, head_span(base + index)]
            states.append(state.astype(bf16))
        off = jnp.dot(
            c_ref[tokens, :], jnp.concatenate(states, axis=1), preferred_element_type=f32
        )
        for index in (2 * pair, 2 * pair + 1):
            source = head_span(base + index)
            part = off[:, head_columns(index - 2 * pair)]
            gated = plain_ref[:, source] + gain_ref[:, source] * part
            gated_ref[tokens, head_columns(index)] = gated * weight_ref[:, source]
            square = gated * gated
            squares = square if squares is None else squares + square
    return squares


def own_gated_kernel(
    core_ref, entry_ref, first_ref, cum_ref, c_ref, weight_ref,
    plain0_ref, gain0_ref, plain1_ref, gain1_ref, gated_ref, squares_ref,
):
    parts = (plain0_ref, gain0_ref, plain1_ref, gain1_ref)
    for block in range(2):
        tokens = slice(block * BLOCK, (block + 1) * BLOCK)
        squares_ref[tokens, :] = gated_half(
            4 * core_ref[0], entry_ref, first_ref, cum_ref, c_ref, weight_ref, parts, gated_ref, block
        )


def other_gated_kernel(
    core_ref, entry_ref, first_ref, cum_ref, c_ref, weight_ref,
    plain0_ref, gain0_ref, plain1_ref, gain1_ref, squares_ref, gated_ref, sum_ref,
):
    parts = (plain0_ref, gain0_ref, plain1_ref, gain1_ref)
    for block in range(2):
        tokens = slice(block * BLOCK, (block + 1) * BLOCK)
        squares = squares_ref[tokens, :] + gated_half(
            4 * (1 - core_ref[0]), entry_ref, first_ref, cum_ref, c_ref, weight_ref, parts, gated_ref, block
        )
        column = jnp.sum(squares, axis=1, keepdims=True)
        rows = jnp.concatenate([column_to_row(column[:128]), column_to_row(column[128:])], axis=0)
        for peer in range(8):
            sum_ref[peer, 2 * block : 2 * block + 2, :] = rows


def gated_call(core, entry, first, cum, c_in, weight, parts, squares=None):
    last = squares is not None
    extra = (squares,) if last else ()
    shape = jax.ShapeDtypeStruct((8, 4, 128) if last else (TOK, HEAD_DIM), f32)
    return pl.pallas_call(
        other_gated_kernel if last else own_gated_kernel,
        in_specs=[smem_spec()] + [vmem_spec()] * (9 + len(extra)),
        out_specs=[vmem_spec(), vmem_spec()],
        out_shape=[jax.ShapeDtypeStruct((TOK, HALF), f32), shape],
        compiler_params=params(),
        cost_estimate=pl.CostEstimate(
            flops=70_000_000, bytes_accessed=3_000_000, transcendentals=1_000
        ),
        name="other_gated" if last else "own_gated",
    )(core, entry, first, cum, c_in, weight, *parts, *extra)


def scale_kernel(core_ref, sums_ref, own_ref, other_ref, out_hbm, buffer, sems):
    total = jnp.sum(sums_ref[...], axis=0)
    inverse = lax.rsqrt(total / (HEAD_TOTAL * HEAD_DIM) + epsilon)
    core = core_ref[0]
    copies = []
    for part in range(4):
        tokens = slice(part * 128, (part + 1) * 128)
        column = jnp.broadcast_to(inverse[part : part + 1, :], (128, 128)).T
        for base, gated_ref in ((core * HALF, own_ref), ((1 - core) * HALF, other_ref)):
            for head in range(4):
                columns = pl.ds(pl.multiple_of(base + head * HEAD_DIM, HEAD_DIM), HEAD_DIM)
                scaled = gated_ref[tokens, head_columns(head)] * column
                buffer[tokens, columns] = scaled.astype(bf16)
        copy = pltpu.make_async_copy(buffer.at[tokens, :], out_hbm.at[tokens, :], sems.at[part])
        copy.start()
        copies.append(copy)
    for copy in copies:
        copy.wait()


def scale_call(core, sums, own, other):
    return pl.pallas_call(
        scale_kernel,
        in_specs=[smem_spec()] + [vmem_spec()] * 3,
        out_specs=hbm_spec(),
        out_shape=jax.ShapeDtypeStruct((TOK, WIDTH), bf16),
        scratch_shapes=[pltpu.VMEM((TOK, WIDTH), bf16), pltpu.SemaphoreType.DMA((4,))],
        compiler_params=params(),
        name="scale",
    )(core, sums, own, other)


def shards(x_in, z_in, b_in, c_in, decays, d_skip, norm_weight):
    core = (lax.axis_index("seq") % 2).astype(jnp.int32).reshape(1)
    swap = [(i, i ^ 1) for i in range(2 * CHIPS)]
    groups = [[2 * chip + c for chip in range(CHIPS)] for c in range(2)]
    first, send, keep, cum, *inputs = state_call(core, x_in, z_in, b_in, c_in, decays, d_skip)
    c_in = inputs[-1]
    recv = lax.ppermute(send, "seq", swap)
    part0 = diagonal_call(0, core, inputs, cum)
    recv, *part0 = lax.optimization_barrier((recv, *part0))
    pay, base = chip_call(core, keep, recv)
    pay = pay.reshape(CHIPS, 1, PIECE * HEAD_DIM)
    pay = lax.all_to_all(pay, "seq", 0, 0, axis_index_groups=groups, tiled=True)
    pre = scan_call(pay.reshape(CHIPS * PIECE, HEAD_DIM))
    pre = lax.all_to_all(pre, "seq", 0, 0, axis_index_groups=groups, tiled=True)
    pre, cum_late = lax.optimization_barrier((pre, cum))
    part1 = diagonal_call(1, core, inputs, cum_late, only=1)
    send, own = entry_call(core, pre, base)
    send, *part1 = lax.optimization_barrier((send, *part1))
    recv = lax.ppermute(send, "seq", swap)
    part1 = diagonal_call(1, core, inputs, cum, only=0, previous=part1)
    parts = (*part0, *part1)
    weight = norm_weight.astype(f32).reshape(1, WIDTH)
    own_gated, squares = gated_call(core, own, first, cum, c_in, weight, parts)
    other_gated, sums = gated_call(core, recv, first, cum, c_in, weight, parts, squares)
    sums = lax.all_to_all(sums, "tp", 0, 0, tiled=True)
    return scale_call(core, sums, own_gated, other_gated)


def solution(mesh):
    return jax.shard_map(
        shards,
        mesh=mesh,
        in_specs=(
            P("seq", "tp"),
            P("seq", "tp"),
            P("seq", "tp"),
            P("seq", "tp"),
            P("tp", "seq"),
            P("tp"),
            P("tp"),
        ),
        out_specs=P("seq", "tp"),
        check_vma=False,
    )
```

```python
import functools

import jax
import jax.numpy as jnp
from jax import lax
from jax.experimental import pallas as pl
from jax.experimental.pallas import tpu as pltpu
from jax.sharding import PartitionSpec as P

HEAD_TOTAL = 64
HEAD_DIM = 128
STATE = 128
BLOCK = 256
CHIPS = 32

epsilon = 1e-05

HEADS = 8
TOK = 512
WIDTH = HEADS * HEAD_DIM
HALF = WIDTH // 2
ROWS = STATE // CHIPS
PIECE = 4 * ROWS + 1

VMEM_BYTES = 16 << 20
f32 = jnp.float32
bf16 = jnp.bfloat16


def params():
    return pltpu.CompilerParams(vmem_limit_bytes=VMEM_BYTES)


def smem_spec():
    return pl.BlockSpec(memory_space=pltpu.SMEM)


def vmem_spec():
    return pl.BlockSpec(memory_space=pltpu.VMEM)


def hbm_spec():
    return pl.BlockSpec(memory_space=pltpu.HBM)


def head_columns(head):
    return slice(head * HEAD_DIM, (head + 1) * HEAD_DIM)


def split3(value):
    high = value.astype(bf16)
    rest = value - high.astype(f32)
    middle = rest.astype(bf16)
    low = (rest - middle.astype(f32)).astype(bf16)
    return high, middle, low


def half_states(base, b_t, to_end, cum_ref, x_ref, first_ref, slab_ref):
    for index in range(4):
        head = base + index
        source = pl.ds(pl.multiple_of(head * HEAD_DIM, HEAD_DIM), HEAD_DIM)
        target = head_columns(index)
        weight = to_end[pl.ds(head, 1), :]
        cum = cum_ref[pl.ds(head, 1), :]
        last0 = cum[:, BLOCK - 1 : BLOCK]
        last1 = cum[:, 2 * BLOCK - 1 :]
        states = []
        for block in range(2):
            span = slice(block * BLOCK, (block + 1) * BLOCK)
            b_weighted = (b_t[:, span] * weight[:, span]).astype(bf16)
            states.append(jnp.dot(b_weighted, x_ref[span, source], preferred_element_type=f32))
        first_ref[:, target] = states[0]
        slab_ref[:STATE, target] = jnp.exp2(last1) * states[0] + states[1]
        slab_ref[STATE:, target] = jnp.broadcast_to(last0 + last1, (8, HEAD_DIM))


def send_state_kernel(
    core_ref, x_hbm, z_hbm, b_hbm, c_hbm, decay_hbm, skip_hbm,
    send_ref, first_ref, cum_ref, to_end_ref, b_t_ref, skip_ref, x_ref, z_ref, b_ref, c_ref,
    decay_ref, skip_smem, sems,
):
    copies = [
        pltpu.make_async_copy(source, target, sems.at[index])
        for index, (source, target) in enumerate(
            (
                (decay_hbm, decay_ref),
                (b_hbm, b_ref),
                (x_hbm, x_ref),
                (skip_hbm, skip_smem),
                (c_hbm, c_ref),
                (z_hbm, z_ref),
            )
        )
    ]
    for copy in copies:
        copy.start()
    row = lax.broadcasted_iota(jnp.int32, (BLOCK, BLOCK), 0)
    col = lax.broadcasted_iota(jnp.int32, (BLOCK, BLOCK), 1)
    upper = jnp.where(row <= col, 1.0, 0.0).astype(bf16)
    copies[0].wait()
    copies[1].wait()
    b_t = b_ref[...].astype(f32).T
    b_t_ref[...] = b_t
    logs = jnp.log2(decay_ref[...])
    for block in range(2):
        span = slice(block * BLOCK, (block + 1) * BLOCK)
        total = jnp.zeros((HEADS, BLOCK), f32)
        for part in reversed(split3(logs[:, span])):
            total = total + jnp.dot(part, upper, preferred_element_type=f32)
        cum_ref[:, span] = total
        to_end_ref[:, span] = jnp.exp2(total[:, BLOCK - 1 :] - total)
    copies[2].wait()
    half_states(4 * (1 - core_ref[0]), b_t, to_end_ref, cum_ref, x_ref, first_ref, send_ref)
    for copy in copies[3:]:
        copy.wait()
    for head in range(HEADS):
        skip_ref[head : head + 1, :] = jnp.full((1, HEAD_DIM), skip_smem[head], f32)


def send_state_call(core, x_in, z_in, b_in, c_in, decays, d_skip):
    arrays = [
        pltpu.with_memory_space_constraint(array, pltpu.HBM)
        for array in (x_in, z_in, b_in, c_in, decays, d_skip)
    ]
    return pl.pallas_call(
        send_state_kernel,
        in_specs=[smem_spec()] + [hbm_spec()] * 6,
        out_specs=[vmem_spec()] * 10,
        out_shape=[
            jax.ShapeDtypeStruct((STATE + 8, HALF), f32),
            jax.ShapeDtypeStruct((STATE, HALF), f32),
            jax.ShapeDtypeStruct((HEADS, TOK), f32),
            jax.ShapeDtypeStruct((HEADS, TOK), f32),
            jax.ShapeDtypeStruct((STATE, TOK), f32),
            jax.ShapeDtypeStruct((HEADS, HEAD_DIM), f32),
            jax.ShapeDtypeStruct((TOK, WIDTH), bf16),
            jax.ShapeDtypeStruct((TOK, WIDTH), bf16),
            jax.ShapeDtypeStruct((TOK, STATE), bf16),
            jax.ShapeDtypeStruct((TOK, STATE), bf16),
        ],
        scratch_shapes=[
            pltpu.VMEM((HEADS, TOK), f32),
            pltpu.SMEM((HEADS,), f32),
            pltpu.SemaphoreType.DMA((6,)),
        ],
        compiler_params=params(),
        name="send_state",
    )(core, *arrays)


def keep_state_kernel(core_ref, b_t_ref, to_end_ref, cum_ref, x_ref, keep_ref, first_ref):
    half_states(4 * core_ref[0], b_t_ref[...], to_end_ref, cum_ref, x_ref, first_ref, keep_ref)


def keep_state_call(core, b_t, to_end, cum, x_in):
    return pl.pallas_call(
        keep_state_kernel,
        in_specs=[smem_spec()] + [vmem_spec()] * 4,
        out_specs=[vmem_spec()] * 2,
        out_shape=[
            jax.ShapeDtypeStruct((STATE + 8, HALF), f32),
            jax.ShapeDtypeStruct((STATE, HALF), f32),
        ],
        compiler_params=params(),
        cost_estimate=pl.CostEstimate(
            flops=70_000_000, bytes_accessed=1_500_000, transcendentals=1_000
        ),
        name="keep_state",
    )(core, b_t, to_end, cum, x_in)


def chip_kernel(core_ref, keep_ref, recv_ref, pay_ref, base_ref):
    def write(early_ref, late_ref):
        base_ref[...] = early_ref[...]
        chip_logs = []
        for head in range(4):
            columns = head_columns(head)
            late_log = late_ref[STATE : STATE + 1, columns]
            chip_logs.append(early_ref[STATE : STATE + 1, columns] + late_log)
            state = jnp.exp2(late_log) * early_ref[:STATE, columns] + late_ref[:STATE, columns]
            for chip in range(CHIPS):
                row = chip * PIECE + head * ROWS
                pay_ref[row : row + ROWS, :] = state[chip * ROWS : (chip + 1) * ROWS, :]
        lane = lax.broadcasted_iota(jnp.int32, (1, HEAD_DIM), 1)
        logs = chip_logs[3]
        for head in range(3):
            quarter = (head + 1) * (HEAD_DIM // 4)
            inside = (lane >= quarter - HEAD_DIM // 4) & (lane < quarter)
            logs = jnp.where(inside, chip_logs[head], logs)
        for chip in range(CHIPS):
            row = (chip + 1) * PIECE - 1
            pay_ref[row : row + 1, :] = logs

    @pl.when(core_ref[0] == 0)
    def _():
        write(keep_ref, recv_ref)

    @pl.when(core_ref[0] != 0)
    def _():
        write(recv_ref, keep_ref)


def chip_call(core, keep, recv):
    return pl.pallas_call(
        chip_kernel,
        in_specs=[smem_spec(), vmem_spec(), vmem_spec()],
        out_specs=[vmem_spec(), vmem_spec()],
        out_shape=[
            jax.ShapeDtypeStruct((CHIPS * PIECE, HEAD_DIM), f32),
            jax.ShapeDtypeStruct((STATE + 8, HALF), f32),
        ],
        compiler_params=params(),
        name="chip_state",
    )(core, keep, recv)


def scan_kernel(pay_ref, out_ref):
    carries = [jnp.zeros((ROWS, HEAD_DIM), f32) for _ in range(4)]
    for chip in range(CHIPS):
        first_row = chip * PIECE
        factors = jnp.exp2(pay_ref[first_row + PIECE - 1 : first_row + PIECE, :])
        for head in range(4):
            lane = head * (HEAD_DIM // 4)
            out_ref[chip, head * ROWS : (head + 1) * ROWS, :] = carries[head]
            row = first_row + head * ROWS
            carries[head] = factors[:, lane : lane + 1] * carries[head] + pay_ref[row : row + ROWS, :]


def scan_call(pay):
    return pl.pallas_call(
        scan_kernel,
        in_specs=[vmem_spec()],
        out_specs=vmem_spec(),
        out_shape=jax.ShapeDtypeStruct((CHIPS, 4 * ROWS, HEAD_DIM), f32),
        compiler_params=params(),
        name="chip_scan",
    )(pay)


def entry_kernel(core_ref, pre_ref, base_ref, send_ref, own_ref):
    def write(plain_ref, moved_ref):
        for head in range(4):
            columns = head_columns(head)
            factor = jnp.exp2(base_ref[STATE : STATE + 1, columns])
            rows = slice(head * ROWS, (head + 1) * ROWS)
            entry = jnp.concatenate([pre_ref[chip, rows, :] for chip in range(CHIPS)], axis=0)
            plain_ref[:, columns] = entry
            moved_ref[:, columns] = factor * entry + base_ref[:STATE, columns]

    @pl.when(core_ref[0] == 0)
    def _():
        write(own_ref, send_ref)

    @pl.when(core_ref[0] != 0)
    def _():
        write(send_ref, own_ref)


def entry_call(core, pre, base):
    half_shape = jax.ShapeDtypeStruct((STATE, HALF), f32)
    return pl.pallas_call(
        entry_kernel,
        in_specs=[smem_spec(), vmem_spec(), vmem_spec()],
        out_specs=[vmem_spec(), vmem_spec()],
        out_shape=[half_shape, half_shape],
        compiler_params=params(),
        name="slab_entry",
    )(core, pre, base)


def diagonal_kernel(block, only, core_ref, skip_ref, x_ref, z_ref, b_ref, c_ref, cum_ref, *refs):
    if only is None:
        diagonal_body(block, skip_ref, x_ref, z_ref, b_ref, c_ref, cum_ref, *refs[-2:])
    else:

        @pl.when(core_ref[0] == only)
        def _():
            diagonal_body(block, skip_ref, x_ref, z_ref, b_ref, c_ref, cum_ref, *refs[-2:])


def diagonal_body(block, skip_ref, x_ref, z_ref, b_ref, c_ref, cum_ref, plain_ref, gain_ref):
    tokens = slice(block * BLOCK, (block + 1) * BLOCK)
    start = block * BLOCK
    cum = cum_ref[:, tokens]
    cum_t = cum.T
    row = lax.broadcasted_iota(jnp.int32, (128, 128), 0)
    col = lax.broadcasted_iota(jnp.int32, (128, 128), 1)
    causal = row >= col
    c_block = c_ref[tokens, :]
    b_block = b_ref[tokens, :]
    scores = []
    for tile in range(2):
        rows = slice(tile * 128, (tile + 1) * 128)
        for other in range(tile + 1):
            across = slice(other * 128, (other + 1) * 128)
            scores.append(
                lax.dot_general(
                    c_block[rows], b_block[across], (((1,), (1,)), ((), ())), preferred_element_type=f32
                )
            )
    for head in range(HEADS):
        columns = head_columns(head)
        cum_row = cum[head : head + 1, :]
        for tile in range(2):
            rows = slice(tile * 128, (tile + 1) * 128)
            here = slice(start + tile * 128, start + (tile + 1) * 128)
            cum_col = jnp.broadcast_to(cum_t[rows, head : head + 1], (128, HEAD_DIM))
            exponent = jnp.where(causal, cum_col - cum_row[:, rows], -jnp.inf)
            weights = (scores[0 if tile == 0 else 2] * jnp.exp2(exponent)).astype(bf16)
            if tile == 1:
                before = (scores[1] * jnp.exp2(cum_col - cum_row[:, :128])).astype(bf16)
                weights = jnp.concatenate([before, weights], axis=1)
            x_head = x_ref[slice(start, start + (tile + 1) * 128), columns]
            y = jnp.dot(weights, x_head, preferred_element_type=f32)
            y = y + skip_ref[head : head + 1, :] * x_ref[here, columns].astype(f32)
            half_z = 0.5 * z_ref[here, columns].astype(f32)
            gate = half_z + half_z * jnp.tanh(half_z)
            plain_ref[rows, columns] = y * gate
            gain_ref[rows, columns] = jnp.exp2(cum_col) * gate


def diagonal_call(block, core, inputs, cum, only=None, previous=()):
    shape = jax.ShapeDtypeStruct((BLOCK, WIDTH), f32)
    return pl.pallas_call(
        functools.partial(diagonal_kernel, block, only),
        in_specs=[smem_spec()] + [vmem_spec()] * (6 + len(previous)),
        out_specs=[vmem_spec(), vmem_spec()],
        out_shape=[shape, shape],
        input_output_aliases={7 + index: index for index in range(len(previous))},
        compiler_params=params(),
        cost_estimate=pl.CostEstimate(
            flops=300_000_000, bytes_accessed=3_500_000, transcendentals=1_000_000
        ),
        name="diagonal",
    )(core, *inputs, cum, *previous)


def column_to_row(column):
    row = lax.broadcasted_iota(jnp.int32, (128, 128), 0)
    col = lax.broadcasted_iota(jnp.int32, (128, 128), 1)
    spread = jnp.where(row == col, jnp.broadcast_to(column, (128, 128)), 0.0)
    return jnp.sum(spread, axis=0, keepdims=True)


def head_span(head):
    return pl.ds(pl.multiple_of(head * HEAD_DIM, HEAD_DIM), HEAD_DIM)


def gated_half(
    base, entry_ref, first_ref, cum_ref, c_ref, weight_ref, parts, gated_ref, block
):
    plain_ref, gain_ref = parts[2 * block : 2 * block + 2]
    tokens = slice(block * BLOCK, (block + 1) * BLOCK)
    squares = None
    for pair in range(2):
        states = []
        for index in (2 * pair, 2 * pair + 1):
            columns = head_columns(index)
            state = entry_ref[:, columns]
            if block == 1:
                last = cum_ref[pl.ds(base + index, 1), :BLOCK][:, BLOCK - 1 :]
                state = jnp.exp2(last) * state + first_ref[:, columns]
            states.append(state.astype(bf16))
        off = jnp.dot(
            c_ref[tokens, :], jnp.concatenate(states, axis=1), preferred_element_type=f32
        )
        for index in (2 * pair, 2 * pair + 1):
            source = head_span(base + index)
            part = off[:, head_columns(index - 2 * pair)]
            gated = plain_ref[:, source] + gain_ref[:, source] * part
            gated_ref[tokens, head_columns(index)] = gated * weight_ref[:, source]
            square = gated * gated
            squares = square if squares is None else squares + square
    return squares


def own_gated_kernel(
    core_ref, entry_ref, first_ref, cum_ref, c_ref, weight_ref,
    plain0_ref, gain0_ref, plain1_ref, gain1_ref, gated_ref, squares_ref,
):
    parts = (plain0_ref, gain0_ref, plain1_ref, gain1_ref)
    for block in range(2):
        tokens = slice(block * BLOCK, (block + 1) * BLOCK)
        squares_ref[tokens, :] = gated_half(
            4 * core_ref[0], entry_ref, first_ref, cum_ref, c_ref, weight_ref, parts, gated_ref, block
        )


def other_gated_kernel(
    core_ref, entry_ref, first_ref, cum_ref, c_ref, weight_ref,
    plain0_ref, gain0_ref, plain1_ref, gain1_ref, squares_ref, gated_ref, sum_ref,
):
    parts = (plain0_ref, gain0_ref, plain1_ref, gain1_ref)
    for block in range(2):
        tokens = slice(block * BLOCK, (block + 1) * BLOCK)
        squares = squares_ref[tokens, :] + gated_half(
            4 * (1 - core_ref[0]), entry_ref, first_ref, cum_ref, c_ref, weight_ref, parts, gated_ref, block
        )
        column = jnp.sum(squares, axis=1, keepdims=True)
        rows = jnp.concatenate([column_to_row(column[:128]), column_to_row(column[128:])], axis=0)
        for peer in range(8):
            sum_ref[peer, 2 * block : 2 * block + 2, :] = rows


def gated_call(core, entry, first, cum, c_in, weight, parts, squares=None):
    last = squares is not None
    extra = (squares,) if last else ()
    shape = jax.ShapeDtypeStruct((8, 4, 128) if last else (TOK, HEAD_DIM), f32)
    return pl.pallas_call(
        other_gated_kernel if last else own_gated_kernel,
        in_specs=[smem_spec()] + [vmem_spec()] * (9 + len(extra)),
        out_specs=[vmem_spec(), vmem_spec()],
        out_shape=[jax.ShapeDtypeStruct((TOK, HALF), f32), shape],
        compiler_params=params(),
        cost_estimate=pl.CostEstimate(
            flops=70_000_000, bytes_accessed=3_000_000, transcendentals=1_000
        ),
        name="other_gated" if last else "own_gated",
    )(core, entry, first, cum, c_in, weight, *parts, *extra)


def scale_kernel(core_ref, sums_ref, own_ref, other_ref, out_hbm, buffer, sems):
    total = jnp.sum(sums_ref[...], axis=0)
    inverse = lax.rsqrt(total / (HEAD_TOTAL * HEAD_DIM) + epsilon)
    core = core_ref[0]
    copies = []
    for part in range(4):
        tokens = slice(part * 128, (part + 1) * 128)
        column = jnp.broadcast_to(inverse[part : part + 1, :], (128, 128)).T
        for base, gated_ref in ((core * HALF, own_ref), ((1 - core) * HALF, other_ref)):
            for head in range(4):
                columns = pl.ds(pl.multiple_of(base + head * HEAD_DIM, HEAD_DIM), HEAD_DIM)
                scaled = gated_ref[tokens, head_columns(head)] * column
                buffer[tokens, columns] = scaled.astype(bf16)
        copy = pltpu.make_async_copy(buffer.at[tokens, :], out_hbm.at[tokens, :], sems.at[part])
        copy.start()
        copies.append(copy)
    for copy in copies:
        copy.wait()


def scale_call(core, sums, own, other):
    return pl.pallas_call(
        scale_kernel,
        in_specs=[smem_spec()] + [vmem_spec()] * 3,
        out_specs=hbm_spec(),
        out_shape=jax.ShapeDtypeStruct((TOK, WIDTH), bf16),
        scratch_shapes=[pltpu.VMEM((TOK, WIDTH), bf16), pltpu.SemaphoreType.DMA((4,))],
        compiler_params=params(),
        name="scale",
    )(core, sums, own, other)


def shards(x_in, z_in, b_in, c_in, decays, d_skip, norm_weight):
    core = (lax.axis_index("seq") % 2).astype(jnp.int32).reshape(1)
    swap = [(i, i ^ 1) for i in range(2 * CHIPS)]
    groups = [[2 * chip + c for chip in range(CHIPS)] for c in range(2)]
    send, first_send, cum, to_end, b_t, *inputs = send_state_call(
        core, x_in, z_in, b_in, c_in, decays, d_skip
    )
    c_in = inputs[-1]
    recv = lax.ppermute(send, "seq", swap)
    keep, first_keep = keep_state_call(core, b_t, to_end, cum, inputs[1])
    part0 = diagonal_call(0, core, inputs, cum, only=0)
    recv, *part0 = lax.optimization_barrier((recv, *part0))
    pay, base = chip_call(core, keep, recv)
    pay = pay.reshape(CHIPS, 1, PIECE * HEAD_DIM)
    pay = lax.all_to_all(pay, "seq", 0, 0, axis_index_groups=groups, tiled=True)
    pre = scan_call(pay.reshape(CHIPS * PIECE, HEAD_DIM))
    pre = lax.all_to_all(pre, "seq", 0, 0, axis_index_groups=groups, tiled=True)
    pre, cum_late = lax.optimization_barrier((pre, cum))
    part0 = diagonal_call(0, core, inputs, cum_late, only=1, previous=part0)
    part1 = diagonal_call(1, core, inputs, cum_late, only=1)
    send, own = entry_call(core, pre, base)
    send, *parts = lax.optimization_barrier((send, *part0, *part1))
    part0, part1 = parts[:2], parts[2:]
    recv = lax.ppermute(send, "seq", swap)
    part1 = diagonal_call(1, core, inputs, cum, only=0, previous=part1)
    parts = (*part0, *part1)
    weight = norm_weight.astype(f32).reshape(1, WIDTH)
    own_gated, squares = gated_call(core, own, first_keep, cum, c_in, weight, parts)
    other_gated, sums = gated_call(core, recv, first_send, cum, c_in, weight, parts, squares)
    sums = lax.all_to_all(sums, "tp", 0, 0, tiled=True)
    return scale_call(core, sums, own_gated, other_gated)


def solution(mesh):
    return jax.shard_map(
        shards,
        mesh=mesh,
        in_specs=(
            P("seq", "tp"),
            P("seq", "tp"),
            P("seq", "tp"),
            P("seq", "tp"),
            P("tp", "seq"),
            P("tp"),
            P("tp"),
        ),
        out_specs=P("seq", "tp"),
        check_vma=False,
    )
```

```python
import functools

import jax
import jax.numpy as jnp
from jax import lax
from jax.experimental import pallas as pl
from jax.experimental.pallas import tpu as pltpu
from jax.sharding import PartitionSpec as P

HEAD_TOTAL = 64
HEAD_DIM = 128
STATE = 128
BLOCK = 256
CHIPS = 32

epsilon = 1e-05

HEADS = 8
TOK = 512
WIDTH = HEADS * HEAD_DIM
HALF = WIDTH // 2
ROWS = STATE // CHIPS
PIECE = 4 * ROWS + 1

VMEM_BYTES = 16 << 20
f32 = jnp.float32
bf16 = jnp.bfloat16


def params():
    return pltpu.CompilerParams(vmem_limit_bytes=VMEM_BYTES)


def smem_spec():
    return pl.BlockSpec(memory_space=pltpu.SMEM)


def vmem_spec():
    return pl.BlockSpec(memory_space=pltpu.VMEM)


def hbm_spec():
    return pl.BlockSpec(memory_space=pltpu.HBM)


def head_columns(head):
    return slice(head * HEAD_DIM, (head + 1) * HEAD_DIM)


def split3(value):
    high = value.astype(bf16)
    rest = value - high.astype(f32)
    middle = rest.astype(bf16)
    low = (rest - middle.astype(f32)).astype(bf16)
    return high, middle, low


def half_states(base, b_t, to_end, cum_ref, x_ref, first_ref, slab_ref):
    for index in range(4):
        head = base + index
        source = pl.ds(pl.multiple_of(head * HEAD_DIM, HEAD_DIM), HEAD_DIM)
        target = head_columns(index)
        weight = to_end[pl.ds(head, 1), :]
        cum = cum_ref[pl.ds(head, 1), :]
        last0 = cum[:, BLOCK - 1 : BLOCK]
        last1 = cum[:, 2 * BLOCK - 1 :]
        states = []
        for block in range(2):
            span = slice(block * BLOCK, (block + 1) * BLOCK)
            b_weighted = (b_t[:, span] * weight[:, span]).astype(bf16)
            states.append(jnp.dot(b_weighted, x_ref[span, source], preferred_element_type=f32))
        first_ref[:, target] = states[0]
        slab_ref[:STATE, target] = jnp.exp2(last1) * states[0] + states[1]
        slab_ref[STATE:, target] = jnp.broadcast_to(last0 + last1, (8, HEAD_DIM))


def send_state_kernel(
    core_ref, x_hbm, z_hbm, b_hbm, c_hbm, decay_hbm, skip_hbm,
    send_ref, first_ref, cum_ref, to_end_ref, b_t_ref, skip_ref, x_ref, z_ref, b_ref, c_ref,
    decay_ref, skip_smem, sems,
):
    copies = [
        pltpu.make_async_copy(source, target, sems.at[index])
        for index, (source, target) in enumerate(
            (
                (decay_hbm, decay_ref),
                (b_hbm, b_ref),
                (x_hbm, x_ref),
                (skip_hbm, skip_smem),
                (c_hbm, c_ref),
                (z_hbm, z_ref),
            )
        )
    ]
    for copy in copies:
        copy.start()
    row = lax.broadcasted_iota(jnp.int32, (BLOCK, BLOCK), 0)
    col = lax.broadcasted_iota(jnp.int32, (BLOCK, BLOCK), 1)
    upper = jnp.where(row <= col, 1.0, 0.0).astype(bf16)
    copies[0].wait()
    copies[1].wait()
    b_t = b_ref[...].astype(f32).T
    b_t_ref[...] = b_t
    logs = jnp.log2(decay_ref[...])
    for block in range(2):
        span = slice(block * BLOCK, (block + 1) * BLOCK)
        total = jnp.zeros((HEADS, BLOCK), f32)
        for part in reversed(split3(logs[:, span])):
            total = total + jnp.dot(part, upper, preferred_element_type=f32)
        cum_ref[:, span] = total
        to_end_ref[:, span] = jnp.exp2(total[:, BLOCK - 1 :] - total)
    copies[2].wait()
    half_states(4 * (1 - core_ref[0]), b_t, to_end_ref, cum_ref, x_ref, first_ref, send_ref)
    for copy in copies[3:]:
        copy.wait()
    for head in range(HEADS):
        skip_ref[head : head + 1, :] = jnp.full((1, HEAD_DIM), skip_smem[head], f32)


def send_state_call(core, x_in, z_in, b_in, c_in, decays, d_skip):
    arrays = [
        pltpu.with_memory_space_constraint(array, pltpu.HBM)
        for array in (x_in, z_in, b_in, c_in, decays, d_skip)
    ]
    return pl.pallas_call(
        send_state_kernel,
        in_specs=[smem_spec()] + [hbm_spec()] * 6,
        out_specs=[vmem_spec()] * 10,
        out_shape=[
            jax.ShapeDtypeStruct((STATE + 8, HALF), f32),
            jax.ShapeDtypeStruct((STATE, HALF), f32),
            jax.ShapeDtypeStruct((HEADS, TOK), f32),
            jax.ShapeDtypeStruct((HEADS, TOK), f32),
            jax.ShapeDtypeStruct((STATE, TOK), f32),
            jax.ShapeDtypeStruct((HEADS, HEAD_DIM), f32),
            jax.ShapeDtypeStruct((TOK, WIDTH), bf16),
            jax.ShapeDtypeStruct((TOK, WIDTH), bf16),
            jax.ShapeDtypeStruct((TOK, STATE), bf16),
            jax.ShapeDtypeStruct((TOK, STATE), bf16),
        ],
        scratch_shapes=[
            pltpu.VMEM((HEADS, TOK), f32),
            pltpu.SMEM((HEADS,), f32),
            pltpu.SemaphoreType.DMA((6,)),
        ],
        compiler_params=params(),
        name="send_state",
    )(core, *arrays)


def keep_state_kernel(core_ref, b_t_ref, to_end_ref, cum_ref, x_ref, keep_ref, first_ref):
    half_states(4 * core_ref[0], b_t_ref[...], to_end_ref, cum_ref, x_ref, first_ref, keep_ref)


def keep_state_call(core, b_t, to_end, cum, x_in):
    return pl.pallas_call(
        keep_state_kernel,
        in_specs=[smem_spec()] + [vmem_spec()] * 4,
        out_specs=[vmem_spec()] * 2,
        out_shape=[
            jax.ShapeDtypeStruct((STATE + 8, HALF), f32),
            jax.ShapeDtypeStruct((STATE, HALF), f32),
        ],
        compiler_params=params(),
        cost_estimate=pl.CostEstimate(
            flops=70_000_000, bytes_accessed=1_500_000, transcendentals=1_000
        ),
        name="keep_state",
    )(core, b_t, to_end, cum, x_in)


def chip_kernel(core_ref, keep_ref, recv_ref, pay_ref, base_ref):
    def write(early_ref, late_ref):
        base_ref[...] = early_ref[...]
        chip_logs = []
        for head in range(4):
            columns = head_columns(head)
            late_log = late_ref[STATE : STATE + 1, columns]
            chip_logs.append(early_ref[STATE : STATE + 1, columns] + late_log)
            state = jnp.exp2(late_log) * early_ref[:STATE, columns] + late_ref[:STATE, columns]
            for chip in range(CHIPS):
                row = chip * PIECE + head * ROWS
                pay_ref[row : row + ROWS, :] = state[chip * ROWS : (chip + 1) * ROWS, :]
        lane = lax.broadcasted_iota(jnp.int32, (1, HEAD_DIM), 1)
        logs = chip_logs[3]
        for head in range(3):
            quarter = (head + 1) * (HEAD_DIM // 4)
            inside = (lane >= quarter - HEAD_DIM // 4) & (lane < quarter)
            logs = jnp.where(inside, chip_logs[head], logs)
        for chip in range(CHIPS):
            row = (chip + 1) * PIECE - 1
            pay_ref[row : row + 1, :] = logs

    @pl.when(core_ref[0] == 0)
    def _():
        write(keep_ref, recv_ref)

    @pl.when(core_ref[0] != 0)
    def _():
        write(recv_ref, keep_ref)


def chip_call(core, keep, recv):
    return pl.pallas_call(
        chip_kernel,
        in_specs=[smem_spec(), vmem_spec(), vmem_spec()],
        out_specs=[vmem_spec(), vmem_spec()],
        out_shape=[
            jax.ShapeDtypeStruct((CHIPS * PIECE, HEAD_DIM), f32),
            jax.ShapeDtypeStruct((STATE + 8, HALF), f32),
        ],
        compiler_params=params(),
        name="chip_state",
    )(core, keep, recv)


def scan_kernel(pay_ref, out_ref):
    carries = [jnp.zeros((ROWS, HEAD_DIM), f32) for _ in range(4)]
    for chip in range(CHIPS):
        first_row = chip * PIECE
        factors = jnp.exp2(pay_ref[first_row + PIECE - 1 : first_row + PIECE, :])
        for head in range(4):
            lane = head * (HEAD_DIM // 4)
            out_ref[chip, head * ROWS : (head + 1) * ROWS, :] = carries[head]
            row = first_row + head * ROWS
            carries[head] = factors[:, lane : lane + 1] * carries[head] + pay_ref[row : row + ROWS, :]


def scan_call(pay):
    return pl.pallas_call(
        scan_kernel,
        in_specs=[vmem_spec()],
        out_specs=vmem_spec(),
        out_shape=jax.ShapeDtypeStruct((CHIPS, 4 * ROWS, HEAD_DIM), f32),
        compiler_params=params(),
        name="chip_scan",
    )(pay)


def entry_kernel(core_ref, pre_ref, base_ref, send_ref, own_ref):
    def write(plain_ref, moved_ref):
        for head in range(4):
            columns = head_columns(head)
            factor = jnp.exp2(base_ref[STATE : STATE + 1, columns])
            rows = slice(head * ROWS, (head + 1) * ROWS)
            entry = jnp.concatenate([pre_ref[chip, rows, :] for chip in range(CHIPS)], axis=0)
            plain_ref[:, columns] = entry
            moved_ref[:, columns] = factor * entry + base_ref[:STATE, columns]

    @pl.when(core_ref[0] == 0)
    def _():
        write(own_ref, send_ref)

    @pl.when(core_ref[0] != 0)
    def _():
        write(send_ref, own_ref)


def entry_call(core, pre, base):
    half_shape = jax.ShapeDtypeStruct((STATE, HALF), f32)
    return pl.pallas_call(
        entry_kernel,
        in_specs=[smem_spec(), vmem_spec(), vmem_spec()],
        out_specs=[vmem_spec(), vmem_spec()],
        out_shape=[half_shape, half_shape],
        compiler_params=params(),
        name="slab_entry",
    )(core, pre, base)


def diagonal_kernel(block, only, core_ref, skip_ref, x_ref, z_ref, b_ref, c_ref, cum_ref, *refs):
    if only is None:
        diagonal_body(block, skip_ref, x_ref, z_ref, b_ref, c_ref, cum_ref, *refs[-2:])
    else:

        @pl.when(core_ref[0] == only)
        def _():
            diagonal_body(block, skip_ref, x_ref, z_ref, b_ref, c_ref, cum_ref, *refs[-2:])


def diagonal_body(block, skip_ref, x_ref, z_ref, b_ref, c_ref, cum_ref, plain_ref, gain_ref):
    tokens = slice(block * BLOCK, (block + 1) * BLOCK)
    start = block * BLOCK
    cum = cum_ref[:, tokens]
    cum_t = cum.T
    row = lax.broadcasted_iota(jnp.int32, (128, 128), 0)
    col = lax.broadcasted_iota(jnp.int32, (128, 128), 1)
    causal = row >= col
    c_block = c_ref[tokens, :]
    b_block = b_ref[tokens, :]
    scores = []
    for tile in range(2):
        rows = slice(tile * 128, (tile + 1) * 128)
        for other in range(tile + 1):
            across = slice(other * 128, (other + 1) * 128)
            scores.append(
                lax.dot_general(
                    c_block[rows], b_block[across], (((1,), (1,)), ((), ())), preferred_element_type=f32
                )
            )
    for head in range(HEADS):
        columns = head_columns(head)
        cum_row = cum[head : head + 1, :]
        for tile in range(2):
            rows = slice(tile * 128, (tile + 1) * 128)
            here = slice(start + tile * 128, start + (tile + 1) * 128)
            cum_col = jnp.broadcast_to(cum_t[rows, head : head + 1], (128, HEAD_DIM))
            exponent = jnp.where(causal, cum_col - cum_row[:, rows], -jnp.inf)
            weights = (scores[0 if tile == 0 else 2] * jnp.exp2(exponent)).astype(bf16)
            if tile == 1:
                before = (scores[1] * jnp.exp2(cum_col - cum_row[:, :128])).astype(bf16)
                weights = jnp.concatenate([before, weights], axis=1)
            x_head = x_ref[slice(start, start + (tile + 1) * 128), columns]
            y = jnp.dot(weights, x_head, preferred_element_type=f32)
            y = y + skip_ref[head : head + 1, :] * x_ref[here, columns].astype(f32)
            half_z = 0.5 * z_ref[here, columns].astype(f32)
            gate = half_z + half_z * jnp.tanh(half_z)
            plain_ref[rows, columns] = y * gate
            gain_ref[rows, columns] = jnp.exp2(cum_col) * gate


def diagonal_call(block, core, inputs, cum, only=None, previous=()):
    shape = jax.ShapeDtypeStruct((BLOCK, WIDTH), f32)
    return pl.pallas_call(
        functools.partial(diagonal_kernel, block, only),
        in_specs=[smem_spec()] + [vmem_spec()] * (6 + len(previous)),
        out_specs=[vmem_spec(), vmem_spec()],
        out_shape=[shape, shape],
        input_output_aliases={7 + index: index for index in range(len(previous))},
        compiler_params=params(),
        cost_estimate=pl.CostEstimate(
            flops=300_000_000, bytes_accessed=3_500_000, transcendentals=1_000_000
        ),
        name="diagonal",
    )(core, *inputs, cum, *previous)


def gated_half(
    base, entry_ref, first_ref, cum_ref, c_ref, weight_ref, parts, gated_ref, block
):
    plain_ref, gain_ref = parts[2 * block : 2 * block + 2]
    wide = pl.ds(pl.multiple_of(base * HEAD_DIM, HALF), HALF)
    plain, gain, weight = plain_ref[:, wide], gain_ref[:, wide], weight_ref[:, wide]
    tokens = slice(block * BLOCK, (block + 1) * BLOCK)
    squares = None
    for pair in range(2):
        states = []
        for index in (2 * pair, 2 * pair + 1):
            columns = head_columns(index)
            state = entry_ref[:, columns]
            if block == 1:
                last = cum_ref[pl.ds(base + index, 1), :BLOCK][:, BLOCK - 1 :]
                state = jnp.exp2(last) * state + first_ref[:, columns]
            states.append(state.astype(bf16))
        off = jnp.dot(
            c_ref[tokens, :], jnp.concatenate(states, axis=1), preferred_element_type=f32
        )
        for index in (2 * pair, 2 * pair + 1):
            part = off[:, head_columns(index - 2 * pair)]
            gated = plain[:, head_columns(index)] + gain[:, head_columns(index)] * part
            gated_ref[tokens, head_columns(index)] = gated * weight[:, head_columns(index)]
            square = gated * gated
            squares = square if squares is None else squares + square
    return squares


def own_gated_kernel(
    core_ref, entry_ref, first_ref, cum_ref, c_ref, weight_ref,
    plain0_ref, gain0_ref, plain1_ref, gain1_ref, gated_ref, squares_ref,
):
    parts = (plain0_ref, gain0_ref, plain1_ref, gain1_ref)
    for block in range(2):
        tokens = slice(block * BLOCK, (block + 1) * BLOCK)
        squares_ref[tokens, :] = gated_half(
            4 * core_ref[0], entry_ref, first_ref, cum_ref, c_ref, weight_ref, parts, gated_ref, block
        )


def other_gated_kernel(
    core_ref, entry_ref, first_ref, cum_ref, c_ref, weight_ref,
    plain0_ref, gain0_ref, plain1_ref, gain1_ref, squares_ref, gated_ref, sum_ref,
):
    parts = (plain0_ref, gain0_ref, plain1_ref, gain1_ref)
    for block in range(2):
        tokens = slice(block * BLOCK, (block + 1) * BLOCK)
        squares = squares_ref[tokens, :] + gated_half(
            4 * (1 - core_ref[0]), entry_ref, first_ref, cum_ref, c_ref, weight_ref, parts, gated_ref, block
        )
        rows = jnp.concatenate([jnp.sum(squares[h * 128 : h * 128 + 128, :].T, axis=0, keepdims=True) for h in range(2)], axis=0)
        for peer in range(8):
            sum_ref[peer, 2 * block : 2 * block + 2, :] = rows


def gated_call(core, entry, first, cum, c_in, weight, parts, squares=None):
    last = squares is not None
    extra = (squares,) if last else ()
    shape = jax.ShapeDtypeStruct((8, 4, 128) if last else (TOK, HEAD_DIM), f32)
    return pl.pallas_call(
        other_gated_kernel if last else own_gated_kernel,
        in_specs=[smem_spec()] + [vmem_spec()] * (9 + len(extra)),
        out_specs=[vmem_spec(), vmem_spec()],
        out_shape=[jax.ShapeDtypeStruct((TOK, HALF), f32), shape],
        compiler_params=params(),
        cost_estimate=pl.CostEstimate(
            flops=70_000_000, bytes_accessed=3_000_000, transcendentals=1_000
        ),
        name="other_gated" if last else "own_gated",
    )(core, entry, first, cum, c_in, weight, *parts, *extra)


def scale_kernel(core_ref, sums_ref, own_ref, other_ref, out_hbm, buffer, sems):
    total = jnp.sum(sums_ref[...], axis=0)
    inverse = lax.rsqrt(total / (HEAD_TOTAL * HEAD_DIM) + epsilon)
    core = core_ref[0]
    copies = []
    for part in range(4):
        tokens = slice(part * 128, (part + 1) * 128)
        column = jnp.broadcast_to(inverse[part : part + 1, :], (128, 128)).T
        for base, gated_ref in ((core * HALF, own_ref), ((1 - core) * HALF, other_ref)):
            scaled = [gated_ref[tokens, head_columns(head)] * column for head in range(4)]
            wide = pl.ds(pl.multiple_of(base, HALF), HALF)
            buffer[tokens, wide] = jnp.concatenate(scaled, axis=1).astype(bf16)
        copy = pltpu.make_async_copy(buffer.at[tokens, :], out_hbm.at[tokens, :], sems.at[part])
        copy.start()
        copies.append(copy)
    for copy in copies:
        copy.wait()


def scale_call(core, sums, own, other):
    return pl.pallas_call(
        scale_kernel,
        in_specs=[smem_spec()] + [vmem_spec()] * 3,
        out_specs=hbm_spec(),
        out_shape=jax.ShapeDtypeStruct((TOK, WIDTH), bf16),
        scratch_shapes=[pltpu.VMEM((TOK, WIDTH), bf16), pltpu.SemaphoreType.DMA((4,))],
        compiler_params=params(),
        name="scale",
    )(core, sums, own, other)


def shards(x_in, z_in, b_in, c_in, decays, d_skip, norm_weight):
    core = (lax.axis_index("seq") % 2).astype(jnp.int32).reshape(1)
    swap = [(i, i ^ 1) for i in range(2 * CHIPS)]
    groups = [[2 * chip + c for chip in range(CHIPS)] for c in range(2)]
    send, first_send, cum, to_end, b_t, *inputs = send_state_call(
        core, x_in, z_in, b_in, c_in, decays, d_skip
    )
    c_in = inputs[-1]
    recv = lax.ppermute(send, "seq", swap)
    keep, first_keep = keep_state_call(core, b_t, to_end, cum, inputs[1])
    part0 = diagonal_call(0, core, inputs, cum, only=0)
    recv, *part0 = lax.optimization_barrier((recv, *part0))
    pay, base = chip_call(core, keep, recv)
    pay = pay.reshape(CHIPS, 1, PIECE * HEAD_DIM)
    pay = lax.all_to_all(pay, "seq", 0, 0, axis_index_groups=groups, tiled=True)
    pre = scan_call(pay.reshape(CHIPS * PIECE, HEAD_DIM))
    pre = lax.all_to_all(pre, "seq", 0, 0, axis_index_groups=groups, tiled=True)
    pre, cum_late = lax.optimization_barrier((pre, cum))
    part0 = diagonal_call(0, core, inputs, cum_late, only=1, previous=part0)
    part1 = diagonal_call(1, core, inputs, cum_late, only=1)
    send, own = entry_call(core, pre, base)
    send, *parts = lax.optimization_barrier((send, *part0, *part1))
    part0, part1 = parts[:2], parts[2:]
    recv = lax.ppermute(send, "seq", swap)
    part1 = diagonal_call(1, core, inputs, cum, only=0, previous=part1)
    parts = (*part0, *part1)
    weight = norm_weight.astype(f32).reshape(1, WIDTH)
    own_gated, squares = gated_call(core, own, first_keep, cum, c_in, weight, parts)
    other_gated, sums = gated_call(core, recv, first_send, cum, c_in, weight, parts, squares)
    sums = lax.all_to_all(sums, "tp", 0, 0, tiled=True)
    return scale_call(core, sums, own_gated, other_gated)


def solution(mesh):
    return jax.shard_map(
        shards,
        mesh=mesh,
        in_specs=(
            P("seq", "tp"),
            P("seq", "tp"),
            P("seq", "tp"),
            P("seq", "tp"),
            P("tp", "seq"),
            P("tp"),
            P("tp"),
        ),
        out_specs=P("seq", "tp"),
        check_vma=False,
    )
```

```python
import functools

import jax
import jax.numpy as jnp
from jax import lax
from jax.experimental import pallas as pl
from jax.experimental.pallas import tpu as pltpu
from jax.sharding import PartitionSpec as P

HEAD_TOTAL = 64
HEAD_DIM = 128
STATE = 128
BLOCK = 256
CHIPS = 32

epsilon = 1e-05

HEADS = 8
TOK = 512
WIDTH = HEADS * HEAD_DIM
HALF = WIDTH // 2
ROWS = STATE // CHIPS
PIECE = 4 * ROWS + 1

VMEM_BYTES = 16 << 20
f32 = jnp.float32
bf16 = jnp.bfloat16


def params():
    return pltpu.CompilerParams(vmem_limit_bytes=VMEM_BYTES)


def smem_spec():
    return pl.BlockSpec(memory_space=pltpu.SMEM)


def vmem_spec():
    return pl.BlockSpec(memory_space=pltpu.VMEM)


def hbm_spec():
    return pl.BlockSpec(memory_space=pltpu.HBM)


def head_columns(head):
    return slice(head * HEAD_DIM, (head + 1) * HEAD_DIM)


def split3(value):
    high = value.astype(bf16)
    rest = value - high.astype(f32)
    middle = rest.astype(bf16)
    low = (rest - middle.astype(f32)).astype(bf16)
    return high, middle, low


def half_states(base, b_t, to_end, cum_ref, x_ref, first_ref, slab_ref):
    for index in range(4):
        head = base + index
        source = pl.ds(pl.multiple_of(head * HEAD_DIM, HEAD_DIM), HEAD_DIM)
        target = head_columns(index)
        weight = to_end[pl.ds(head, 1), :]
        cum = cum_ref[pl.ds(head, 1), :]
        last0 = cum[:, BLOCK - 1 : BLOCK]
        last1 = cum[:, 2 * BLOCK - 1 :]
        states = []
        for block in range(2):
            span = slice(block * BLOCK, (block + 1) * BLOCK)
            b_weighted = (b_t[:, span] * weight[:, span]).astype(bf16)
            states.append(jnp.dot(b_weighted, x_ref[span, source], preferred_element_type=f32))
        first_ref[:, target] = states[0]
        slab_ref[:STATE, target] = jnp.exp2(last1) * states[0] + states[1]
        slab_ref[STATE:, target] = jnp.broadcast_to(last0 + last1, (8, HEAD_DIM))


def send_state_kernel(
    core_ref, x_hbm, z_hbm, b_hbm, c_hbm, decay_hbm, skip_hbm,
    send_ref, first_ref, cum_ref, to_end_ref, b_t_ref, skip_ref, x_ref, z_ref, b_ref, c_ref,
    decay_ref, skip_smem, sems,
):
    copies = [
        pltpu.make_async_copy(source, target, sems.at[index])
        for index, (source, target) in enumerate(
            (
                (decay_hbm, decay_ref),
                (b_hbm, b_ref),
                (x_hbm, x_ref),
                (skip_hbm, skip_smem),
                (c_hbm, c_ref),
                (z_hbm, z_ref),
            )
        )
    ]
    for copy in copies:
        copy.start()
    row = lax.broadcasted_iota(jnp.int32, (BLOCK, BLOCK), 0)
    col = lax.broadcasted_iota(jnp.int32, (BLOCK, BLOCK), 1)
    upper = jnp.where(row <= col, 1.0, 0.0).astype(bf16)
    copies[0].wait()
    copies[1].wait()
    b_t = b_ref[...].astype(f32).T
    b_t_ref[...] = b_t
    logs = jnp.log2(decay_ref[...])
    for block in range(2):
        span = slice(block * BLOCK, (block + 1) * BLOCK)
        total = jnp.zeros((HEADS, BLOCK), f32)
        for part in reversed(split3(logs[:, span])):
            total = total + jnp.dot(part, upper, preferred_element_type=f32)
        cum_ref[:, span] = total
        to_end_ref[:, span] = jnp.exp2(total[:, BLOCK - 1 :] - total)
    copies[2].wait()
    half_states(4 * (1 - core_ref[0]), b_t, to_end_ref, cum_ref, x_ref, first_ref, send_ref)
    for copy in copies[3:]:
        copy.wait()
    for head in range(HEADS):
        skip_ref[head : head + 1, :] = jnp.full((1, HEAD_DIM), skip_smem[head], f32)


def send_state_call(core, x_in, z_in, b_in, c_in, decays, d_skip):
    arrays = [
        pltpu.with_memory_space_constraint(array, pltpu.HBM)
        for array in (x_in, z_in, b_in, c_in, decays, d_skip)
    ]
    return pl.pallas_call(
        send_state_kernel,
        in_specs=[smem_spec()] + [hbm_spec()] * 6,
        out_specs=[vmem_spec()] * 10,
        out_shape=[
            jax.ShapeDtypeStruct((STATE + 8, HALF), f32),
            jax.ShapeDtypeStruct((STATE, HALF), f32),
            jax.ShapeDtypeStruct((HEADS, TOK), f32),
            jax.ShapeDtypeStruct((HEADS, TOK), f32),
            jax.ShapeDtypeStruct((STATE, TOK), f32),
            jax.ShapeDtypeStruct((HEADS, HEAD_DIM), f32),
            jax.ShapeDtypeStruct((TOK, WIDTH), bf16),
            jax.ShapeDtypeStruct((TOK, WIDTH), bf16),
            jax.ShapeDtypeStruct((TOK, STATE), bf16),
            jax.ShapeDtypeStruct((TOK, STATE), bf16),
        ],
        scratch_shapes=[
            pltpu.VMEM((HEADS, TOK), f32),
            pltpu.SMEM((HEADS,), f32),
            pltpu.SemaphoreType.DMA((6,)),
        ],
        compiler_params=params(),
        name="send_state",
    )(core, *arrays)


def keep_state_kernel(core_ref, b_t_ref, to_end_ref, cum_ref, x_ref, keep_ref, first_ref):
    half_states(4 * core_ref[0], b_t_ref[...], to_end_ref, cum_ref, x_ref, first_ref, keep_ref)


def keep_state_call(core, b_t, to_end, cum, x_in):
    return pl.pallas_call(
        keep_state_kernel,
        in_specs=[smem_spec()] + [vmem_spec()] * 4,
        out_specs=[vmem_spec()] * 2,
        out_shape=[
            jax.ShapeDtypeStruct((STATE + 8, HALF), f32),
            jax.ShapeDtypeStruct((STATE, HALF), f32),
        ],
        compiler_params=params(),
        cost_estimate=pl.CostEstimate(
            flops=70_000_000, bytes_accessed=1_500_000, transcendentals=1_000
        ),
        name="keep_state",
    )(core, b_t, to_end, cum, x_in)


def chip_kernel(core_ref, keep_ref, recv_ref, pay_ref, base_ref):
    def write(early_ref, late_ref):
        base_ref[...] = early_ref[...]
        chip_logs = []
        for head in range(4):
            columns = head_columns(head)
            late_log = late_ref[STATE : STATE + 1, columns]
            chip_logs.append(early_ref[STATE : STATE + 1, columns] + late_log)
            state = jnp.exp2(late_log) * early_ref[:STATE, columns] + late_ref[:STATE, columns]
            for chip in range(CHIPS):
                row = chip * PIECE + head * ROWS
                pay_ref[row : row + ROWS, :] = state[chip * ROWS : (chip + 1) * ROWS, :]
        lane = lax.broadcasted_iota(jnp.int32, (1, HEAD_DIM), 1)
        logs = chip_logs[3]
        for head in range(3):
            quarter = (head + 1) * (HEAD_DIM // 4)
            inside = (lane >= quarter - HEAD_DIM // 4) & (lane < quarter)
            logs = jnp.where(inside, chip_logs[head], logs)
        for chip in range(CHIPS):
            row = (chip + 1) * PIECE - 1
            pay_ref[row : row + 1, :] = logs

    @pl.when(core_ref[0] == 0)
    def _():
        write(keep_ref, recv_ref)

    @pl.when(core_ref[0] != 0)
    def _():
        write(recv_ref, keep_ref)


def chip_call(core, keep, recv):
    return pl.pallas_call(
        chip_kernel,
        in_specs=[smem_spec(), vmem_spec(), vmem_spec()],
        out_specs=[vmem_spec(), vmem_spec()],
        out_shape=[
            jax.ShapeDtypeStruct((CHIPS * PIECE, HEAD_DIM), f32),
            jax.ShapeDtypeStruct((STATE + 8, HALF), f32),
        ],
        compiler_params=params(),
        name="chip_state",
    )(core, keep, recv)


def scan_kernel(pay_ref, out_ref):
    upper = lax.broadcasted_iota(jnp.int32, (2 * ROWS, HEAD_DIM), 0) < ROWS
    carries = [jnp.zeros((2 * ROWS, HEAD_DIM), f32) for _ in range(2)]
    for chip in range(CHIPS):
        first_row = chip * PIECE
        factors = jnp.exp2(pay_ref[first_row + PIECE - 1 : first_row + PIECE, :])
        for pair in range(2):
            lane = 2 * pair * (HEAD_DIM // 4)
            other = lane + HEAD_DIM // 4
            factor = jnp.where(upper, factors[:, lane : lane + 1], factors[:, other : other + 1])
            out_ref[chip, 2 * pair * ROWS : 2 * (pair + 1) * ROWS, :] = carries[pair]
            row = first_row + 2 * pair * ROWS
            carries[pair] = factor * carries[pair] + pay_ref[row : row + 2 * ROWS, :]


def scan_call(pay):
    return pl.pallas_call(
        scan_kernel,
        in_specs=[vmem_spec()],
        out_specs=vmem_spec(),
        out_shape=jax.ShapeDtypeStruct((CHIPS, 4 * ROWS, HEAD_DIM), f32),
        compiler_params=params(),
        name="chip_scan",
    )(pay)


def entry_kernel(core_ref, pre_ref, base_ref, send_ref, own_ref):
    def write(plain_ref, moved_ref):
        for head in range(4):
            columns = head_columns(head)
            factor = jnp.exp2(base_ref[STATE : STATE + 1, columns])
            rows = slice(head * ROWS, (head + 1) * ROWS)
            entry = jnp.concatenate([pre_ref[chip, rows, :] for chip in range(CHIPS)], axis=0)
            plain_ref[:, columns] = entry
            moved_ref[:, columns] = factor * entry + base_ref[:STATE, columns]

    @pl.when(core_ref[0] == 0)
    def _():
        write(own_ref, send_ref)

    @pl.when(core_ref[0] != 0)
    def _():
        write(send_ref, own_ref)


def entry_call(core, pre, base):
    half_shape = jax.ShapeDtypeStruct((STATE, HALF), f32)
    return pl.pallas_call(
        entry_kernel,
        in_specs=[smem_spec(), vmem_spec(), vmem_spec()],
        out_specs=[vmem_spec(), vmem_spec()],
        out_shape=[half_shape, half_shape],
        compiler_params=params(),
        name="slab_entry",
    )(core, pre, base)


def diagonal_kernel(block, only, core_ref, skip_ref, x_ref, z_ref, b_ref, c_ref, cum_ref, *refs):
    if only is None:
        diagonal_body(block, skip_ref, x_ref, z_ref, b_ref, c_ref, cum_ref, *refs[-2:])
    else:

        @pl.when(core_ref[0] == only)
        def _():
            diagonal_body(block, skip_ref, x_ref, z_ref, b_ref, c_ref, cum_ref, *refs[-2:])


def diagonal_body(block, skip_ref, x_ref, z_ref, b_ref, c_ref, cum_ref, plain_ref, gain_ref):
    tokens = slice(block * BLOCK, (block + 1) * BLOCK)
    start = block * BLOCK
    cum = cum_ref[:, tokens]
    cum_t = cum.T
    row = lax.broadcasted_iota(jnp.int32, (128, 128), 0)
    col = lax.broadcasted_iota(jnp.int32, (128, 128), 1)
    causal = row >= col
    c_block = c_ref[tokens, :]
    b_block = b_ref[tokens, :]
    scores = []
    for tile in range(2):
        rows = slice(tile * 128, (tile + 1) * 128)
        for other in range(tile + 1):
            across = slice(other * 128, (other + 1) * 128)
            scores.append(
                lax.dot_general(
                    c_block[rows], b_block[across], (((1,), (1,)), ((), ())), preferred_element_type=f32
                )
            )
    for head in range(HEADS):
        columns = head_columns(head)
        cum_row = cum[head : head + 1, :]
        for tile in range(2):
            rows = slice(tile * 128, (tile + 1) * 128)
            here = slice(start + tile * 128, start + (tile + 1) * 128)
            cum_col = jnp.broadcast_to(cum_t[rows, head : head + 1], (128, HEAD_DIM))
            exponent = jnp.where(causal, cum_col - cum_row[:, rows], -jnp.inf)
            weights = (scores[0 if tile == 0 else 2] * jnp.exp2(exponent)).astype(bf16)
            if tile == 1:
                before = (scores[1] * jnp.exp2(cum_col - cum_row[:, :128])).astype(bf16)
                weights = jnp.concatenate([before, weights], axis=1)
            x_head = x_ref[slice(start, start + (tile + 1) * 128), columns]
            y = jnp.dot(weights, x_head, preferred_element_type=f32)
            y = y + skip_ref[head : head + 1, :] * x_ref[here, columns].astype(f32)
            half_z = 0.5 * z_ref[here, columns].astype(f32)
            gate = half_z + half_z * jnp.tanh(half_z)
            plain_ref[rows, columns] = y * gate
            gain_ref[rows, columns] = jnp.exp2(cum_col) * gate


def diagonal_call(block, core, inputs, cum, only=None, previous=()):
    shape = jax.ShapeDtypeStruct((BLOCK, WIDTH), f32)
    return pl.pallas_call(
        functools.partial(diagonal_kernel, block, only),
        in_specs=[smem_spec()] + [vmem_spec()] * (6 + len(previous)),
        out_specs=[vmem_spec(), vmem_spec()],
        out_shape=[shape, shape],
        input_output_aliases={7 + index: index for index in range(len(previous))},
        compiler_params=params(),
        cost_estimate=pl.CostEstimate(
            flops=300_000_000, bytes_accessed=3_500_000, transcendentals=1_000_000
        ),
        name="diagonal",
    )(core, *inputs, cum, *previous)


def gated_half(
    base, entry_ref, first_ref, cum_ref, c_ref, weight_ref, parts, gated_ref, block
):
    plain_ref, gain_ref = parts[2 * block : 2 * block + 2]
    wide = pl.ds(pl.multiple_of(base * HEAD_DIM, HALF), HALF)
    plain, gain, weight = plain_ref[:, wide], gain_ref[:, wide], weight_ref[:, wide]
    tokens = slice(block * BLOCK, (block + 1) * BLOCK)
    squares = None
    for pair in range(2):
        states = []
        for index in (2 * pair, 2 * pair + 1):
            columns = head_columns(index)
            state = entry_ref[:, columns]
            if block == 1:
                last = cum_ref[pl.ds(base + index, 1), :BLOCK][:, BLOCK - 1 :]
                state = jnp.exp2(last) * state + first_ref[:, columns]
            states.append(state.astype(bf16))
        off = jnp.dot(
            c_ref[tokens, :], jnp.concatenate(states, axis=1), preferred_element_type=f32
        )
        for index in (2 * pair, 2 * pair + 1):
            part = off[:, head_columns(index - 2 * pair)]
            gated = plain[:, head_columns(index)] + gain[:, head_columns(index)] * part
            gated_ref[tokens, head_columns(index)] = gated * weight[:, head_columns(index)]
            square = gated * gated
            squares = square if squares is None else squares + square
    return squares


def own_gated_kernel(
    core_ref, entry_ref, first_ref, cum_ref, c_ref, weight_ref,
    plain0_ref, gain0_ref, plain1_ref, gain1_ref, gated_ref, squares_ref,
):
    parts = (plain0_ref, gain0_ref, plain1_ref, gain1_ref)
    for block in range(2):
        tokens = slice(block * BLOCK, (block + 1) * BLOCK)
        squares_ref[tokens, :] = gated_half(
            4 * core_ref[0], entry_ref, first_ref, cum_ref, c_ref, weight_ref, parts, gated_ref, block
        )


def other_gated_kernel(
    core_ref, entry_ref, first_ref, cum_ref, c_ref, weight_ref,
    plain0_ref, gain0_ref, plain1_ref, gain1_ref, squares_ref, gated_ref, sum_ref,
):
    parts = (plain0_ref, gain0_ref, plain1_ref, gain1_ref)
    for block in range(2):
        tokens = slice(block * BLOCK, (block + 1) * BLOCK)
        squares = squares_ref[tokens, :] + gated_half(
            4 * (1 - core_ref[0]), entry_ref, first_ref, cum_ref, c_ref, weight_ref, parts, gated_ref, block
        )
        rows = jnp.concatenate([jnp.sum(squares[h * 128 : h * 128 + 128, :].T, axis=0, keepdims=True) for h in range(2)], axis=0)
        for peer in range(8):
            sum_ref[peer, 2 * block : 2 * block + 2, :] = rows


def gated_call(core, entry, first, cum, c_in, weight, parts, squares=None):
    last = squares is not None
    extra = (squares,) if last else ()
    shape = jax.ShapeDtypeStruct((8, 4, 128) if last else (TOK, HEAD_DIM), f32)
    return pl.pallas_call(
        other_gated_kernel if last else own_gated_kernel,
        in_specs=[smem_spec()] + [vmem_spec()] * (9 + len(extra)),
        out_specs=[vmem_spec(), vmem_spec()],
        out_shape=[jax.ShapeDtypeStruct((TOK, HALF), f32), shape],
        compiler_params=params(),
        cost_estimate=pl.CostEstimate(
            flops=70_000_000, bytes_accessed=3_000_000, transcendentals=1_000
        ),
        name="other_gated" if last else "own_gated",
    )(core, entry, first, cum, c_in, weight, *parts, *extra)


def scale_kernel(core_ref, sums_ref, own_ref, other_ref, out_hbm, buffer, sems):
    total = jnp.sum(sums_ref[...], axis=0)
    inverse = lax.rsqrt(total / (HEAD_TOTAL * HEAD_DIM) + epsilon)
    core = core_ref[0]
    copies = []
    for part in range(4):
        tokens = slice(part * 128, (part + 1) * 128)
        column = jnp.broadcast_to(inverse[part : part + 1, :], (128, 128)).T
        for base, gated_ref in ((core * HALF, own_ref), ((1 - core) * HALF, other_ref)):
            scaled = [gated_ref[tokens, head_columns(head)] * column for head in range(4)]
            wide = pl.ds(pl.multiple_of(base, HALF), HALF)
            buffer[tokens, wide] = jnp.concatenate(scaled, axis=1).astype(bf16)
        copy = pltpu.make_async_copy(buffer.at[tokens, :], out_hbm.at[tokens, :], sems.at[part])
        copy.start()
        copies.append(copy)
    for copy in copies:
        copy.wait()


def scale_call(core, sums, own, other):
    return pl.pallas_call(
        scale_kernel,
        in_specs=[smem_spec()] + [vmem_spec()] * 3,
        out_specs=hbm_spec(),
        out_shape=jax.ShapeDtypeStruct((TOK, WIDTH), bf16),
        scratch_shapes=[pltpu.VMEM((TOK, WIDTH), bf16), pltpu.SemaphoreType.DMA((4,))],
        compiler_params=params(),
        name="scale",
    )(core, sums, own, other)


def shards(x_in, z_in, b_in, c_in, decays, d_skip, norm_weight):
    core = (lax.axis_index("seq") % 2).astype(jnp.int32).reshape(1)
    swap = [(i, i ^ 1) for i in range(2 * CHIPS)]
    groups = [[2 * chip + c for chip in range(CHIPS)] for c in range(2)]
    send, first_send, cum, to_end, b_t, *inputs = send_state_call(
        core, x_in, z_in, b_in, c_in, decays, d_skip
    )
    c_in = inputs[-1]
    recv = lax.ppermute(send, "seq", swap)
    keep, first_keep = keep_state_call(core, b_t, to_end, cum, inputs[1])
    part0 = diagonal_call(0, core, inputs, cum, only=0)
    recv, *part0 = lax.optimization_barrier((recv, *part0))
    pay, base = chip_call(core, keep, recv)
    pay = pay.reshape(CHIPS, 1, PIECE * HEAD_DIM)
    pay = lax.all_to_all(pay, "seq", 0, 0, axis_index_groups=groups, tiled=True)
    pre = scan_call(pay.reshape(CHIPS * PIECE, HEAD_DIM))
    pre = lax.all_to_all(pre, "seq", 0, 0, axis_index_groups=groups, tiled=True)
    pre, cum_late = lax.optimization_barrier((pre, cum))
    part0 = diagonal_call(0, core, inputs, cum_late, only=1, previous=part0)
    part1 = diagonal_call(1, core, inputs, cum_late, only=1)
    send, own = entry_call(core, pre, base)
    send, *parts = lax.optimization_barrier((send, *part0, *part1))
    part0, part1 = parts[:2], parts[2:]
    recv = lax.ppermute(send, "seq", swap)
    part1 = diagonal_call(1, core, inputs, cum, only=0, previous=part1)
    parts = (*part0, *part1)
    weight = norm_weight.astype(f32).reshape(1, WIDTH)
    own_gated, squares = gated_call(core, own, first_keep, cum, c_in, weight, parts)
    other_gated, sums = gated_call(core, recv, first_send, cum, c_in, weight, parts, squares)
    sums = lax.all_to_all(sums, "tp", 0, 0, tiled=True)
    return scale_call(core, sums, own_gated, other_gated)


def solution(mesh):
    return jax.shard_map(
        shards,
        mesh=mesh,
        in_specs=(
            P("seq", "tp"),
            P("seq", "tp"),
            P("seq", "tp"),
            P("seq", "tp"),
            P("tp", "seq"),
            P("tp"),
            P("tp"),
        ),
        out_specs=P("seq", "tp"),
        check_vma=False,
    )
```

```python
import functools

import jax
import jax.numpy as jnp
from jax import lax
from jax.experimental import pallas as pl
from jax.experimental.pallas import tpu as pltpu
from jax.sharding import PartitionSpec as P

HEAD_TOTAL = 64
HEAD_DIM = 128
STATE = 128
BLOCK = 256
CHIPS = 32

epsilon = 1e-05

HEADS = 8
TOK = 512
WIDTH = HEADS * HEAD_DIM
HALF = WIDTH // 2
ROWS = STATE // CHIPS
PIECE = 4 * ROWS + 1

VMEM_BYTES = 16 << 20
f32 = jnp.float32
bf16 = jnp.bfloat16


def params():
    return pltpu.CompilerParams(vmem_limit_bytes=VMEM_BYTES)


def smem_spec():
    return pl.BlockSpec(memory_space=pltpu.SMEM)


def vmem_spec():
    return pl.BlockSpec(memory_space=pltpu.VMEM)


def hbm_spec():
    return pl.BlockSpec(memory_space=pltpu.HBM)


def head_columns(head):
    return slice(head * HEAD_DIM, (head + 1) * HEAD_DIM)


def split3(value):
    high = value.astype(bf16)
    rest = value - high.astype(f32)
    middle = rest.astype(bf16)
    low = (rest - middle.astype(f32)).astype(bf16)
    return high, middle, low


def half_states(base, b_t, to_end, cum_ref, x_ref, first_ref, slab_ref):
    for index in range(4):
        head = base + index
        source = pl.ds(pl.multiple_of(head * HEAD_DIM, HEAD_DIM), HEAD_DIM)
        target = head_columns(index)
        weight = to_end[pl.ds(head, 1), :]
        cum = cum_ref[pl.ds(head, 1), :]
        last0 = cum[:, BLOCK - 1 : BLOCK]
        last1 = cum[:, 2 * BLOCK - 1 :]
        states = []
        for block in range(2):
            span = slice(block * BLOCK, (block + 1) * BLOCK)
            b_weighted = (b_t[:, span] * weight[:, span]).astype(bf16)
            states.append(jnp.dot(b_weighted, x_ref[span, source], preferred_element_type=f32))
        first_ref[:, target] = states[0]
        slab_ref[:STATE, target] = jnp.exp2(last1) * states[0] + states[1]
        slab_ref[STATE:, target] = jnp.broadcast_to(last0 + last1, (8, HEAD_DIM))


def send_state_kernel(
    core_ref, x_hbm, z_hbm, b_hbm, c_hbm, decay_hbm, skip_hbm,
    send_ref, first_ref, cum_ref, to_end_ref, b_t_ref, skip_ref, x_ref, z_ref, b_ref, c_ref,
    decay_ref, skip_smem, sems,
):
    copies = [
        pltpu.make_async_copy(source, target, sems.at[index])
        for index, (source, target) in enumerate(
            (
                (decay_hbm, decay_ref),
                (b_hbm, b_ref),
                (x_hbm, x_ref),
                (skip_hbm, skip_smem),
                (c_hbm, c_ref),
                (z_hbm, z_ref),
            )
        )
    ]
    for copy in copies:
        copy.start()
    row = lax.broadcasted_iota(jnp.int32, (BLOCK, BLOCK), 0)
    col = lax.broadcasted_iota(jnp.int32, (BLOCK, BLOCK), 1)
    upper = jnp.where(row <= col, 1.0, 0.0).astype(bf16)
    copies[0].wait()
    copies[1].wait()
    b_t = b_ref[...].astype(f32).T
    b_t_ref[...] = b_t
    logs = jnp.log2(decay_ref[...])
    for block in range(2):
        span = slice(block * BLOCK, (block + 1) * BLOCK)
        total = jnp.zeros((HEADS, BLOCK), f32)
        for part in reversed(split3(logs[:, span])):
            total = total + jnp.dot(part, upper, preferred_element_type=f32)
        cum_ref[:, span] = total
        to_end_ref[:, span] = jnp.exp2(total[:, BLOCK - 1 :] - total)
    copies[2].wait()
    half_states(4 * (1 - core_ref[0]), b_t, to_end_ref, cum_ref, x_ref, first_ref, send_ref)
    for copy in copies[3:]:
        copy.wait()
    for head in range(HEADS):
        skip_ref[head : head + 1, :] = jnp.full((1, HEAD_DIM), skip_smem[head], f32)


def send_state_call(core, x_in, z_in, b_in, c_in, decays, d_skip):
    arrays = [
        pltpu.with_memory_space_constraint(array, pltpu.HBM)
        for array in (x_in, z_in, b_in, c_in, decays, d_skip)
    ]
    return pl.pallas_call(
        send_state_kernel,
        in_specs=[smem_spec()] + [hbm_spec()] * 6,
        out_specs=[vmem_spec()] * 10,
        out_shape=[
            jax.ShapeDtypeStruct((STATE + 8, HALF), f32),
            jax.ShapeDtypeStruct((STATE, HALF), f32),
            jax.ShapeDtypeStruct((HEADS, TOK), f32),
            jax.ShapeDtypeStruct((HEADS, TOK), f32),
            jax.ShapeDtypeStruct((STATE, TOK), f32),
            jax.ShapeDtypeStruct((HEADS, HEAD_DIM), f32),
            jax.ShapeDtypeStruct((TOK, WIDTH), bf16),
            jax.ShapeDtypeStruct((TOK, WIDTH), bf16),
            jax.ShapeDtypeStruct((TOK, STATE), bf16),
            jax.ShapeDtypeStruct((TOK, STATE), bf16),
        ],
        scratch_shapes=[
            pltpu.VMEM((HEADS, TOK), f32),
            pltpu.SMEM((HEADS,), f32),
            pltpu.SemaphoreType.DMA((6,)),
        ],
        compiler_params=params(),
        name="send_state",
    )(core, *arrays)


def keep_state_kernel(core_ref, b_t_ref, to_end_ref, cum_ref, x_ref, keep_ref, first_ref):
    half_states(4 * core_ref[0], b_t_ref[...], to_end_ref, cum_ref, x_ref, first_ref, keep_ref)


def keep_state_call(core, b_t, to_end, cum, x_in):
    return pl.pallas_call(
        keep_state_kernel,
        in_specs=[smem_spec()] + [vmem_spec()] * 4,
        out_specs=[vmem_spec()] * 2,
        out_shape=[
            jax.ShapeDtypeStruct((STATE + 8, HALF), f32),
            jax.ShapeDtypeStruct((STATE, HALF), f32),
        ],
        compiler_params=params(),
        cost_estimate=pl.CostEstimate(
            flops=70_000_000, bytes_accessed=1_500_000, transcendentals=1_000
        ),
        name="keep_state",
    )(core, b_t, to_end, cum, x_in)


def chip_kernel(core_ref, keep_ref, recv_ref, pay_ref, base_ref):
    def write(early_ref, late_ref):
        base_ref[...] = early_ref[...]
        chip_logs = []
        for head in range(4):
            columns = head_columns(head)
            late_log = late_ref[STATE : STATE + 1, columns]
            chip_logs.append(early_ref[STATE : STATE + 1, columns] + late_log)
            state = jnp.exp2(late_log) * early_ref[:STATE, columns] + late_ref[:STATE, columns]
            for chip in range(CHIPS):
                row = chip * PIECE + head * ROWS
                pay_ref[row : row + ROWS, :] = state[chip * ROWS : (chip + 1) * ROWS, :]
        lane = lax.broadcasted_iota(jnp.int32, (1, HEAD_DIM), 1)
        logs = chip_logs[3]
        for head in range(3):
            quarter = (head + 1) * (HEAD_DIM // 4)
            inside = (lane >= quarter - HEAD_DIM // 4) & (lane < quarter)
            logs = jnp.where(inside, chip_logs[head], logs)
        for chip in range(CHIPS):
            row = (chip + 1) * PIECE - 1
            pay_ref[row : row + 1, :] = logs

    @pl.when(core_ref[0] == 0)
    def _():
        write(keep_ref, recv_ref)

    @pl.when(core_ref[0] != 0)
    def _():
        write(recv_ref, keep_ref)


def chip_call(core, keep, recv):
    return pl.pallas_call(
        chip_kernel,
        in_specs=[smem_spec(), vmem_spec(), vmem_spec()],
        out_specs=[vmem_spec(), vmem_spec()],
        out_shape=[
            jax.ShapeDtypeStruct((CHIPS * PIECE, HEAD_DIM), f32),
            jax.ShapeDtypeStruct((STATE + 8, HALF), f32),
        ],
        compiler_params=params(),
        name="chip_state",
    )(core, keep, recv)


def scan_kernel(pay_ref, out_ref):
    upper = lax.broadcasted_iota(jnp.int32, (2 * ROWS, HEAD_DIM), 0) < ROWS
    carries = [jnp.zeros((2 * ROWS, HEAD_DIM), f32) for _ in range(2)]
    logs = pay_ref[pl.ds(PIECE - 1, CHIPS, stride=PIECE), :]
    decayed = jnp.exp2(logs)
    spread = [
        jnp.broadcast_to(decayed[:, head * (HEAD_DIM // 4) : head * (HEAD_DIM // 4) + 1], (CHIPS, HEAD_DIM))
        for head in range(4)
    ]
    for chip in range(CHIPS):
        first_row = chip * PIECE
        for pair in range(2):
            here = slice(chip, chip + 1)
            factor = jnp.where(upper, spread[2 * pair][here, :], spread[2 * pair + 1][here, :])
            out_ref[chip, 2 * pair * ROWS : 2 * (pair + 1) * ROWS, :] = carries[pair]
            row = first_row + 2 * pair * ROWS
            carries[pair] = factor * carries[pair] + pay_ref[row : row + 2 * ROWS, :]


def scan_call(pay):
    return pl.pallas_call(
        scan_kernel,
        in_specs=[vmem_spec()],
        out_specs=vmem_spec(),
        out_shape=jax.ShapeDtypeStruct((CHIPS, 4 * ROWS, HEAD_DIM), f32),
        compiler_params=params(),
        name="chip_scan",
    )(pay)


def entry_kernel(core_ref, pre_ref, base_ref, send_ref, own_ref):
    def write(plain_ref, moved_ref):
        for head in range(4):
            columns = head_columns(head)
            factor = jnp.exp2(base_ref[STATE : STATE + 1, columns])
            rows = slice(head * ROWS, (head + 1) * ROWS)
            entry = jnp.concatenate([pre_ref[chip, rows, :] for chip in range(CHIPS)], axis=0)
            plain_ref[:, columns] = entry
            moved_ref[:, columns] = factor * entry + base_ref[:STATE, columns]

    @pl.when(core_ref[0] == 0)
    def _():
        write(own_ref, send_ref)

    @pl.when(core_ref[0] != 0)
    def _():
        write(send_ref, own_ref)


def entry_call(core, pre, base):
    half_shape = jax.ShapeDtypeStruct((STATE, HALF), f32)
    return pl.pallas_call(
        entry_kernel,
        in_specs=[smem_spec(), vmem_spec(), vmem_spec()],
        out_specs=[vmem_spec(), vmem_spec()],
        out_shape=[half_shape, half_shape],
        compiler_params=params(),
        name="slab_entry",
    )(core, pre, base)


def diagonal_kernel(block, only, core_ref, skip_ref, x_ref, z_ref, b_ref, c_ref, cum_ref, *refs):
    if only is None:
        diagonal_body(block, skip_ref, x_ref, z_ref, b_ref, c_ref, cum_ref, *refs[-2:])
    else:

        @pl.when(core_ref[0] == only)
        def _():
            diagonal_body(block, skip_ref, x_ref, z_ref, b_ref, c_ref, cum_ref, *refs[-2:])


def diagonal_body(block, skip_ref, x_ref, z_ref, b_ref, c_ref, cum_ref, plain_ref, gain_ref):
    tokens = slice(block * BLOCK, (block + 1) * BLOCK)
    start = block * BLOCK
    cum = cum_ref[:, tokens]
    cum_t = cum.T
    row = lax.broadcasted_iota(jnp.int32, (128, 128), 0)
    col = lax.broadcasted_iota(jnp.int32, (128, 128), 1)
    causal = row >= col
    c_block = c_ref[tokens, :]
    b_block = b_ref[tokens, :]
    scores = []
    for tile in range(2):
        rows = slice(tile * 128, (tile + 1) * 128)
        for other in range(tile + 1):
            across = slice(other * 128, (other + 1) * 128)
            scores.append(
                lax.dot_general(
                    c_block[rows], b_block[across], (((1,), (1,)), ((), ())), preferred_element_type=f32
                )
            )
    for head in range(HEADS):
        columns = head_columns(head)
        cum_row = cum[head : head + 1, :]
        for tile in range(2):
            rows = slice(tile * 128, (tile + 1) * 128)
            here = slice(start + tile * 128, start + (tile + 1) * 128)
            cum_col = jnp.broadcast_to(cum_t[rows, head : head + 1], (128, HEAD_DIM))
            exponent = jnp.where(causal, cum_col - cum_row[:, rows], -jnp.inf)
            weights = (scores[0 if tile == 0 else 2] * jnp.exp2(exponent)).astype(bf16)
            if tile == 1:
                before = (scores[1] * jnp.exp2(cum_col - cum_row[:, :128])).astype(bf16)
                weights = jnp.concatenate([before, weights], axis=1)
            x_head = x_ref[slice(start, start + (tile + 1) * 128), columns]
            y = jnp.dot(weights, x_head, preferred_element_type=f32)
            y = y + skip_ref[head : head + 1, :] * x_ref[here, columns].astype(f32)
            half_z = 0.5 * z_ref[here, columns].astype(f32)
            gate = half_z + half_z * jnp.tanh(half_z)
            plain_ref[rows, columns] = y * gate
            gain_ref[rows, columns] = jnp.exp2(cum_col) * gate


def diagonal_call(block, core, inputs, cum, only=None, previous=()):
    shape = jax.ShapeDtypeStruct((BLOCK, WIDTH), f32)
    return pl.pallas_call(
        functools.partial(diagonal_kernel, block, only),
        in_specs=[smem_spec()] + [vmem_spec()] * (6 + len(previous)),
        out_specs=[vmem_spec(), vmem_spec()],
        out_shape=[shape, shape],
        input_output_aliases={7 + index: index for index in range(len(previous))},
        compiler_params=params(),
        cost_estimate=pl.CostEstimate(
            flops=300_000_000, bytes_accessed=3_500_000, transcendentals=1_000_000
        ),
        name="diagonal",
    )(core, *inputs, cum, *previous)


def gated_half(
    base, entry_ref, first_ref, cum_ref, c_ref, weight_ref, parts, gated_ref, block
):
    plain_ref, gain_ref = parts[2 * block : 2 * block + 2]
    wide = pl.ds(pl.multiple_of(base * HEAD_DIM, HALF), HALF)
    plain, gain, weight = plain_ref[:, wide], gain_ref[:, wide], weight_ref[:, wide]
    tokens = slice(block * BLOCK, (block + 1) * BLOCK)
    squares = None
    for pair in range(2):
        states = []
        for index in (2 * pair, 2 * pair + 1):
            columns = head_columns(index)
            state = entry_ref[:, columns]
            if block == 1:
                last = cum_ref[pl.ds(base + index, 1), :BLOCK][:, BLOCK - 1 :]
                state = jnp.exp2(last) * state + first_ref[:, columns]
            states.append(state.astype(bf16))
        off = jnp.dot(
            c_ref[tokens, :], jnp.concatenate(states, axis=1), preferred_element_type=f32
        )
        for index in (2 * pair, 2 * pair + 1):
            part = off[:, head_columns(index - 2 * pair)]
            gated = plain[:, head_columns(index)] + gain[:, head_columns(index)] * part
            gated_ref[tokens, head_columns(index)] = gated * weight[:, head_columns(index)]
            square = gated * gated
            squares = square if squares is None else squares + square
    return squares


def own_gated_kernel(
    core_ref, entry_ref, first_ref, cum_ref, c_ref, weight_ref,
    plain0_ref, gain0_ref, plain1_ref, gain1_ref, gated_ref, squares_ref,
):
    parts = (plain0_ref, gain0_ref, plain1_ref, gain1_ref)
    for block in range(2):
        tokens = slice(block * BLOCK, (block + 1) * BLOCK)
        squares_ref[tokens, :] = gated_half(
            4 * core_ref[0], entry_ref, first_ref, cum_ref, c_ref, weight_ref, parts, gated_ref, block
        )


def other_gated_kernel(
    core_ref, entry_ref, first_ref, cum_ref, c_ref, weight_ref,
    plain0_ref, gain0_ref, plain1_ref, gain1_ref, squares_ref, gated_ref, sum_ref,
):
    parts = (plain0_ref, gain0_ref, plain1_ref, gain1_ref)
    for block in range(2):
        tokens = slice(block * BLOCK, (block + 1) * BLOCK)
        squares = squares_ref[tokens, :] + gated_half(
            4 * (1 - core_ref[0]), entry_ref, first_ref, cum_ref, c_ref, weight_ref, parts, gated_ref, block
        )
        rows = jnp.concatenate([jnp.sum(squares[h * 128 : h * 128 + 128, :].T, axis=0, keepdims=True) for h in range(2)], axis=0)
        for peer in range(8):
            sum_ref[peer, 2 * block : 2 * block + 2, :] = rows


def gated_call(core, entry, first, cum, c_in, weight, parts, squares=None):
    last = squares is not None
    extra = (squares,) if last else ()
    shape = jax.ShapeDtypeStruct((8, 4, 128) if last else (TOK, HEAD_DIM), f32)
    return pl.pallas_call(
        other_gated_kernel if last else own_gated_kernel,
        in_specs=[smem_spec()] + [vmem_spec()] * (9 + len(extra)),
        out_specs=[vmem_spec(), vmem_spec()],
        out_shape=[jax.ShapeDtypeStruct((TOK, HALF), f32), shape],
        compiler_params=params(),
        cost_estimate=pl.CostEstimate(
            flops=70_000_000, bytes_accessed=3_000_000, transcendentals=1_000
        ),
        name="other_gated" if last else "own_gated",
    )(core, entry, first, cum, c_in, weight, *parts, *extra)


def scale_kernel(core_ref, sums_ref, own_ref, other_ref, out_hbm, buffer, sems):
    total = jnp.sum(sums_ref[...], axis=0)
    inverse = lax.rsqrt(total / (HEAD_TOTAL * HEAD_DIM) + epsilon)
    core = core_ref[0]
    copies = []
    for part in range(4):
        tokens = slice(part * 128, (part + 1) * 128)
        column = jnp.broadcast_to(inverse[part : part + 1, :], (128, 128)).T
        for base, gated_ref in ((core * HALF, own_ref), ((1 - core) * HALF, other_ref)):
            scaled = [gated_ref[tokens, head_columns(head)] * column for head in range(4)]
            wide = pl.ds(pl.multiple_of(base, HALF), HALF)
            buffer[tokens, wide] = jnp.concatenate(scaled, axis=1).astype(bf16)
        copy = pltpu.make_async_copy(buffer.at[tokens, :], out_hbm.at[tokens, :], sems.at[part])
        copy.start()
        copies.append(copy)
    for copy in copies:
        copy.wait()


def scale_call(core, sums, own, other):
    return pl.pallas_call(
        scale_kernel,
        in_specs=[smem_spec()] + [vmem_spec()] * 3,
        out_specs=hbm_spec(),
        out_shape=jax.ShapeDtypeStruct((TOK, WIDTH), bf16),
        scratch_shapes=[pltpu.VMEM((TOK, WIDTH), bf16), pltpu.SemaphoreType.DMA((4,))],
        compiler_params=params(),
        name="scale",
    )(core, sums, own, other)


def shards(x_in, z_in, b_in, c_in, decays, d_skip, norm_weight):
    core = (lax.axis_index("seq") % 2).astype(jnp.int32).reshape(1)
    swap = [(i, i ^ 1) for i in range(2 * CHIPS)]
    groups = [[2 * chip + c for chip in range(CHIPS)] for c in range(2)]
    send, first_send, cum, to_end, b_t, *inputs = send_state_call(
        core, x_in, z_in, b_in, c_in, decays, d_skip
    )
    c_in = inputs[-1]
    recv = lax.ppermute(send, "seq", swap)
    keep, first_keep = keep_state_call(core, b_t, to_end, cum, inputs[1])
    part0 = diagonal_call(0, core, inputs, cum, only=0)
    recv, *part0 = lax.optimization_barrier((recv, *part0))
    pay, base = chip_call(core, keep, recv)
    pay = pay.reshape(CHIPS, 1, PIECE * HEAD_DIM)
    pay = lax.all_to_all(pay, "seq", 0, 0, axis_index_groups=groups, tiled=True)
    pre = scan_call(pay.reshape(CHIPS * PIECE, HEAD_DIM))
    pre = lax.all_to_all(pre, "seq", 0, 0, axis_index_groups=groups, tiled=True)
    pre, cum_late = lax.optimization_barrier((pre, cum))
    part0 = diagonal_call(0, core, inputs, cum_late, only=1, previous=part0)
    part1 = diagonal_call(1, core, inputs, cum_late, only=1)
    send, own = entry_call(core, pre, base)
    send, *parts = lax.optimization_barrier((send, *part0, *part1))
    part0, part1 = parts[:2], parts[2:]
    recv = lax.ppermute(send, "seq", swap)
    part1 = diagonal_call(1, core, inputs, cum, only=0, previous=part1)
    parts = (*part0, *part1)
    weight = norm_weight.astype(f32).reshape(1, WIDTH)
    own_gated, squares = gated_call(core, own, first_keep, cum, c_in, weight, parts)
    other_gated, sums = gated_call(core, recv, first_send, cum, c_in, weight, parts, squares)
    sums = lax.all_to_all(sums, "tp", 0, 0, tiled=True)
    return scale_call(core, sums, own_gated, other_gated)


def solution(mesh):
    return jax.shard_map(
        shards,
        mesh=mesh,
        in_specs=(
            P("seq", "tp"),
            P("seq", "tp"),
            P("seq", "tp"),
            P("seq", "tp"),
            P("tp", "seq"),
            P("tp"),
            P("tp"),
        ),
        out_specs=P("seq", "tp"),
        check_vma=False,
    )
```
